32 devices in a mesh: dp: 32 (over z, y, x, core).
Axes of the slice: x: 2, y: 2, z: 4, core: 2. Of those that a mesh axis runs over, the one named last changes fastest.
Arguments:
- hidden: bfloat16 [32, 1024, 1024], P(None, 'dp'), may hold values from -6 to 6
- cotangent: bfloat16 [32, 1024, 1024], P(None, 'dp'), may hold values from -6 to 6
- lengths: int32 [32], replicated, may hold values from 1 to 1024, 20480 in all
- permutation: int32 [32], replicated, may hold values from 0 to 31, each once
- query_weight: bfloat16 [1024, 1024], P('dp'), may hold values from -0.1875 to 0.1875
- key_weight: bfloat16 [1024, 1024], P('dp'), may hold values from -0.1875 to 0.1875
- value_weight: bfloat16 [1024, 1024], P('dp'), may hold values from -0.1875 to 0.1875
- output_weight: bfloat16 [1024, 1024], P('dp'), may hold values from -2 to 2
- query_bias: bfloat16 [1024], P('dp'), may hold values from -3 to 3
- value_bias: bfloat16 [1024], P('dp'), may hold values from -3 to 3
- output_bias: bfloat16 [1024], P('dp'), may hold values from -3 to 3
- first_gain: bfloat16 [1024], P('dp'), may hold values from 0.5 to 1.5
- first_shift: bfloat16 [1024], P('dp'), may hold values from -2 to 2
- inner_weight: bfloat16 [1024, 4096], P('dp'), may hold values from -0.1875 to 0.1875
- inner_bias: bfloat16 [4096], P('dp'), may hold values from -3 to 3
- outer_weight: bfloat16 [4096, 1024], P('dp'), may hold values from -0.125 to 0.125
- outer_bias: bfloat16 [1024], P('dp'), may hold values from -3 to 3
- second_gain: bfloat16 [1024], P('dp'), may hold values from 0.5 to 1.5
- second_shift: bfloat16 [1024], P('dp'), may hold values from -2 to 2
Outputs:
- layer_out: bfloat16 [32, 1024, 1024], P(None, 'dp')
- input_gradient: bfloat16 [32, 1024, 1024], P(None, 'dp')
- query_weight_gradient: float32 [1024, 1024], P('dp')
- key_weight_gradient: float32 [1024, 1024], P('dp')
- value_weight_gradient: float32 [1024, 1024], P('dp')
- output_weight_gradient: float32 [1024, 1024], P('dp')
- query_bias_gradient: float32 [1024], P('dp')
- value_bias_gradient: float32 [1024], P('dp')
- output_bias_gradient: float32 [1024], P('dp')
- first_gain_gradient: float32 [1024], P('dp')
- first_shift_gradient: float32 [1024], P('dp')
- inner_weight_gradient: float32 [1024, 4096], P('dp')
- inner_bias_gradient: float32 [4096], P('dp')
- outer_weight_gradient: float32 [4096, 1024], P('dp')
- outer_bias_gradient: float32 [1024], P('dp')
- second_gain_gradient: float32 [1024], P('dp')
- second_shift_gradient: float32 [1024], P('dp')
- rms_input: float32 [], replicated
- rms_attention: float32 [], replicated
- rms_feed: float32 [], replicated
The draws below stay inside these ranges and needn't reach their ends.
Inputs may be any that keep to these rules, and one draw needn't show every extreme that they name: The lengths sum to 20480 and one of them is exactly 1024. `permutation`: every sequence index appears exactly once.
All inputs are finite; a program needn't handle non-finite values.
Results may differ from the reference program's by a relative error of at most 0.015.
Values may be sent and summed in bfloat16 or wider, within the bound.
No kernel may reach another device: no remote copies, remote signals or barrier semaphores. Data moves between devices by JAX's collectives and lax.ppermute only.
A program may use at most 256 MiB of HBM per device.

```python
import math
import jax
import jax.numpy as jnp
import numpy as np
from jax import lax

D = 1024
HEADS = 16
HEAD_DIM = 64
FF = 4096
MAXLEN = 1024
S_ALL = 32
LIVE_TOKENS = 20480


def levels(stream_key, extent, split, smallest, top_value):
    gain = 1.0
    for position, blocks in split:
        steps = jax.random.uniform(jax.random.fold_in(jax.random.fold_in(stream_key, 6), position), (blocks,), jnp.float32, smallest / len(split), top_value / len(split))
        gain = gain * jnp.repeat(jnp.exp(steps), extent[position] // blocks).reshape((-1,) + (1,) * (len(extent) - 1 - position))
    return gain


def profile(amount, total, limit, skew):
    loads = [(1 << 20) // math.isqrt(standing ** skew) + 1 for standing in range(2, amount + 1)]
    surplus, given = total - limit - (amount - 1), [1] * (amount - 1)
    while surplus > 0:
        free = [i for i in range(amount - 1) if given[i] < limit]
        mass, left = sum([loads[i] for i in free]), surplus
        for i in free:
            extra = min(limit - given[i], max(1, left * loads[i] // mass), surplus)
            given[i] = given[i] + extra
            surplus = surplus - extra
    return np.array([limit] + given)


def uneven(own_key, count, total, bound, lean):
    if count == 2:
        one = jax.random.randint(own_key, (), max(1, total - bound), min(bound, total - 1) + 1)
        return jnp.stack([one, total - one])
    sizes = jnp.asarray(profile(count, total, bound, lean), jnp.int32)
    couples = (count - 1) // 2
    source_of, taker = sizes[1:1 + 2 * couples:2], sizes[2:2 + 2 * couples:2]
    room = jnp.minimum(source_of - 1, bound - taker)
    moved = jax.random.randint(jax.random.fold_in(own_key, 1), (couples,), 0, 1 << 20) % (room + 1)
    sizes = sizes.at[1:1 + 2 * couples:2].set(source_of - moved).at[2:2 + 2 * couples:2].set(taker + moved)
    return sizes[jax.random.permutation(jax.random.fold_in(own_key, 2), count)]


def noise(stream_key, shape, scale, most, shards=(), held_as=jnp.bfloat16):
    level = levels(stream_key, shape, shards, -0.22, 0.18) if shards else 1.0
    values = jax.random.normal(stream_key, shape, jnp.float32) * scale * level
    return jnp.minimum(jnp.maximum(values, -most), most).astype(held_as)


def setup_inputs(seed: int = 0) -> dict:
    key_list = jax.random.split(jax.random.key(seed), 20)
    return {
        "hidden": noise(key_list[0], (S_ALL, MAXLEN, D), 1.0, 6.0, ((1, 32),)),
        "cotangent": noise(key_list[1], (S_ALL, MAXLEN, D), 1.0, 6.0, ((1, 32),)),
        "lengths": uneven(key_list[2], S_ALL, LIVE_TOKENS, MAXLEN, 1).astype(jnp.int32),
        "permutation": jax.random.permutation(key_list[3], S_ALL).astype(jnp.int32),
        "query_weight": noise(key_list[4], (D, D), D ** -0.5, 0.1875, ((0, 32),)),
        "key_weight": noise(key_list[5], (D, D), D ** -0.5, 0.1875, ((0, 32),)),
        "value_weight": noise(key_list[6], (D, D), D ** -0.5, 0.1875, ((0, 32),)),
        "output_weight": noise(key_list[7], (D, D), (max(D // 128, 1)) ** -0.5, 2.0, ((0, 32),)),
        "query_bias": noise(key_list[8], (D,), 0.5, 3.0, ((0, 32),)),
        "value_bias": noise(key_list[9], (D,), 0.5, 3.0, ((0, 32),)),
        "output_bias": noise(key_list[10], (D,), 0.5, 3.0, ((0, 32),)),
        "first_gain": jnp.clip(1.0 + 0.1 * jax.random.normal(key_list[11], (D,), jnp.float32), 0.5, 1.5).astype(jnp.bfloat16),
        "first_shift": noise(key_list[12], (D,), 0.3, 2.0, ((0, 32),)),
        "inner_weight": noise(key_list[13], (D, FF), D ** -0.5, 0.1875, ((0, 32),)),
        "inner_bias": noise(key_list[14], (FF,), 0.5, 3.0, ((0, 32),)),
        "outer_weight": noise(key_list[15], (FF, D), (FF // 2) ** -0.5, 0.125, ((0, 32),)),
        "outer_bias": noise(key_list[16], (D,), 0.5, 3.0, ((0, 32),)),
        "second_gain": jnp.clip(1.0 + 0.1 * jax.random.normal(key_list[17], (D,), jnp.float32), 0.5, 1.5).astype(jnp.bfloat16),
        "second_shift": noise(key_list[18], (D,), 0.3, 2.0, ((0, 32),)),
    }


EPS = 1e-05
NEG = -1e+30
HIGH = lax.Precision.HIGHEST

@jax.custom_vjp
def low(v):
    return lax.optimization_barrier(v.astype(jnp.bfloat16)).astype(jnp.float32)

@jax.custom_vjp
def low_back(v):
    return v

def low_keep(v):
    return (low(v), None)

def low_pass(kept, grad):
    return (grad,)

def back_keep(v):
    return (v, None)

def back_low(kept, grad):
    return (low(grad),)
low.defvjp(low_keep, low_pass)
low_back.defvjp(back_keep, back_low)

def both(value):
    return low(low_back(value))

def matmul(left, right):
    return jnp.dot(left, right, precision=HIGH, preferred_element_type=jnp.float32)

def normalize(resid):
    center = resid - lax.optimization_barrier(jnp.mean(resid, -1, keepdims=True))
    return center * lax.rsqrt(lax.optimization_barrier(jnp.mean(center * center, -1, keepdims=True)) + EPS)

def group_forward(params, block_in, lens):
    query_weight, key_weight, value_weight, output_weight, query_bias, value_bias, output_bias, first_gain, first_shift, inner_weight, inner_bias, outer_weight, outer_bias, second_gain, second_shift = params
    group, length, width = block_in.shape
    rows = block_in.reshape(group * length, width)
    places = jnp.arange(length, dtype=jnp.int32)
    key_table = places[None, :] < lens[:, None]
    valid = key_table.astype(jnp.float32).reshape(group * length, 1)
    query = both(matmul(rows, query_weight) + query_bias).reshape(group, length, HEADS, HEAD_DIM)
    keys = both(matmul(rows, key_weight)).reshape(group, length, HEADS, HEAD_DIM)
    values = both(matmul(rows, value_weight) + value_bias).reshape(group, length, HEADS, HEAD_DIM)
    block = min(512, length)

    def attend(index):
        query_block = lax.dynamic_slice_in_dim(query, index * block, block, 1)
        raw = low_back(jnp.einsum('gqhd,gkhd->ghqk', query_block, keys, precision=HIGH))
        scores = jnp.where(key_table[:, None, None, :], raw * HEAD_DIM ** (-0.5), NEG)
        probs = jax.nn.softmax(scores, axis=-1)
        return jnp.einsum('ghqk,gkhd->gqhd', low(probs), values, precision=HIGH)
    pieces = lax.map(jax.checkpoint(attend), jnp.arange(length // block, dtype=jnp.int32))
    mixed = both(jnp.moveaxis(pieces, 0, 1).reshape(group * length, width))
    branch = low_back(matmul(mixed, output_weight) + output_bias)
    first = low(normalize(rows + branch) * first_gain + first_shift)
    inner = low_back(matmul(first, inner_weight) + inner_bias)
    act = low(jax.nn.gelu(inner, approximate=False))
    second = low_back(matmul(act, outer_weight) + outer_bias)
    result = (normalize(first + second) * second_gain + second_shift) * valid
    sums = jnp.stack([jnp.sum(valid * rows * rows), jnp.sum(valid * branch * branch), jnp.sum(valid * second * second)])
    return (result.reshape(group, length, width), sums)

def forward_all(params, hidden_all, seq_len):
    group = math.gcd(S_ALL, max(1, 4096 // MAXLEN))
    turns = S_ALL // group
    shaped = hidden_all.reshape(turns, group, MAXLEN, D)
    lens = seq_len.reshape(turns, group)

    def one(carry, item):
        result, sums = jax.checkpoint(group_forward)(params, item[0], item[1])
        return (carry + sums, result)
    total, results = lax.scan(one, jnp.zeros(3, jnp.float32), (shaped, lens))
    return (results.reshape(S_ALL, MAXLEN, D), total)

def reference(hidden, cotangent, lengths, permutation, query_weight, key_weight, value_weight, output_weight, query_bias, value_bias, output_bias, first_gain, first_shift, inner_weight, inner_bias, outer_weight, outer_bias, second_gain, second_shift):
    seq_len = jnp.zeros(S_ALL, jnp.int32).at[permutation].set(lengths.astype(jnp.int32))
    params = tuple((item.astype(jnp.float32) for item in (query_weight, key_weight, value_weight, output_weight, query_bias, value_bias, output_bias, first_gain, first_shift, inner_weight, inner_bias, outer_weight, outer_bias, second_gain, second_shift)))
    wide_hidden = hidden.astype(jnp.float32)
    result, backward, totals = jax.vjp(lambda prm, hid: forward_all(prm, hid, seq_len), params, wide_hidden, has_aux=True)
    param_grads, hidden_grad = backward(cotangent.astype(jnp.float32))
    count = jnp.sum(lengths).astype(jnp.float32) * D
    rms_values = jnp.sqrt(totals / count)
    return (result.astype(jnp.bfloat16), hidden_grad.astype(jnp.bfloat16), param_grads[0], param_grads[1], param_grads[2], param_grads[3], param_grads[4], param_grads[5], param_grads[6], param_grads[7], param_grads[8], param_grads[9], param_grads[10], param_grads[11], param_grads[12], param_grads[13], param_grads[14], rms_values[0], rms_values[1], rms_values[2])
```

```python
import functools
import math

import jax
import jax.numpy as jnp
from jax import lax
from jax.experimental import pallas as pl
from jax.experimental.pallas import tpu as pltpu
from jax.sharding import PartitionSpec as P

HEADS = 16
EPS = 1e-05
NEG = -1e30
LOG2E = math.log2(math.e)
BF = jnp.bfloat16
F32 = jnp.float32
BQ = 256
BR = 256
NT = (((1,), (1,)), ((), ()))
TN = (((0,), (0,)), ((), ()))


def normalize(resid):
    center = resid - jnp.mean(resid, -1, keepdims=True)
    return center * lax.rsqrt(jnp.mean(center * center, -1, keepdims=True) + EPS)


def matmul(left, right):
    return jnp.dot(left, right, preferred_element_type=F32)


def left_product(left, right):
    return lax.dot_general(left, right, TN, preferred_element_type=F32)


def right_product(left, right):
    return lax.dot_general(left, right, NT, preferred_element_type=F32)


def column_sum(values):
    return jnp.sum(values.astype(F32), 0)


def head_keys(k, lane, half, key_bias):
    own = (lane >= 64 * half) & (lane < 64 * half + 64)
    spare = lane == 64 * (1 - half)
    return jnp.where(own, k, jnp.where(spare, key_bias, jnp.zeros_like(k)))


def head_queries(q, lane, half):
    return jnp.where(lane == 64 * (1 - half), jnp.ones_like(q), q)


def forward_kernel(len_ref, q_ref, k_ref, v_ref, o_ref, lse_ref, kh, vt):
    qi = pl.program_id(1)
    size = k_ref.shape[0]
    length = len_ref[0]

    @pl.when(qi == 0)
    def _():
        lane = lax.broadcasted_iota(jnp.int32, (size, 128), 1)
        row = lax.broadcasted_iota(jnp.int32, (size, 128), 0)
        key_bias = jnp.where(row < length, 0.0, NEG).astype(BF)
        k = k_ref[...]
        for half in (0, 1):
            kh[half] = head_keys(k, lane, half, key_bias)
        vt[...] = v_ref[...].T

    @pl.when(qi * BQ < length)
    def _():
        q = q_ref[...]
        lane = lax.broadcasted_iota(jnp.int32, q.shape, 1)
        scale = 0.125 * LOG2E
        outs = []
        for half in (0, 1):
            st = lax.dot_general(kh[half], head_queries(q, lane, half), NT, preferred_element_type=F32)
            peak = jnp.max(st, 0, keepdims=True) * scale
            pt = jnp.exp2(st * scale - peak)
            total = jnp.sum(pt, 0, keepdims=True)
            ot = jnp.dot(vt[64 * half : 64 * half + 64, :], pt.astype(BF), preferred_element_type=F32)
            outs.append(ot / total)
            lse_ref[0, half : half + 1, :] = peak + jnp.log2(total)
        o_ref[...] = jnp.concatenate(outs, 0).T.astype(BF)

    @pl.when(qi * BQ >= length)
    def _():
        o_ref[...] = jnp.zeros_like(o_ref)
        lse_ref[...] = jnp.zeros_like(lse_ref)


def attention_forward(lens, q, k, v):
    size, width = q.shape
    pairs = width // 128
    return pl.pallas_call(
        forward_kernel,
        out_shape=(
            jax.ShapeDtypeStruct((size, width), BF),
            jax.ShapeDtypeStruct((pairs, 8, size), F32),
        ),
        grid_spec=pltpu.PrefetchScalarGridSpec(
            num_scalar_prefetch=1,
            grid=(pairs, size // BQ),
            in_specs=[
                pl.BlockSpec((BQ, 128), lambda h, i, n: (i, h)),
                pl.BlockSpec((size, 128), lambda h, i, n: (0, h)),
                pl.BlockSpec((size, 128), lambda h, i, n: (0, h)),
            ],
            out_specs=[
                pl.BlockSpec((BQ, 128), lambda h, i, n: (i, h)),
                pl.BlockSpec((1, 8, BQ), lambda h, i, n: (h, 0, i)),
            ],
            scratch_shapes=[pltpu.VMEM((2, size, 128), BF), pltpu.VMEM((128, size), BF)],
        ),
        compiler_params=pltpu.CompilerParams(vmem_limit_bytes=40 << 20),
        cost_estimate=pl.CostEstimate(
            flops=16 * size * size * width, bytes_accessed=8 * size * width, transcendentals=size * size * HEADS
        ),
        name="attention_forward",
    )(lens, q, k, v)


def backward_kernel(len_ref, q_ref, k_ref, v_ref, o_ref, g_ref, lse_ref, dq_ref, dk_ref, dv_ref, kh, vh, kt, dka, dva):
    qi = pl.program_id(1)
    size = k_ref.shape[0]
    length = len_ref[0]

    @pl.when(qi == 0)
    def _():
        lane = lax.broadcasted_iota(jnp.int32, (size, 128), 1)
        row = lax.broadcasted_iota(jnp.int32, (size, 128), 0)
        key_bias = jnp.where(row < length, 0.0, NEG).astype(BF)
        k = k_ref[...]
        v = v_ref[...]
        for half in (0, 1):
            kh[half] = head_keys(k, lane, half, key_bias)
            vh[half] = head_keys(v, lane, half, jnp.zeros_like(v))
        kt[...] = k.T
        dka[...] = jnp.zeros_like(dka)
        dva[...] = jnp.zeros_like(dva)

    @pl.when(qi * BQ < length)
    def _():
        q = q_ref[...]
        g = g_ref[...]
        lane = lax.broadcasted_iota(jnp.int32, q.shape, 1)
        scale = 0.125 * LOG2E
        dots = (g.astype(F32) * o_ref[...].astype(F32)).T
        outs = []
        for half in (0, 1):
            qh = head_queries(q, lane, half)
            st = lax.dot_general(kh[half], qh, NT, preferred_element_type=F32)
            pt = jnp.exp2(st * scale - lse_ref[0, half : half + 1, :])
            dpt = lax.dot_general(vh[half], g, NT, preferred_element_type=F32)
            delta = jnp.sum(dots[64 * half : 64 * half + 64, :], 0, keepdims=True)
            dst = (pt * (dpt - delta)).astype(BF)
            dva[half] += jnp.dot(pt.astype(BF), g, preferred_element_type=F32)
            dka[half] += jnp.dot(dst, qh, preferred_element_type=F32)
            outs.append(jnp.dot(kt[64 * half : 64 * half + 64, :], dst, preferred_element_type=F32))
        dq_ref[...] = (jnp.concatenate(outs, 0) * 0.125).T.astype(BF)

    @pl.when(qi * BQ >= length)
    def _():
        dq_ref[...] = jnp.zeros_like(dq_ref)

    @pl.when(qi == pl.num_programs(1) - 1)
    def _():
        lane = lax.broadcasted_iota(jnp.int32, (size, 128), 1)
        dk_ref[...] = (jnp.where(lane < 64, dka[0], dka[1]) * 0.125).astype(BF)
        dv_ref[...] = jnp.where(lane < 64, dva[0], dva[1]).astype(BF)


def attention_backward(lens, q, k, v, o, g, lse):
    size, width = q.shape
    pairs = width // 128
    rows = pl.BlockSpec((BQ, 128), lambda h, i, n: (i, h))
    whole = pl.BlockSpec((size, 128), lambda h, i, n: (0, h))
    shape = jax.ShapeDtypeStruct((size, width), BF)
    return pl.pallas_call(
        backward_kernel,
        out_shape=(shape, shape, shape),
        grid_spec=pltpu.PrefetchScalarGridSpec(
            num_scalar_prefetch=1,
            grid=(pairs, size // BQ),
            in_specs=[rows, whole, whole, rows, rows, pl.BlockSpec((1, 8, BQ), lambda h, i, n: (h, 0, i))],
            out_specs=[rows, whole, whole],
            scratch_shapes=[
                pltpu.VMEM((2, size, 128), BF),
                pltpu.VMEM((2, size, 128), BF),
                pltpu.VMEM((128, size), BF),
                pltpu.VMEM((2, size, 128), F32),
                pltpu.VMEM((2, size, 128), F32),
            ],
        ),
        compiler_params=pltpu.CompilerParams(vmem_limit_bytes=40 << 20),
        cost_estimate=pl.CostEstimate(
            flops=40 * size * size * width, bytes_accessed=16 * size * width, transcendentals=size * size * HEADS
        ),
        name="attention_backward",
    )(lens, q, k, v, o, g, lse)


def feed_forward_kernel(first_ref, w1_ref, w2_ref, b1_ref, b2_ref, act_ref, slope_ref, second_ref):
    width = first_ref.shape[1]
    w1 = w1_ref[...].reshape(width, width)
    w2 = w2_ref[...].reshape(width, width)

    @pl.when(pl.program_id(0) == 0)
    def _():
        second_ref[...] = jnp.broadcast_to(b2_ref[...], second_ref.shape)

    for start in range(0, first_ref.shape[0], BR):
        at = slice(start, start + BR)
        inner = jnp.dot(first_ref[at, :], w1, preferred_element_type=F32) + b1_ref[...]
        cdf = 0.5 + 0.5 * lax.erf(inner * (0.5**0.5))
        act = (inner * cdf).astype(BF)
        slope = cdf + inner * (jnp.exp2(inner * inner * (-0.5 * LOG2E)) * ((0.5 / math.pi) ** 0.5))
        act_ref[at, :] = act
        slope_ref[at, :] = slope.astype(BF)
        second_ref[at, :] += jnp.dot(act, w2, preferred_element_type=F32)


def weight_specs(feed, fb, first_slot):
    n, slots, r, width = feed.shape
    if n == 1:
        inner = pl.BlockSpec((1, 1, r, width), lambda j: (0, first_slot + j, 0, 0))
        outer = pl.BlockSpec((1, 1, r, width), lambda j: (0, first_slot + fb + j, 0, 0))
    else:
        inner = pl.BlockSpec((n, 1, r, width), lambda j: (0, first_slot + j, 0, 0))
        outer = pl.BlockSpec((n // fb, fb, r, width), lambda j: (j, first_slot // fb + 1, 0, 0))
    return inner, outer


def feed_forward(first, feed, fb, b1, b2):
    size, width = first.shape
    inner_spec, outer_spec = weight_specs(feed, fb, 0)
    block = pl.BlockSpec((size, width), lambda j: (0, j))
    whole = pl.BlockSpec((size, width), lambda j: (0, 0))
    line = pl.BlockSpec((1, width), lambda j: (0, j))
    const = pl.BlockSpec((1, width), lambda j: (0, 0))
    return pl.pallas_call(
        feed_forward_kernel,
        out_shape=(
            jax.ShapeDtypeStruct((size, fb * width), BF),
            jax.ShapeDtypeStruct((size, fb * width), BF),
            jax.ShapeDtypeStruct((size, width), F32),
        ),
        grid=(fb,),
        in_specs=[whole, inner_spec, outer_spec, line, const],
        out_specs=[block, block, whole],
        compiler_params=pltpu.CompilerParams(vmem_limit_bytes=56 << 20),
        cost_estimate=pl.CostEstimate(
            flops=4 * size * width * width * fb, bytes_accessed=40 << 20, transcendentals=2 * size * width * fb
        ),
        name="feed_forward",
    )(first, feed, feed, b1, b2)


def feed_backward_kernel(
    gs_ref, first_ref, w1_ref, w2_ref, act_ref, slope_ref, base_ref, grads_ref, gfirst_ref, gbias_ref, one, two, sems
):
    j = pl.program_id(0)
    fb = pl.num_programs(0)
    size, width = gs_ref.shape
    slot = lax.rem(j, 2)
    chunks, slots, r, _ = grads_ref.shape
    steps = slots // 2

    def copies(index, at):
        if chunks == 1:
            there = grads_ref.at[:, pl.ds(steps + index, 1)]
        else:
            there = grads_ref.at[pl.ds(index * (chunks // steps), chunks // steps), pl.ds(steps, steps)]
        return (
            pltpu.make_async_copy(one.at[at], grads_ref.at[:, pl.ds(index, 1)], sems.at[0, at]),
            pltpu.make_async_copy(two.at[at], there, sems.at[1, at]),
        )

    @pl.when(j >= 2)
    def _():
        for copy in copies(j - 2, slot):
            copy.wait()

    w1 = w1_ref[...].reshape(width, width)
    w2 = w2_ref[...].reshape(width, width)
    gs = gs_ref[...]
    two[slot] = (
        lax.dot_general(act_ref[...], gs, TN, preferred_element_type=F32).astype(BF).reshape(two.shape[1:])
    )

    @pl.when(j == 0)
    def _():
        gfirst_ref[...] = base_ref[...]

    total = jnp.zeros((1, width), F32)
    pieces = []
    for start in range(0, size, BR):
        at = slice(start, start + BR)
        wide = lax.dot_general(gs_ref[at, :], w2, NT, preferred_element_type=F32) * slope_ref[at, :].astype(F32)
        piece = wide.astype(BF)
        total += jnp.sum(piece.astype(F32), 0, keepdims=True)
        gfirst_ref[at, :] += lax.dot_general(piece, w1, NT, preferred_element_type=F32)
        pieces.append(piece)
    gbias_ref[...] = total
    ginner = jnp.concatenate(pieces, 0)
    one[slot] = (
        lax.dot_general(first_ref[...], ginner, TN, preferred_element_type=F32).astype(BF).reshape(one.shape[1:])
    )
    for copy in copies(j, slot):
        copy.start()

    @pl.when(j == fb - 1)
    def _():
        for copy in copies(j - 1, 1 - slot):
            copy.wait()
        for copy in copies(j, slot):
            copy.wait()


def feed_backward(gs, first, feed, fb, act, slope, base):
    size, width = first.shape
    n, slots, r, _ = feed.shape
    assert fb >= 2
    inner_spec, outer_spec = weight_specs(feed, fb, 0)
    block = pl.BlockSpec((size, width), lambda j: (0, j))
    whole = pl.BlockSpec((size, width), lambda j: (0, 0))
    return pl.pallas_call(
        feed_backward_kernel,
        out_shape=(
            jax.ShapeDtypeStruct((n, 2 * fb, r, width), BF),
            jax.ShapeDtypeStruct((size, width), F32),
            jax.ShapeDtypeStruct((1, fb * width), F32),
        ),
        grid=(fb,),
        in_specs=[whole, whole, inner_spec, outer_spec, block, block, whole],
        out_specs=[pl.BlockSpec(memory_space=pl.ANY), whole, pl.BlockSpec((1, width), lambda j: (0, j))],
        scratch_shapes=[
            pltpu.VMEM((2,) + tuple(inner_spec.block_shape), BF),
            pltpu.VMEM((2,) + tuple(outer_spec.block_shape), BF),
            pltpu.SemaphoreType.DMA((2, 2)),
        ],
        compiler_params=pltpu.CompilerParams(vmem_limit_bytes=60 << 20),
        cost_estimate=pl.CostEstimate(
            flops=8 * size * width * width * fb, bytes_accessed=60 << 20, transcendentals=0
        ),
        name="feed_backward",
    )(gs, first, feed, feed, act, slope, base)


def reduce_halving(blocks):
    n = blocks.shape[0]
    bits = n.bit_length() - 1
    me = lax.axis_index("dp")
    tail = blocks.shape[1:]

    def step(value, left, bit):
        axis = left.index(bit)
        here = (me >> bit) & 1
        away = lax.dynamic_index_in_dim(value, 1 - here, axis, keepdims=False)
        mine = lax.dynamic_index_in_dim(value, here, axis, keepdims=False)
        got = lax.ppermute(away, "dp", [(i, i ^ (1 << bit)) for i in range(n)])
        return mine.astype(F32) + got.astype(F32), [b for b in left if b != bit]

    left = list(range(bits - 1, -1, -1))
    value, left = step(blocks.reshape((2,) * bits + tail), left, 0)
    value = value.astype(BF)
    half = tail[0] // 2
    results = []
    for part in (0, 1):
        piece = lax.slice_in_dim(value, part * half, (part + 1) * half, axis=value.ndim - 2)
        order = list(range(1, bits))
        if part:
            order[0], order[1] = order[1], order[0]
        remaining = left
        for count, bit in enumerate(order):
            piece, remaining = step(piece, remaining, bit)
            if count < len(order) - 1:
                piece = piece.astype(BF)
        results.append(piece)
    return jnp.concatenate(results, 0)


def local(
    hidden,
    cotangent,
    lengths,
    permutation,
    query_weight,
    key_weight,
    value_weight,
    output_weight,
    query_bias,
    value_bias,
    output_bias,
    first_gain,
    first_shift,
    inner_weight,
    inner_bias,
    outer_weight,
    outer_bias,
    second_gain,
    second_shift,
):
    n = lax.axis_size("dp")
    me = lax.axis_index("dp")
    seq_count, part_len, width = hidden.shape
    assert seq_count == n
    length = part_len * n
    r = query_weight.shape[0]
    ff = inner_weight.shape[1]
    fb = ff // width

    def deal(values):
        dealt = jnp.take(values, permutation, axis=0, mode="clip")
        return lax.all_to_all(dealt, "dp", split_axis=0, concat_axis=0, tiled=True).reshape(length, width)

    def collect(values):
        return lax.all_to_all(values.reshape(n, part_len, width), "dp", split_axis=0, concat_axis=0, tiled=True)

    rows = deal(hidden)
    small = jnp.concatenate(
        (query_bias, value_bias, output_bias, first_gain, first_shift, outer_bias, second_gain, second_shift, inner_bias)
    )
    small = lax.all_to_all(
        jnp.broadcast_to(small[None], (n, small.shape[0])), "dp", split_axis=0, concat_axis=0, tiled=True
    )
    vectors = [small[:, i * r : (i + 1) * r].reshape(1, width).astype(F32) for i in range(8)]
    full_query_bias, full_value_bias, full_output_bias, full_first_gain, full_first_shift = vectors[:5]
    full_outer_bias, full_second_gain, full_second_shift = vectors[5:]
    full_inner_bias = small[:, 8 * r :].reshape(1, ff).astype(F32)

    attention_pack = jnp.stack((query_weight, key_weight, value_weight, output_weight))
    gathered = lax.all_gather(attention_pack, "dp", axis=0, tiled=False)
    gathered = jnp.moveaxis(gathered, 1, 0).reshape(4, width, width)
    full_query, full_key, full_value, full_output = (gathered[i] for i in range(4))
    slabs = r % 16 == 0
    feed_pack = jnp.concatenate(
        (jnp.moveaxis(inner_weight.reshape(r, fb, width), 1, 0), outer_weight.reshape(fb, r, width)), 0
    )
    feed = lax.all_gather(feed_pack, "dp", axis=0, tiled=False)
    if not slabs:
        feed = jnp.concatenate(
            (
                jnp.moveaxis(feed[:, :fb], 1, 0).reshape(1, fb, width, width),
                feed[:, fb:].reshape(1, fb, width, width),
            ),
            1,
        )

    rows_wide = rows.astype(F32)
    my_len = lax.dynamic_slice_in_dim(lengths, me, 1)
    valid = (jnp.arange(length, dtype=jnp.int32) < my_len[0]).astype(F32)[:, None]

    query = (matmul(rows, full_query) + full_query_bias).astype(BF)
    keys = matmul(rows, full_key).astype(BF)
    values = (matmul(rows, full_value) + full_value_bias).astype(BF)
    mixed, lse = attention_forward(my_len, query, keys, values)
    branch = matmul(mixed, full_output) + full_output_bias
    first_norm, first_back = jax.vjp(normalize, rows_wide + branch)
    first = (first_norm * full_first_gain + full_first_shift).astype(BF)
    act, slope, second = feed_forward(first, feed, fb, full_inner_bias, full_outer_bias)
    second_norm, second_back = jax.vjp(normalize, first.astype(F32) + second)
    result = ((second_norm * full_second_gain + full_second_shift) * valid).astype(BF)
    squares = jnp.stack(
        (
            jnp.sum(valid * rows_wide * rows_wide),
            jnp.sum(valid * branch * branch),
            jnp.sum(valid * second * second),
        )
    )
    out_back = collect(result)

    grad_out = deal(cotangent).astype(F32) * valid
    second_gain_grad = jnp.sum(grad_out * second_norm, 0)
    second_shift_grad = jnp.sum(grad_out, 0)
    (grad_res2,) = second_back(grad_out * full_second_gain)
    grad_second = grad_res2.astype(BF)
    outer_bias_grad = column_sum(grad_second)
    feed_blocks, grad_first, inner_bias_grad = feed_backward(grad_second, first, feed, fb, act, slope, grad_res2)
    if not slabs:
        feed_blocks = jnp.concatenate(
            (
                jnp.moveaxis(feed_blocks[0, :fb].reshape(fb, n, r, width), 0, 1),
                feed_blocks[0, fb:].reshape(n, fb, r, width),
            ),
            1,
        )
    feed_owned = lax.psum_scatter(feed_blocks, "dp", scatter_dimension=0, tiled=True).astype(F32)[0]

    first_gain_grad = jnp.sum(grad_first * first_norm, 0)
    first_shift_grad = jnp.sum(grad_first, 0)
    (grad_res1,) = first_back(grad_first * full_first_gain)
    grad_branch = grad_res1.astype(BF)
    output_weight_grad = left_product(mixed, grad_branch).astype(BF)
    output_bias_grad = column_sum(grad_branch)
    grad_mixed = right_product(grad_branch, full_output).astype(BF)
    grad_query, grad_keys, grad_values = attention_backward(my_len, query, keys, values, mixed, grad_mixed, lse)
    input_grad = (
        grad_res1
        + right_product(grad_query, full_query)
        + right_product(grad_keys, full_key)
        + right_product(grad_values, full_value)
    )
    input_back = collect(input_grad.astype(BF))
    attention_blocks = jnp.concatenate(
        [
            g.astype(BF).reshape(n, r, width)
            for g in (
                left_product(rows, grad_query),
                left_product(rows, grad_keys),
                left_product(rows, grad_values),
                output_weight_grad,
            )
        ],
        1,
    )
    attention_owned = reduce_halving(attention_blocks)

    vector_grads = [
        column_sum(grad_query),
        column_sum(grad_values),
        output_bias_grad,
        first_gain_grad,
        first_shift_grad,
        outer_bias_grad,
        second_gain_grad,
        second_shift_grad,
        inner_bias_grad,
    ]
    spread = jnp.concatenate(
        [g.reshape(n, -1) for g in vector_grads] + [jnp.broadcast_to(squares[None], (n, 3)), jnp.zeros((n, 125), F32)], 1
    )
    owned = jnp.sum(lax.all_to_all(spread, "dp", split_axis=0, concat_axis=0, tiled=True), 0)
    sums = owned[-128:-125]

    inverse = jnp.zeros(seq_count, jnp.int32).at[permutation].set(jnp.arange(seq_count, dtype=jnp.int32))
    layer_out = jnp.take(out_back, inverse, axis=0, mode="clip")
    input_gradient = jnp.take(input_back, inverse, axis=0, mode="clip")
    rms = jnp.sqrt(sums / (jnp.sum(lengths).astype(F32) * width))
    return (
        layer_out,
        input_gradient,
        attention_owned[:r],
        attention_owned[r : 2 * r],
        attention_owned[2 * r : 3 * r],
        attention_owned[3 * r :],
        owned[:r],
        owned[r : 2 * r],
        owned[2 * r : 3 * r],
        owned[3 * r : 4 * r],
        owned[4 * r : 5 * r],
        jnp.moveaxis(feed_owned[:fb], 0, 1).reshape(r, ff),
        owned[8 * r : 8 * r + ff // n],
        feed_owned[fb:].reshape(r * fb, width),
        owned[5 * r : 6 * r],
        owned[6 * r : 7 * r],
        owned[7 * r : 8 * r],
        rms[0],
        rms[1],
        rms[2],
    )


def solution(mesh):
    seq, mat, vec = P(None, "dp", None), P("dp", None), P("dp")
    return jax.shard_map(
        local,
        mesh=mesh,
        in_specs=(seq, seq, P(), P(), mat, mat, mat, mat, vec, vec, vec, vec, vec, mat, vec, mat, vec, vec, vec),
        out_specs=(seq, seq, mat, mat, mat, mat, vec, vec, vec, vec, vec, mat, vec, mat, vec, vec, vec, P(), P(), P()),
        check_vma=False,
    )
```

```python
import functools
import math

import jax
import jax.numpy as jnp
from jax import lax
from jax.experimental import pallas as pl
from jax.experimental.pallas import tpu as pltpu
from jax.sharding import PartitionSpec as P

HEADS = 16
EPS = 1e-05
NEG = -1e30
LOG2E = math.log2(math.e)
BF = jnp.bfloat16
F32 = jnp.float32
BQ = 1024
BR = 256
SPARE = 16
COST = pl.CostEstimate(flops=1 << 20, bytes_accessed=1 << 20, transcendentals=0)
NT = (((1,), (1,)), ((), ()))
TN = (((0,), (0,)), ((), ()))


def matmul(left, right):
    return jnp.dot(left, right, preferred_element_type=F32)


def left_product(left, right):
    return lax.dot_general(left, right, TN, preferred_element_type=F32)


def right_product(left, right):
    return lax.dot_general(left, right, NT, preferred_element_type=F32)


def column_sum(values):
    return jnp.sum(values.astype(F32), 0)


def head_keys(k, lane, half, key_bias):
    own = (lane >= 64 * half) & (lane < 64 * half + 64)
    spare = lane == 64 * (1 - half)
    return jnp.where(own, k, jnp.where(spare, key_bias, jnp.zeros_like(k)))


def head_queries(q, lane, half):
    return jnp.where(lane == 64 * (1 - half), jnp.ones_like(q), q)


def forward_kernel(len_ref, q_ref, k_ref, v_ref, o_ref, lse_ref, kh, vt):
    qi = pl.program_id(1)
    size = k_ref.shape[1]
    length = len_ref[0]

    @pl.when(qi == 0)
    def _():
        lane = lax.broadcasted_iota(jnp.int32, (size, 128), 1)
        row = lax.broadcasted_iota(jnp.int32, (size, 128), 0)
        key_bias = jnp.where(row < length, 0.0, NEG).astype(BF)
        k = k_ref[0]
        for half in (0, 1):
            kh[half] = head_keys(k, lane, half, key_bias)
        vt[...] = v_ref[0].T

    @pl.when(qi * BQ < length)
    def _():
        q = q_ref[0]
        lane = lax.broadcasted_iota(jnp.int32, q.shape, 1)
        scale = 0.125 * LOG2E
        outs = []
        for half in (0, 1):
            st = lax.dot_general(kh[half], head_queries(q, lane, half), NT, preferred_element_type=F32)
            peak = jnp.max(st, 0, keepdims=True) * scale
            pt = jnp.exp2(st * scale - peak)
            total = jnp.sum(pt, 0, keepdims=True)
            ot = jnp.dot(vt[64 * half : 64 * half + 64, :], pt.astype(BF), preferred_element_type=F32)
            outs.append(ot / total)
            lse_ref[0, half : half + 1, :] = peak + jnp.log2(total)
        o_ref[...] = jnp.concatenate(outs, 0).T.astype(BF)

    @pl.when(qi * BQ >= length)
    def _():
        o_ref[...] = jnp.zeros_like(o_ref)
        lse_ref[...] = jnp.zeros_like(lse_ref)


def qkv_specs(size):
    return [
        pl.BlockSpec((1, BQ, 128), lambda h, i, n: (0, i, h)),
        pl.BlockSpec((1, size, 128), lambda h, i, n: (1, 0, h)),
        pl.BlockSpec((1, size, 128), lambda h, i, n: (2, 0, h)),
    ]


def attention_forward(lens, qkv):
    _, size, width = qkv.shape
    pairs = width // 128
    return pl.pallas_call(
        forward_kernel,
        out_shape=(
            jax.ShapeDtypeStruct((size, width), BF),
            jax.ShapeDtypeStruct((pairs, 8, size), F32),
        ),
        grid_spec=pltpu.PrefetchScalarGridSpec(
            num_scalar_prefetch=1,
            grid=(pairs, size // BQ),
            in_specs=qkv_specs(size),
            out_specs=[
                pl.BlockSpec((BQ, 128), lambda h, i, n: (i, h)),
                pl.BlockSpec((1, 8, BQ), lambda h, i, n: (h, 0, i)),
            ],
            scratch_shapes=[pltpu.VMEM((2, size, 128), BF), pltpu.VMEM((128, size), BF)],
        ),
        compiler_params=pltpu.CompilerParams(vmem_limit_bytes=40 << 20),
        cost_estimate=pl.CostEstimate(flops=32 << 30, bytes_accessed=16 << 20, transcendentals=0),
        name="attention_forward",
    )(lens, qkv, qkv, qkv)


def backward_kernel(len_ref, q_ref, k_ref, v_ref, o_ref, g_ref, lse_ref, out_ref, kh, vh, kt, dka, dva):
    qi = pl.program_id(1)
    size = k_ref.shape[1]
    length = len_ref[0]
    here = pl.ds(pl.multiple_of(qi * BQ, BQ), BQ)

    @pl.when(qi == 0)
    def _():
        lane = lax.broadcasted_iota(jnp.int32, (size, 128), 1)
        row = lax.broadcasted_iota(jnp.int32, (size, 128), 0)
        key_bias = jnp.where(row < length, 0.0, NEG).astype(BF)
        k = k_ref[0]
        v = v_ref[0]
        for half in (0, 1):
            kh[half] = head_keys(k, lane, half, key_bias)
            vh[half] = head_keys(v, lane, half, jnp.zeros_like(v))
        kt[...] = k.T
        dka[...] = jnp.zeros_like(dka)
        dva[...] = jnp.zeros_like(dva)

    @pl.when(qi * BQ < length)
    def _():
        q = q_ref[0]
        g = g_ref[...]
        lane = lax.broadcasted_iota(jnp.int32, q.shape, 1)
        scale = 0.125 * LOG2E
        dots = (g.astype(F32) * o_ref[...].astype(F32)).T
        outs = []
        for half in (0, 1):
            qh = head_queries(q, lane, half)
            st = lax.dot_general(kh[half], qh, NT, preferred_element_type=F32)
            pt = jnp.exp2(st * scale - lse_ref[0, half : half + 1, :])
            dpt = lax.dot_general(vh[half], g, NT, preferred_element_type=F32)
            delta = jnp.sum(dots[64 * half : 64 * half + 64, :], 0, keepdims=True)
            dst = (pt * (dpt - delta)).astype(BF)
            dva[half] += jnp.dot(pt.astype(BF), g, preferred_element_type=F32)
            dka[half] += jnp.dot(dst, qh, preferred_element_type=F32)
            outs.append(jnp.dot(kt[64 * half : 64 * half + 64, :], dst, preferred_element_type=F32))
        out_ref[0, here, :] = (jnp.concatenate(outs, 0) * 0.125).T.astype(BF)

    @pl.when(qi * BQ >= length)
    def _():
        out_ref[0, here, :] = jnp.zeros((BQ, 128), BF)

    @pl.when(qi == pl.num_programs(1) - 1)
    def _():
        lane = lax.broadcasted_iota(jnp.int32, (size, 128), 1)
        out_ref[1] = (jnp.where(lane < 64, dka[0], dka[1]) * 0.125).astype(BF)
        out_ref[2] = jnp.where(lane < 64, dva[0], dva[1]).astype(BF)


def attention_backward(lens, qkv, o, g, lse):
    _, size, width = qkv.shape
    pairs = width // 128
    rows = pl.BlockSpec((BQ, 128), lambda h, i, n: (i, h))
    return pl.pallas_call(
        backward_kernel,
        out_shape=jax.ShapeDtypeStruct((3, size, width), BF),
        grid_spec=pltpu.PrefetchScalarGridSpec(
            num_scalar_prefetch=1,
            grid=(pairs, size // BQ),
            in_specs=qkv_specs(size) + [rows, rows, pl.BlockSpec((1, 8, BQ), lambda h, i, n: (h, 0, i))],
            out_specs=pl.BlockSpec((3, size, 128), lambda h, i, n: (0, 0, h)),
            scratch_shapes=[
                pltpu.VMEM((2, size, 128), BF),
                pltpu.VMEM((2, size, 128), BF),
                pltpu.VMEM((128, size), BF),
                pltpu.VMEM((2, size, 128), F32),
                pltpu.VMEM((2, size, 128), F32),
            ],
        ),
        compiler_params=pltpu.CompilerParams(vmem_limit_bytes=40 << 20),
        cost_estimate=pl.CostEstimate(flops=40 << 30, bytes_accessed=16 << 20, transcendentals=0),
        name="attention_backward",
    )(lens, qkv, qkv, qkv, o, g, lse)


def gather_orders(n):
    top = list(range(n.bit_length() - 2, 2, -1))
    return top, (top + [2, 1], top + [1, 2])


def distance(index, order):
    return sum(((index >> k) & 1) << bit for k, bit in enumerate(order))


def project_kernel(me_ref, a0, a1, b0, b1, x_ref, bias_ref, qkv_ref, w_ref, scratch, *, r, orders):
    j = pl.program_id(0)

    @pl.when(j == 0)
    def _():
        me = me_ref[0]
        half = r // 2
        for core, (a, b) in enumerate(((a0, b0), (a1, b1))):
            for index in range(a.shape[0]):
                off = pl.multiple_of((me ^ (distance(index, orders[0]) | core)) * r, r)
                scratch[0, pl.ds(off, r), :] = a[index, :r, :]
                scratch[1, pl.ds(off, half), :] = a[index, r : r + half, :]
                off = pl.multiple_of((me ^ (distance(index, orders[1]) | core)) * r, r)
                scratch[1, pl.ds(pl.multiple_of(off + half, half), half), :] = b[index, :half, :]
                scratch[2, pl.ds(off, r), :] = b[index, half : half + r, :]

    w = scratch[j]
    w_ref[0] = w
    qkv_ref[0] = (jnp.dot(x_ref[...], w, preferred_element_type=F32) + bias_ref[0]).astype(BF)


def project(me, pieces, x, bias, r):
    size, width = x.shape
    n = width // r
    whole = [pl.BlockSpec(p.shape, lambda j, m: (0, 0, 0)) for p in pieces]
    return pl.pallas_call(
        functools.partial(project_kernel, r=r, orders=gather_orders(n)[1]),
        out_shape=(jax.ShapeDtypeStruct((3, size, width), BF), jax.ShapeDtypeStruct((3, width, width), BF)),
        grid_spec=pltpu.PrefetchScalarGridSpec(
            num_scalar_prefetch=1,
            grid=(3,),
            in_specs=whole
            + [
                pl.BlockSpec((size, width), lambda j, m: (0, 0)),
                pl.BlockSpec((1, 1, width), lambda j, m: (j, 0, 0)),
            ],
            out_specs=[
                pl.BlockSpec((1, size, width), lambda j, m: (j, 0, 0)),
                pl.BlockSpec((1, width, width), lambda j, m: (j, 0, 0)),
            ],
            scratch_shapes=[pltpu.VMEM((3, width, width), BF)],
        ),
        compiler_params=pltpu.CompilerParams(vmem_limit_bytes=48 << 20),
        cost_estimate=pl.CostEstimate(flops=6 << 30, bytes_accessed=16 << 20, transcendentals=0),
        name="project",
    )(me, *pieces, x, bias)


def project_back_kernel(
    me_ref, x_ref, g_ref, w_ref, base_ref, wo_ref, dx_ref, mine_ref, away_ref, sums_ref, xt, acc, *, r
):
    j = pl.program_id(0)
    half, _, width = mine_ref.shape

    core = me_ref[0] & 1
    at = pl.ds(pl.multiple_of(j * r, r), r)

    @pl.when(j == 0)
    def _():
        xt[...] = x_ref[...].T
        acc[...] = base_ref[...]

    @pl.when(j < 3)
    def _():
        g = g_ref[0]
        emit(core, jnp.dot(xt[...], g, preferred_element_type=F32).astype(BF), mine_ref, away_ref, at, r)
        acc[...] += lax.dot_general(g, w_ref[0], NT, preferred_element_type=F32)
        sums_ref[0] = jnp.sum(g.astype(F32), 0, keepdims=True)

    @pl.when(j == 3)
    def _():
        emit(core, wo_ref[...], mine_ref, away_ref, at, r)
        spare = pl.ds(4 * r, SPARE)
        mine_ref[:, spare, :] = jnp.zeros((half, SPARE, width), BF)
        away_ref[:, spare, :] = jnp.zeros((half, SPARE, width), BF)
        dx_ref[...] = acc[...].astype(BF)


def project_back(me, x, grads, w, base, output_grad, r):
    size, width = x.shape
    half = width // r // 2
    last = lambda j: jnp.minimum(j, 2)
    whole = pl.BlockSpec((size, width), lambda j, m: (0, 0))
    blocks = pl.BlockSpec((half, 4 * r + SPARE, width), lambda j, m: (0, 0, 0))
    return pl.pallas_call(
        functools.partial(project_back_kernel, r=r),
        out_shape=(
            jax.ShapeDtypeStruct((size, width), BF),
            jax.ShapeDtypeStruct((half, 4 * r + SPARE, width), BF),
            jax.ShapeDtypeStruct((half, 4 * r + SPARE, width), BF),
            jax.ShapeDtypeStruct((3, 1, width), F32),
        ),
        grid_spec=pltpu.PrefetchScalarGridSpec(
            num_scalar_prefetch=1,
            grid=(4,),
            in_specs=[
                whole,
                pl.BlockSpec((1, size, width), lambda j, m: (last(j), 0, 0)),
                pl.BlockSpec((1, width, width), lambda j, m: (last(j), 0, 0)),
                whole,
                pl.BlockSpec((width, width), lambda j, m: (0, 0)),
            ],
            out_specs=[whole, blocks, blocks, pl.BlockSpec((1, 1, width), lambda j, m: (last(j), 0, 0))],
            scratch_shapes=[pltpu.VMEM((width, size), BF), pltpu.VMEM((size, width), F32)],
        ),
        compiler_params=pltpu.CompilerParams(vmem_limit_bytes=56 << 20),
        cost_estimate=pl.CostEstimate(flops=12 << 30, bytes_accessed=16 << 20, transcendentals=0),
        name="project_back",
    )(me, x, grads, w, base, output_grad)


def norm_rows(resid):
    center = resid - jnp.mean(resid, -1, keepdims=True)
    inverse_root = lax.rsqrt(jnp.mean(center * center, -1, keepdims=True) + EPS)
    return center * inverse_root, inverse_root


def norm_back(grad, norm, inverse_root):
    return (grad - jnp.mean(grad, -1, keepdims=True) - norm * jnp.mean(grad * norm, -1, keepdims=True)) * inverse_root


def valid_rows(len_ref):
    row = pl.program_id(0) * BR + lax.broadcasted_iota(jnp.int32, (BR, 1), 0)
    return (row < len_ref[0]).astype(F32)


def add_rows(sums_ref, values):
    @pl.when(pl.program_id(0) == 0)
    def _():
        sums_ref[...] = jnp.zeros_like(sums_ref)

    for k, value in enumerate(values):
        sums_ref[k : k + 1, :] += jnp.sum(value, 0, keepdims=True)


def first_norm_kernel(
    len_ref, mixed_ref, wo_ref, bias_ref, x_ref, gain_ref, shift_ref, first_ref, norm_ref, root_ref, sums_ref
):
    width = x_ref.shape[1]
    wo = wo_ref[...].reshape(width, width)
    branch = jnp.dot(mixed_ref[...], wo, preferred_element_type=F32) + bias_ref[...]
    x = x_ref[...].astype(F32)
    norm, root = norm_rows(x + branch)
    first_ref[...] = (norm * gain_ref[...] + shift_ref[...]).astype(BF)
    norm_ref[...] = norm
    root_ref[...] = jnp.broadcast_to(root, root_ref.shape)
    valid = valid_rows(len_ref)
    add_rows(sums_ref, (valid * x * x, valid * branch * branch))


def second_norm_kernel(
    len_ref, second_ref, first_ref, cotangent_ref, gain_ref, shift_ref, result_ref, wide_ref, grad_ref, sums_ref
):
    second = second_ref[...]
    norm, root = norm_rows(first_ref[...].astype(F32) + second)
    valid = valid_rows(len_ref)
    gain = gain_ref[...]
    result_ref[...] = ((norm * gain + shift_ref[...]) * valid).astype(BF)
    grad_out = cotangent_ref[...].astype(F32) * valid
    wide = norm_back(grad_out * gain, norm, root)
    grad = wide.astype(BF)
    wide_ref[...] = wide
    grad_ref[...] = grad
    add_rows(sums_ref, (grad_out * norm, grad_out, grad.astype(F32), valid * second * second))


def first_back_kernel(
    grad_ref, norm_ref, root_ref, gain_ref, mixed_ref, wo_ref, wide_ref, gmixed_ref, gweight_ref, sums_ref, total
):
    i = pl.program_id(0)
    width = norm_ref.shape[1]
    wo = wo_ref[...].reshape(width, width)
    grad_first = grad_ref[...]
    norm = norm_ref[...]
    wide = norm_back(grad_first * gain_ref[...], norm, root_ref[:, 0:1])
    grad = wide.astype(BF)
    wide_ref[...] = wide
    gmixed_ref[...] = lax.dot_general(grad, wo, NT, preferred_element_type=F32).astype(BF)
    part = lax.dot_general(mixed_ref[...], grad, TN, preferred_element_type=F32)

    @pl.when(i == 0)
    def _():
        total[...] = part

    @pl.when(i > 0)
    def _():
        total[...] += part

    @pl.when(i == pl.num_programs(0) - 1)
    def _():
        gweight_ref[...] = total[...].astype(BF)

    add_rows(sums_ref, (grad_first * norm, grad_first, grad.astype(F32)))


def norm_call(kernel, name, size, width, inputs, outputs, scratch=(), lens=None):
    prefetch = 0 if lens is None else 1

    def spec(kind):
        if kind == "rows":
            return pl.BlockSpec((BR, width), lambda i, *_: (i, 0))
        if kind == "root":
            return pl.BlockSpec((BR, 128), lambda i, *_: (i, 0))
        if kind == "line":
            return pl.BlockSpec((1, width), lambda i, *_: (0, 0))
        if kind == "sums":
            return pl.BlockSpec((8, width), lambda i, *_: (0, 0))
        if kind == "whole":
            return pl.BlockSpec((width, width), lambda i, *_: (0, 0))
        n, slot, r = kind
        return pl.BlockSpec((n, 1, r, width), lambda i, *_: (0, slot, 0, 0))

    shapes = {"rows": (size, width), "root": (size, 128), "sums": (8, width), "whole": (width, width)}
    call = pl.pallas_call(
        kernel,
        out_shape=tuple(jax.ShapeDtypeStruct(shapes[kind], dtype) for kind, dtype in outputs),
        grid_spec=pltpu.PrefetchScalarGridSpec(
            num_scalar_prefetch=prefetch,
            grid=(size // BR,),
            in_specs=[spec(kind) for _, kind in inputs],
            out_specs=[spec(kind) for kind, _ in outputs],
            scratch_shapes=list(scratch),
        ),
        compiler_params=pltpu.CompilerParams(vmem_limit_bytes=40 << 20),
        cost_estimate=COST,
        name=name,
    )
    arrays = [array for array, _ in inputs]
    return call(*arrays) if lens is None else call(lens, *arrays)


def feed_forward_kernel(first_ref, w1_ref, w2_ref, b1_ref, b2_ref, act_ref, slope_ref, second_ref):
    width = first_ref.shape[1]
    w1 = w1_ref[...].reshape(width, width)
    w2 = w2_ref[...].reshape(width, width)

    @pl.when(pl.program_id(0) == 0)
    def _():
        second_ref[...] = jnp.broadcast_to(b2_ref[...], second_ref.shape)

    for start in range(0, first_ref.shape[0], BR):
        at = slice(start, start + BR)
        inner = jnp.dot(first_ref[at, :], w1, preferred_element_type=F32) + b1_ref[...]
        cdf = 0.5 + 0.5 * lax.erf(inner * (0.5**0.5))
        act = (inner * cdf).astype(BF)
        slope = cdf + inner * (jnp.exp2(inner * inner * (-0.5 * LOG2E)) * ((0.5 / math.pi) ** 0.5))
        act_ref[at, :] = act
        slope_ref[at, :] = slope.astype(BF)
        second_ref[at, :] += jnp.dot(act, w2, preferred_element_type=F32)


def weight_specs(feed, fb, first_slot):
    n, slots, r, width = feed.shape
    if n == 1:
        inner = pl.BlockSpec((1, 1, r, width), lambda j: (0, first_slot + j, 0, 0))
        outer = pl.BlockSpec((1, 1, r, width), lambda j: (0, first_slot + fb + j, 0, 0))
    else:
        inner = pl.BlockSpec((n, 1, r, width), lambda j: (0, first_slot + j, 0, 0))
        outer = pl.BlockSpec((n // fb, fb, r, width), lambda j: (j, first_slot // fb + 1, 0, 0))
    return inner, outer


def feed_forward(first, feed, fb, b1, b2):
    size, width = first.shape
    inner_spec, outer_spec = weight_specs(feed, fb, 0)
    block = pl.BlockSpec((size, width), lambda j: (0, j))
    whole = pl.BlockSpec((size, width), lambda j: (0, 0))
    line = pl.BlockSpec((1, width), lambda j: (0, j))
    const = pl.BlockSpec((1, width), lambda j: (0, 0))
    return pl.pallas_call(
        feed_forward_kernel,
        out_shape=(
            jax.ShapeDtypeStruct((size, fb * width), BF),
            jax.ShapeDtypeStruct((size, fb * width), BF),
            jax.ShapeDtypeStruct((size, width), F32),
        ),
        grid=(fb,),
        in_specs=[whole, inner_spec, outer_spec, line, const],
        out_specs=[block, block, whole],
        compiler_params=pltpu.CompilerParams(vmem_limit_bytes=56 << 20),
        cost_estimate=pl.CostEstimate(flops=20 << 30, bytes_accessed=16 << 20, transcendentals=0),
        name="feed_forward",
    )(first, feed, feed, b1, b2)


def outer_gradient_kernel(act_ref, gs_ref, grad_ref):
    grad = lax.dot_general(act_ref[...], gs_ref[...], TN, preferred_element_type=F32)
    grad_ref[...] = grad.astype(BF).reshape(grad_ref.shape)


def outer_gradient(act, gs, feed, fb):
    size, width = gs.shape
    n, _, r, _ = feed.shape
    if n == 1:
        spec = pl.BlockSpec((1, 1, r, width), lambda j: (0, j, 0, 0))
    else:
        spec = pl.BlockSpec((n // fb, fb, r, width), lambda j: (j, 0, 0, 0))
    return pl.pallas_call(
        outer_gradient_kernel,
        out_shape=jax.ShapeDtypeStruct((n, fb, r, width), BF),
        grid=(fb,),
        in_specs=[
            pl.BlockSpec((size, width), lambda j: (0, j)),
            pl.BlockSpec((size, width), lambda j: (0, 0)),
        ],
        out_specs=spec,
        compiler_params=pltpu.CompilerParams(vmem_limit_bytes=40 << 20),
        cost_estimate=COST,
        name="outer_gradient",
    )(act, gs)


def emit(core, grad, mine_ref, away_ref, at, r):
    for index in range(mine_ref.shape[0]):
        even = grad[2 * index * r : (2 * index + 1) * r, :]
        odd = grad[(2 * index + 1) * r : (2 * index + 2) * r, :]
        mine_ref[index, at, :] = jnp.where(core == 0, even, odd)
        away_ref[index, at, :] = jnp.where(core == 0, odd, even)


def feed_backward_kernel(
    me_ref, gs_ref, first_ref, w1_ref, w2_ref, slope_ref, base_ref, mine_ref, away_ref, gfirst_ref, gbias_ref, turned
):
    j = pl.program_id(0)
    size, width = gs_ref.shape
    w1 = w1_ref[...].reshape(width, width)
    w2 = w2_ref[...].reshape(width, width)

    @pl.when(j == 0)
    def _():
        gfirst_ref[...] = base_ref[...]
        turned[...] = first_ref[...].T

    total = jnp.zeros((1, width), F32)
    pieces = []
    for start in range(0, size, BR):
        at = slice(start, start + BR)
        wide = lax.dot_general(gs_ref[at, :], w2, NT, preferred_element_type=F32) * slope_ref[at, :].astype(F32)
        piece = wide.astype(BF)
        total += jnp.sum(piece.astype(F32), 0, keepdims=True)
        gfirst_ref[at, :] += lax.dot_general(piece, w1, NT, preferred_element_type=F32)
        pieces.append(piece)
    gbias_ref[...] = total
    grad = jnp.dot(turned[...], jnp.concatenate(pieces, 0), preferred_element_type=F32).astype(BF)
    emit(me_ref[0] & 1, grad, mine_ref, away_ref, slice(None), mine_ref.shape[1])


def feed_backward(me, gs, first, feed, fb, slope, base, r):
    size, width = first.shape
    half = width // r // 2
    inner_spec, outer_spec = weight_specs(feed, fb, 0)
    wrap = lambda spec: pl.BlockSpec(spec.block_shape, lambda j, m, f=spec.index_map: f(j))
    block = pl.BlockSpec((size, width), lambda j, m: (0, j))
    whole = pl.BlockSpec((size, width), lambda j, m: (0, 0))
    sides = pl.BlockSpec((half, r, width), lambda j, m: (0, j, 0))
    side = jax.ShapeDtypeStruct((half, fb * r, width), BF)
    return pl.pallas_call(
        feed_backward_kernel,
        out_shape=(
            side,
            side,
            jax.ShapeDtypeStruct((size, width), F32),
            jax.ShapeDtypeStruct((1, fb * width), F32),
        ),
        grid_spec=pltpu.PrefetchScalarGridSpec(
            num_scalar_prefetch=1,
            grid=(fb,),
            in_specs=[whole, whole, wrap(inner_spec), wrap(outer_spec), block, whole],
            out_specs=[sides, sides, whole, pl.BlockSpec((1, width), lambda j, m: (0, j))],
            scratch_shapes=[pltpu.VMEM((width, size), BF)],
        ),
        compiler_params=pltpu.CompilerParams(vmem_limit_bytes=60 << 20),
        cost_estimate=COST,
        name="feed_backward",
    )(me, gs, first, feed, feed, slope, base)


def send(value, bit):
    n = lax.axis_size("dp")
    return lax.ppermute(value, "dp", [(i, i ^ (1 << bit)) for i in range(n)])


def double(value, bit):
    return jnp.concatenate((value, send(value, bit)), 0)


def split_core(blocks):
    pairs = blocks.reshape((blocks.shape[0] // 2, 2) + blocks.shape[1:])
    core = lax.axis_index("dp") & 1
    take = lambda index: lax.dynamic_index_in_dim(pairs, index, 1, keepdims=False)
    return take(core), take(1 - core)


def reduce_steps(mine, away, cut):
    bits = mine.shape[0].bit_length()
    me = lax.axis_index("dp")

    def split(value, left, bit):
        axis = left.index(bit)
        here = (me >> bit) & 1
        other = lax.dynamic_index_in_dim(value, 1 - here, axis, keepdims=False)
        kept = lax.dynamic_index_in_dim(value, here, axis, keepdims=False)
        return kept, other, [b for b in left if b != bit]

    (got,) = yield [send(away, 0)]
    value = (mine.astype(F32) + got.astype(F32)).astype(BF).reshape((2,) * (bits - 1) + mine.shape[1:])
    axis = value.ndim - 2
    pieces = [lax.slice_in_dim(value, low, high, axis=axis) for low, high in ((0, cut), (cut, mine.shape[1]))]
    lefts = [list(range(bits - 1, 0, -1))] * 2
    for turn in ((1, 2), (2, 1)):
        parted = [split(piece, left, bit) for piece, left, bit in zip(pieces, lefts, turn)]
        gots = yield [send(other, bit) for (_, other, _), bit in zip(parted, turn)]
        pieces = [(kept.astype(F32) + got.astype(F32)).astype(BF) for (kept, _, _), got in zip(parted, gots)]
        lefts = [left for _, _, left in parted]
    value, left = jnp.concatenate(pieces, axis - 2), lefts[0]
    for bit in range(3, bits):
        kept, other, left = split(value.astype(BF), left, bit)
        (got,) = yield [send(other, bit)]
        value = kept.astype(F32) + got.astype(F32)
    return value


def finish(steps, received):
    while True:
        try:
            received = steps.send(received)
        except StopIteration as end:
            return end.value


def local(
    hidden,
    cotangent,
    lengths,
    permutation,
    query_weight,
    key_weight,
    value_weight,
    output_weight,
    query_bias,
    value_bias,
    output_bias,
    first_gain,
    first_shift,
    inner_weight,
    inner_bias,
    outer_weight,
    outer_bias,
    second_gain,
    second_shift,
):
    n = lax.axis_size("dp")
    me = lax.axis_index("dp")
    seq_count, part_len, width = hidden.shape
    assert seq_count == n
    length = part_len * n
    r = query_weight.shape[0]
    ff = inner_weight.shape[1]
    fb = ff // width

    def exchange(dealt):
        return lax.all_to_all(dealt, "dp", split_axis=0, concat_axis=0, tiled=True).reshape(length, width)

    dealt_hidden = jnp.take(hidden, permutation, axis=0, mode="clip")

    def collect(values):
        return lax.all_to_all(values.reshape(n, part_len, width), "dp", split_axis=0, concat_axis=0, tiled=True)

    slabs = r % 32 == 0 and n >= 8
    me_ref = me.astype(jnp.int32).reshape(1)
    tied = lax.optimization_barrier
    small = jnp.concatenate(
        (query_bias, value_bias, output_bias, first_gain, first_shift, outer_bias, second_gain, second_shift, inner_bias)
    )
    feed_pack = jnp.concatenate(
        (jnp.moveaxis(inner_weight.reshape(r, fb, width), 1, 0), outer_weight.reshape(fb, r, width), output_weight[None]), 0
    )
    if slabs:
        top, orders = gather_orders(n)
        line = jnp.pad(small[None], ((0, 15), (0, width - small.shape[0])))
        pack = jnp.concatenate((query_weight, key_weight, value_weight, line), 0)[None]
        pack, dealt_hidden = lax.optimization_barrier((pack, dealt_hidden))
        rows = exchange(dealt_hidden)
        for step, bit in enumerate(top):
            pack = double(pack, bit)
            if step == 0:
                pack, feed_pack = tied((pack, feed_pack))
        cut = 3 * r // 2
        pieces = [pack[:, :cut], pack[:, cut:]]
        for step in (-2, -1):
            pieces = [double(piece, order[step]) for piece, order in zip(pieces, orders)]
        got = [send(piece, 0) for piece in pieces]
        lines = jnp.concatenate((pieces[1][:, cut], got[1][:, cut]), 0)[:, : small.shape[0]]
        apart = me ^ jnp.arange(n, dtype=jnp.int32)
        index = sum(((apart >> bit) & 1) << k for k, bit in enumerate(orders[1])) + (apart & 1) * (n // 2)
        small = jnp.take(lines, index, axis=0, mode="clip")
    else:
        rows = exchange(dealt_hidden)
        small = lax.all_to_all(
            jnp.broadcast_to(small[None], (n, small.shape[0])), "dp", split_axis=0, concat_axis=0, tiled=True
        )
    feed = lax.all_gather(feed_pack, "dp", axis=0, tiled=False)
    full_output = None if slabs else feed[:, 2 * fb].reshape(width, width)
    vectors = [small[:, i * r : (i + 1) * r].reshape(1, width).astype(F32) for i in range(8)]
    full_query_bias, full_value_bias, full_output_bias, full_first_gain, full_first_shift = vectors[:5]
    full_outer_bias, full_second_gain, full_second_shift = vectors[5:]
    full_inner_bias = small[:, 8 * r :].reshape(1, ff).astype(F32)
    bias = jnp.stack((full_query_bias, jnp.zeros_like(full_query_bias), full_value_bias))
    if slabs:
        qkv, weights = project(me_ref, (pieces[0], got[0], pieces[1], got[1]), rows, bias, r)
    else:
        feed = jnp.concatenate(
            (
                jnp.moveaxis(feed[:, :fb], 1, 0).reshape(1, fb, width, width),
                feed[:, fb : 2 * fb].reshape(1, fb, width, width),
            ),
            1,
        )
        gathered = lax.all_gather(jnp.stack((query_weight, key_weight, value_weight)), "dp", axis=0, tiled=False)
        weights = jnp.moveaxis(gathered, 1, 0).reshape(3, width, width)
        qkv = jnp.stack([(matmul(rows, weights[i]) + bias[i]).astype(BF) for i in range(3)])
    dealt_cotangent = jnp.take(cotangent, permutation, axis=0, mode="clip")
    dealt_cotangent, qkv = lax.optimization_barrier((dealt_cotangent, qkv))
    arrived_cotangent = exchange(dealt_cotangent)

    my_len = lax.dynamic_slice_in_dim(lengths, me, 1)
    mixed, lse = attention_forward(my_len, qkv)
    wo = (feed, (n, 2 * fb, r)) if slabs else (full_output[None, None], (1, 0, width))
    first, first_norm, first_root, first_sums = norm_call(
        first_norm_kernel,
        "first_norm",
        length,
        width,
        (
            (mixed, "rows"),
            wo,
            (full_output_bias, "line"),
            (rows, "rows"),
            (full_first_gain, "line"),
            (full_first_shift, "line"),
        ),
        (("rows", BF), ("rows", F32), ("root", F32), ("sums", F32)),
        lens=my_len,
    )
    act, slope, second = feed_forward(first, feed, fb, full_inner_bias, full_outer_bias)
    arrived_cotangent, second = tied((arrived_cotangent, second))
    result, grad_res2, grad_second, second_sums = norm_call(
        second_norm_kernel,
        "second_norm",
        length,
        width,
        (
            (second, "rows"),
            (first, "rows"),
            (arrived_cotangent, "rows"),
            (full_second_gain, "line"),
            (full_second_shift, "line"),
        ),
        (("rows", BF), ("rows", F32), ("rows", BF), ("sums", F32)),
        lens=my_len,
    )
    grad_second, second_sums, result = tied((grad_second, second_sums, result))
    second_gain_grad, second_shift_grad, outer_bias_grad = second_sums[0], second_sums[1], second_sums[2]
    squares = jnp.stack((jnp.sum(first_sums[0]), jnp.sum(first_sums[1]), jnp.sum(second_sums[3])))
    out_back = collect(result)
    outer_blocks = outer_gradient(act, grad_second, feed, fb)
    outer_blocks, grad_second = tied((outer_blocks, grad_second))
    outer_owned = lax.psum_scatter(
        outer_blocks.reshape(n, r * fb, width), "dp", scatter_dimension=0, tiled=True
    ).astype(F32)[0]
    if slabs:
        mine, away, grad_first, inner_bias_grad = feed_backward(
            me_ref, grad_second, first, feed, fb, slope, grad_res2, r
        )
    else:
        even, odd, grad_first, inner_bias_grad = feed_backward(
            jnp.zeros_like(me_ref), grad_second, first, feed, fb, slope, grad_res2, width // 2
        )
        blocks = jnp.stack((even[0], odd[0])).reshape(2, fb, width // 2, width)
        blocks = jnp.moveaxis(blocks, 1, 2).reshape(n, r, fb, width)
        mine, away = split_core(jnp.moveaxis(blocks, 2, 1).reshape(n, fb * r, width))
    inner_steps = reduce_steps(mine, away, fb * r // 2)
    out_back, grad_first, inner_bias_grad, mine, away = tied((out_back, grad_first, inner_bias_grad, mine, away))
    moving = next(inner_steps)
    inverse = jnp.zeros(seq_count, jnp.int32).at[permutation].set(jnp.arange(seq_count, dtype=jnp.int32))
    layer_out = jnp.take(out_back, inverse, axis=0, mode="clip")

    grad_res1, grad_mixed, output_weight_grad, back_sums = norm_call(
        first_back_kernel,
        "first_back",
        length,
        width,
        (
            (grad_first, "rows"),
            (first_norm, "rows"),
            (first_root, "root"),
            (full_first_gain, "line"),
            (mixed, "rows"),
            wo,
        ),
        (("rows", F32), ("rows", BF), ("whole", BF), ("sums", F32)),
        scratch=(pltpu.VMEM((width, width), F32),),
    )
    first_gain_grad, first_shift_grad, output_bias_grad = back_sums[0], back_sums[1], back_sums[2]
    moving, grad_mixed, output_weight_grad = tied((moving, grad_mixed, output_weight_grad))
    moving = inner_steps.send(moving)
    grads = attention_backward(my_len, qkv, mixed, grad_mixed, lse)
    moving, grads = tied((moving, grads))
    moving = inner_steps.send(moving)
    if slabs:
        input_grad, mine, away, sums3 = project_back(me_ref, rows, grads, weights, grad_res1, output_weight_grad, r)
        query_bias_grad, value_bias_grad = sums3[0, 0], sums3[2, 0]
        moving, input_grad, mine, away = tied((moving, input_grad, mine, away))
    else:
        input_grad = grad_res1 + sum(right_product(grads[i], weights[i]) for i in range(3))
        input_grad = input_grad.astype(BF)
        blocks = [left_product(rows, grads[i]).astype(BF) for i in range(3)] + [output_weight_grad]
        blocks = jnp.concatenate([g.reshape(n, r, width) for g in blocks] + [jnp.zeros((n, SPARE, width), BF)], 1)
        mine, away = split_core(blocks)
        query_bias_grad, value_bias_grad = column_sum(grads[0]), column_sum(grads[2])
    input_back = collect(input_grad)
    vector_grads = [
        query_bias_grad,
        value_bias_grad,
        output_bias_grad,
        first_gain_grad,
        first_shift_grad,
        outer_bias_grad,
        second_gain_grad,
        second_shift_grad,
        inner_bias_grad,
    ]
    spread = jnp.concatenate([g.reshape(n, -1) for g in vector_grads] + [jnp.broadcast_to(squares[None], (n, 3))], 1)
    spread = jnp.pad(spread.astype(BF), ((0, 0), (0, width - spread.shape[1])))[:, None]
    spread_mine, spread_away = split_core(spread)
    mine = lax.dynamic_update_slice(mine, spread_mine, (0, 4 * r, 0))
    away = lax.dynamic_update_slice(away, spread_away, (0, 4 * r, 0))
    inner_owned = finish(inner_steps, moving)
    steps = reduce_steps(mine, away, 2 * r)
    reduced = finish(steps, next(steps))
    attention_owned, owned = reduced[: 4 * r], reduced[4 * r]
    sums = owned[8 * r + ff // n : 8 * r + ff // n + 3]

    input_gradient = jnp.take(input_back, inverse, axis=0, mode="clip")
    rms = jnp.sqrt(sums / (jnp.sum(lengths).astype(F32) * width))
    return (
        layer_out,
        input_gradient,
        attention_owned[:r],
        attention_owned[r : 2 * r],
        attention_owned[2 * r : 3 * r],
        attention_owned[3 * r :],
        owned[:r],
        owned[r : 2 * r],
        owned[2 * r : 3 * r],
        owned[3 * r : 4 * r],
        owned[4 * r : 5 * r],
        jnp.moveaxis(inner_owned.reshape(fb, r, width), 0, 1).reshape(r, ff),
        owned[8 * r : 8 * r + ff // n],
        outer_owned,
        owned[5 * r : 6 * r],
        owned[6 * r : 7 * r],
        owned[7 * r : 8 * r],
        rms[0],
        rms[1],
        rms[2],
    )


def solution(mesh):
    seq, mat, vec = P(None, "dp", None), P("dp", None), P("dp")
    return jax.shard_map(
        local,
        mesh=mesh,
        in_specs=(seq, seq, P(), P(), mat, mat, mat, mat, vec, vec, vec, vec, vec, mat, vec, mat, vec, vec, vec),
        out_specs=(seq, seq, mat, mat, mat, mat, vec, vec, vec, vec, vec, mat, vec, mat, vec, vec, vec, P(), P(), P()),
        check_vma=False,
    )
```

```python
import functools
import math

import jax
import jax.numpy as jnp
from jax import lax
from jax.experimental import pallas as pl
from jax.experimental.pallas import tpu as pltpu
from jax.sharding import PartitionSpec as P

HEADS = 16
EPS = 1e-05
NEG = -1e30
LOG2E = math.log2(math.e)
BF = jnp.bfloat16
F32 = jnp.float32
BQ = 1024
BR = 256
SPARE = 16
COST = pl.CostEstimate(flops=1 << 20, bytes_accessed=1 << 20, transcendentals=0)
NT = (((1,), (1,)), ((), ()))
TN = (((0,), (0,)), ((), ()))


def matmul(left, right):
    return jnp.dot(left, right, preferred_element_type=F32)


def left_product(left, right):
    return lax.dot_general(left, right, TN, preferred_element_type=F32)


def right_product(left, right):
    return lax.dot_general(left, right, NT, preferred_element_type=F32)


def column_sum(values):
    return jnp.sum(values.astype(F32), 0)


def head_keys(k, lane, half, key_bias):
    own = (lane >= 64 * half) & (lane < 64 * half + 64)
    spare = lane == 64 * (1 - half)
    return jnp.where(own, k, jnp.where(spare, key_bias, jnp.zeros_like(k)))


def head_queries(q, lane, half):
    return jnp.where(lane == 64 * (1 - half), jnp.ones_like(q), q)


def forward_kernel(len_ref, q_ref, k_ref, v_ref, o_ref, lse_ref, kh, vt):
    qi = pl.program_id(1)
    size = k_ref.shape[1]
    length = len_ref[0]

    @pl.when(qi == 0)
    def _():
        lane = lax.broadcasted_iota(jnp.int32, (size, 128), 1)
        row = lax.broadcasted_iota(jnp.int32, (size, 128), 0)
        key_bias = jnp.where(row < length, 0.0, NEG).astype(BF)
        k = k_ref[0]
        for half in (0, 1):
            kh[half] = head_keys(k, lane, half, key_bias)
        vt[...] = v_ref[0].T

    @pl.when(qi * BQ < length)
    def _():
        q = q_ref[0]
        lane = lax.broadcasted_iota(jnp.int32, q.shape, 1)
        scale = 0.125 * LOG2E
        outs = []
        for half in (0, 1):
            st = lax.dot_general(kh[half], head_queries(q, lane, half), NT, preferred_element_type=F32)
            peak = jnp.max(st, 0, keepdims=True) * scale
            pt = jnp.exp2(st * scale - peak)
            total = jnp.sum(pt, 0, keepdims=True)
            ot = jnp.dot(vt[64 * half : 64 * half + 64, :], pt.astype(BF), preferred_element_type=F32)
            outs.append(ot / total)
            lse_ref[0, half : half + 1, :] = peak + jnp.log2(total)
        o_ref[...] = jnp.concatenate(outs, 0).T.astype(BF)

    @pl.when(qi * BQ >= length)
    def _():
        o_ref[...] = jnp.zeros_like(o_ref)
        lse_ref[...] = jnp.zeros_like(lse_ref)


def qkv_specs(size):
    return [
        pl.BlockSpec((1, BQ, 128), lambda h, i, n: (0, i, h)),
        pl.BlockSpec((1, size, 128), lambda h, i, n: (1, 0, h)),
        pl.BlockSpec((1, size, 128), lambda h, i, n: (2, 0, h)),
    ]


def attention_forward(lens, qkv):
    _, size, width = qkv.shape
    pairs = width // 128
    return pl.pallas_call(
        forward_kernel,
        out_shape=(
            jax.ShapeDtypeStruct((size, width), BF),
            jax.ShapeDtypeStruct((pairs, 8, size), F32),
        ),
        grid_spec=pltpu.PrefetchScalarGridSpec(
            num_scalar_prefetch=1,
            grid=(pairs, size // BQ),
            in_specs=qkv_specs(size),
            out_specs=[
                pl.BlockSpec((BQ, 128), lambda h, i, n: (i, h)),
                pl.BlockSpec((1, 8, BQ), lambda h, i, n: (h, 0, i)),
            ],
            scratch_shapes=[pltpu.VMEM((2, size, 128), BF), pltpu.VMEM((128, size), BF)],
        ),
        compiler_params=pltpu.CompilerParams(vmem_limit_bytes=60 << 20),
        cost_estimate=pl.CostEstimate(flops=32 << 30, bytes_accessed=16 << 20, transcendentals=0),
        name="attention_forward",
    )(lens, qkv, qkv, qkv)


def backward_kernel(len_ref, q_ref, k_ref, v_ref, o_ref, g_ref, lse_ref, out_ref, kh, vh, kt, dka, dva):
    qi = pl.program_id(1)
    size = k_ref.shape[1]
    length = len_ref[0]
    here = pl.ds(pl.multiple_of(qi * BQ, BQ), BQ)

    @pl.when(qi == 0)
    def _():
        lane = lax.broadcasted_iota(jnp.int32, (size, 128), 1)
        row = lax.broadcasted_iota(jnp.int32, (size, 128), 0)
        key_bias = jnp.where(row < length, 0.0, NEG).astype(BF)
        k = k_ref[0]
        v = v_ref[0]
        for half in (0, 1):
            kh[half] = head_keys(k, lane, half, key_bias)
            vh[half] = head_keys(v, lane, half, jnp.zeros_like(v))
        kt[...] = k.T
        dka[...] = jnp.zeros_like(dka)
        dva[...] = jnp.zeros_like(dva)

    @pl.when(qi * BQ < length)
    def _():
        q = q_ref[0]
        g = g_ref[...]
        lane = lax.broadcasted_iota(jnp.int32, q.shape, 1)
        scale = 0.125 * LOG2E
        dots = (g.astype(F32) * o_ref[...].astype(F32)).T
        outs = []
        for half in (0, 1):
            qh = head_queries(q, lane, half)
            st = lax.dot_general(kh[half], qh, NT, preferred_element_type=F32)
            pt = jnp.exp2(st * scale - lse_ref[0, half : half + 1, :])
            dpt = lax.dot_general(vh[half], g, NT, preferred_element_type=F32)
            delta = jnp.sum(dots[64 * half : 64 * half + 64, :], 0, keepdims=True)
            dst = (pt * (dpt - delta)).astype(BF)
            dva[half] += jnp.dot(pt.astype(BF), g, preferred_element_type=F32)
            dka[half] += jnp.dot(dst, qh, preferred_element_type=F32)
            outs.append(jnp.dot(kt[64 * half : 64 * half + 64, :], dst, preferred_element_type=F32))
        out_ref[0, here, :] = (jnp.concatenate(outs, 0) * 0.125).T.astype(BF)

    @pl.when(qi * BQ >= length)
    def _():
        out_ref[0, here, :] = jnp.zeros((BQ, 128), BF)

    @pl.when(qi == pl.num_programs(1) - 1)
    def _():
        lane = lax.broadcasted_iota(jnp.int32, (size, 128), 1)
        out_ref[1] = (jnp.where(lane < 64, dka[0], dka[1]) * 0.125).astype(BF)
        out_ref[2] = jnp.where(lane < 64, dva[0], dva[1]).astype(BF)


def attention_backward(lens, qkv, o, g, lse):
    _, size, width = qkv.shape
    pairs = width // 128
    rows = pl.BlockSpec((BQ, 128), lambda h, i, n: (i, h))
    return pl.pallas_call(
        backward_kernel,
        out_shape=jax.ShapeDtypeStruct((3, size, width), BF),
        grid_spec=pltpu.PrefetchScalarGridSpec(
            num_scalar_prefetch=1,
            grid=(pairs, size // BQ),
            in_specs=qkv_specs(size) + [rows, rows, pl.BlockSpec((1, 8, BQ), lambda h, i, n: (h, 0, i))],
            out_specs=pl.BlockSpec((3, size, 128), lambda h, i, n: (0, 0, h)),
            scratch_shapes=[
                pltpu.VMEM((2, size, 128), BF),
                pltpu.VMEM((2, size, 128), BF),
                pltpu.VMEM((128, size), BF),
                pltpu.VMEM((2, size, 128), F32),
                pltpu.VMEM((2, size, 128), F32),
            ],
        ),
        compiler_params=pltpu.CompilerParams(vmem_limit_bytes=60 << 20),
        cost_estimate=pl.CostEstimate(flops=40 << 30, bytes_accessed=16 << 20, transcendentals=0),
        name="attention_backward",
    )(lens, qkv, qkv, qkv, o, g, lse)


def gather_orders(n):
    top = list(range(n.bit_length() - 2, 2, -1))
    return top, (top + [2, 1], top + [1, 2])


def distance(index, order):
    return sum(((index >> k) & 1) << bit for k, bit in enumerate(order))


def project_kernel(me_ref, a0, a1, b0, b1, x_ref, bias_ref, qkv_ref, w_ref, scratch, *, r, orders):
    j = pl.program_id(0)

    @pl.when(j == 0)
    def _():
        me = me_ref[0]
        half = r // 2
        for core, (a, b) in enumerate(((a0, b0), (a1, b1))):
            for index in range(a.shape[0]):
                off = pl.multiple_of((me ^ (distance(index, orders[0]) | core)) * r, r)
                scratch[0, pl.ds(off, r), :] = a[index, :r, :]
                scratch[1, pl.ds(off, half), :] = a[index, r : r + half, :]
                off = pl.multiple_of((me ^ (distance(index, orders[1]) | core)) * r, r)
                scratch[1, pl.ds(pl.multiple_of(off + half, half), half), :] = b[index, :half, :]
                scratch[2, pl.ds(off, r), :] = b[index, half : half + r, :]

    w = scratch[j]
    w_ref[0] = w
    qkv_ref[0] = (jnp.dot(x_ref[...], w, preferred_element_type=F32) + bias_ref[0]).astype(BF)


def project(me, pieces, x, bias, r):
    size, width = x.shape
    n = width // r
    whole = [pl.BlockSpec(p.shape, lambda j, m: (0, 0, 0)) for p in pieces]
    return pl.pallas_call(
        functools.partial(project_kernel, r=r, orders=gather_orders(n)[1]),
        out_shape=(jax.ShapeDtypeStruct((3, size, width), BF), jax.ShapeDtypeStruct((3, width, width), BF)),
        grid_spec=pltpu.PrefetchScalarGridSpec(
            num_scalar_prefetch=1,
            grid=(3,),
            in_specs=whole
            + [
                pl.BlockSpec((size, width), lambda j, m: (0, 0)),
                pl.BlockSpec((1, 1, width), lambda j, m: (j, 0, 0)),
            ],
            out_specs=[
                pl.BlockSpec((1, size, width), lambda j, m: (j, 0, 0)),
                pl.BlockSpec((1, width, width), lambda j, m: (j, 0, 0)),
            ],
            scratch_shapes=[pltpu.VMEM((3, width, width), BF)],
        ),
        compiler_params=pltpu.CompilerParams(vmem_limit_bytes=60 << 20),
        cost_estimate=pl.CostEstimate(flops=6 << 30, bytes_accessed=16 << 20, transcendentals=0),
        name="project",
    )(me, *pieces, x, bias)


def sum_rows(first_sums, second_sums, back_sums, inner_bias):
    width = first_sums.shape[1]
    rows = [back_sums[k : k + 1, :] for k in (2, 0, 1)] + [second_sums[k : k + 1, :] for k in (2, 0, 1)]
    rows += [inner_bias[0:1, k : k + width] for k in range(0, inner_bias.shape[1], width)]
    return rows + [first_sums[0:1, :], first_sums[1:2, :], second_sums[3:4, :]]


def project_back_kernel(
    me_ref, x_ref, g_ref, w_ref, base_ref, wo_ref, s1_ref, s2_ref, s3_ref, s4_ref, dx_ref, mine_ref, away_ref,
    xt, acc, lines, *, r
):
    j = pl.program_id(0)
    half, _, width = mine_ref.shape

    core = me_ref[0] & 1
    at = pl.ds(pl.multiple_of(j * r, r), r)

    @pl.when(j == 0)
    def _():
        xt[...] = x_ref[...].T
        acc[...] = base_ref[...]
        for k, row in enumerate(sum_rows(s1_ref, s2_ref, s3_ref, s4_ref), 3):
            lines[k : k + 1, :] = row

    @pl.when(j < 3)
    def _():
        g = g_ref[0]
        emit(core, jnp.dot(xt[...], g, preferred_element_type=F32).astype(BF), mine_ref, away_ref, at, r)
        acc[...] += lax.dot_general(g, w_ref[0], NT, preferred_element_type=F32)
        lines[pl.ds(j, 1), :] = jnp.sum(g.astype(F32), 0, keepdims=True)

    @pl.when(j == 3)
    def _():
        emit(core, wo_ref[...], mine_ref, away_ref, at, r)
        block = lines[...].astype(BF)
        for index in range(half):
            mine_ref[index, 4 * r :, :] = block
            away_ref[index, 4 * r :, :] = block
        dx_ref[...] = acc[...].astype(BF)


def project_back(me, x, grads, w, base, output_grad, sums, r):
    size, width = x.shape
    half = width // r // 2
    last = lambda j: jnp.minimum(j, 2)
    whole = pl.BlockSpec((size, width), lambda j, m: (0, 0))
    blocks = pl.BlockSpec((half, 4 * r + SPARE, width), lambda j, m: (0, 0, 0))
    return pl.pallas_call(
        functools.partial(project_back_kernel, r=r),
        out_shape=(
            jax.ShapeDtypeStruct((size, width), BF),
            jax.ShapeDtypeStruct((half, 4 * r + SPARE, width), BF),
            jax.ShapeDtypeStruct((half, 4 * r + SPARE, width), BF),
        ),
        grid_spec=pltpu.PrefetchScalarGridSpec(
            num_scalar_prefetch=1,
            grid=(4,),
            in_specs=[
                whole,
                pl.BlockSpec((1, size, width), lambda j, m: (last(j), 0, 0)),
                pl.BlockSpec((1, width, width), lambda j, m: (last(j), 0, 0)),
                whole,
                pl.BlockSpec((width, width), lambda j, m: (0, 0)),
            ]
            + [pl.BlockSpec(value.shape, lambda j, m: (0, 0)) for value in sums],
            out_specs=[whole, blocks, blocks],
            scratch_shapes=[
                pltpu.VMEM((width, size), BF),
                pltpu.VMEM((size, width), F32),
                pltpu.VMEM((SPARE, width), F32),
            ],
        ),
        compiler_params=pltpu.CompilerParams(vmem_limit_bytes=60 << 20),
        cost_estimate=pl.CostEstimate(flops=12 << 30, bytes_accessed=16 << 20, transcendentals=0),
        name="project_back",
    )(me, x, grads, w, base, output_grad, *sums)


def norm_rows(resid):
    center = resid - jnp.mean(resid, -1, keepdims=True)
    inverse_root = lax.rsqrt(jnp.mean(center * center, -1, keepdims=True) + EPS)
    return center * inverse_root, inverse_root


def norm_back(grad, norm, inverse_root):
    return (grad - jnp.mean(grad, -1, keepdims=True) - norm * jnp.mean(grad * norm, -1, keepdims=True)) * inverse_root


def valid_rows(len_ref):
    row = pl.program_id(0) * BR + lax.broadcasted_iota(jnp.int32, (BR, 1), 0)
    return (row < len_ref[0]).astype(F32)


def add_rows(sums_ref, values):
    @pl.when(pl.program_id(0) == 0)
    def _():
        sums_ref[...] = jnp.zeros_like(sums_ref)

    for k, value in enumerate(values):
        sums_ref[k : k + 1, :] += jnp.sum(value, 0, keepdims=True)


def first_norm_kernel(
    len_ref, mixed_ref, wo_ref, bias_ref, x_ref, gain_ref, shift_ref, first_ref, norm_ref, root_ref, sums_ref
):
    width = x_ref.shape[1]
    wo = wo_ref[...].reshape(width, width)
    branch = jnp.dot(mixed_ref[...], wo, preferred_element_type=F32) + bias_ref[...]
    x = x_ref[...].astype(F32)
    norm, root = norm_rows(x + branch)
    first_ref[...] = (norm * gain_ref[...] + shift_ref[...]).astype(BF)
    norm_ref[...] = norm
    root_ref[...] = jnp.broadcast_to(root, root_ref.shape)
    valid = valid_rows(len_ref)
    add_rows(sums_ref, (valid * x * x, valid * branch * branch))


def second_norm_kernel(
    len_ref, second_ref, first_ref, cotangent_ref, gain_ref, shift_ref, result_ref, wide_ref, grad_ref, sums_ref
):
    second = second_ref[...]
    norm, root = norm_rows(first_ref[...].astype(F32) + second)
    valid = valid_rows(len_ref)
    gain = gain_ref[...]
    result_ref[...] = ((norm * gain + shift_ref[...]) * valid).astype(BF)
    grad_out = cotangent_ref[...].astype(F32) * valid
    wide = norm_back(grad_out * gain, norm, root)
    grad = wide.astype(BF)
    wide_ref[...] = wide
    grad_ref[...] = grad
    add_rows(sums_ref, (grad_out * norm, grad_out, grad.astype(F32), valid * second * second))


def first_back_kernel(
    grad_ref, norm_ref, root_ref, gain_ref, mixed_ref, wo_ref, wide_ref, gmixed_ref, gweight_ref, sums_ref, total
):
    i = pl.program_id(0)
    width = norm_ref.shape[1]
    wo = wo_ref[...].reshape(width, width)
    grad_first = grad_ref[...]
    norm = norm_ref[...]
    wide = norm_back(grad_first * gain_ref[...], norm, root_ref[:, 0:1])
    grad = wide.astype(BF)
    wide_ref[...] = wide
    gmixed_ref[...] = lax.dot_general(grad, wo, NT, preferred_element_type=F32).astype(BF)
    part = lax.dot_general(mixed_ref[...], grad, TN, preferred_element_type=F32)

    @pl.when(i == 0)
    def _():
        total[...] = part

    @pl.when(i > 0)
    def _():
        total[...] += part

    @pl.when(i == pl.num_programs(0) - 1)
    def _():
        gweight_ref[...] = total[...].astype(BF)

    add_rows(sums_ref, (grad_first * norm, grad_first, grad.astype(F32)))


def norm_call(kernel, name, size, width, inputs, outputs, scratch=(), lens=None):
    prefetch = 0 if lens is None else 1

    def spec(kind):
        if kind == "rows":
            return pl.BlockSpec((BR, width), lambda i, *_: (i, 0))
        if kind == "root":
            return pl.BlockSpec((BR, 128), lambda i, *_: (i, 0))
        if kind == "line":
            return pl.BlockSpec((1, width), lambda i, *_: (0, 0))
        if kind == "sums":
            return pl.BlockSpec((8, width), lambda i, *_: (0, 0))
        if kind == "whole":
            return pl.BlockSpec((width, width), lambda i, *_: (0, 0))
        n, slot, r = kind
        return pl.BlockSpec((n, 1, r, width), lambda i, *_: (0, slot, 0, 0))

    shapes = {"rows": (size, width), "root": (size, 128), "sums": (8, width), "whole": (width, width)}
    call = pl.pallas_call(
        kernel,
        out_shape=tuple(jax.ShapeDtypeStruct(shapes[kind], dtype) for kind, dtype in outputs),
        grid_spec=pltpu.PrefetchScalarGridSpec(
            num_scalar_prefetch=prefetch,
            grid=(size // BR,),
            in_specs=[spec(kind) for _, kind in inputs],
            out_specs=[spec(kind) for kind, _ in outputs],
            scratch_shapes=list(scratch),
        ),
        compiler_params=pltpu.CompilerParams(vmem_limit_bytes=60 << 20),
        cost_estimate=COST,
        name=name,
    )
    arrays = [array for array, _ in inputs]
    return call(*arrays) if lens is None else call(lens, *arrays)


def feed_forward_kernel(first_ref, w1_ref, w2_ref, b1_ref, b2_ref, act_ref, slope_ref, second_ref):
    width = first_ref.shape[1]
    w1 = w1_ref[...].reshape(width, width)
    w2 = w2_ref[...].reshape(width, width)

    @pl.when(pl.program_id(0) == 0)
    def _():
        second_ref[...] = jnp.broadcast_to(b2_ref[...], second_ref.shape)

    for start in range(0, first_ref.shape[0], BR):
        at = slice(start, start + BR)
        inner = jnp.dot(first_ref[at, :], w1, preferred_element_type=F32) + b1_ref[...]
        cdf = 0.5 + 0.5 * lax.erf(inner * (0.5**0.5))
        act = (inner * cdf).astype(BF)
        slope = cdf + inner * (jnp.exp2(inner * inner * (-0.5 * LOG2E)) * ((0.5 / math.pi) ** 0.5))
        act_ref[at, :] = act
        slope_ref[at, :] = slope.astype(BF)
        second_ref[at, :] += jnp.dot(act, w2, preferred_element_type=F32)


def weight_specs(feed, fb, first_slot):
    n, slots, r, width = feed.shape
    if n == 1:
        inner = pl.BlockSpec((1, 1, r, width), lambda j: (0, first_slot + j, 0, 0))
        outer = pl.BlockSpec((1, 1, r, width), lambda j: (0, first_slot + fb + j, 0, 0))
    else:
        inner = pl.BlockSpec((n, 1, r, width), lambda j: (0, first_slot + j, 0, 0))
        outer = pl.BlockSpec((n // fb, fb, r, width), lambda j: (j, first_slot // fb + 1, 0, 0))
    return inner, outer


def feed_forward(first, feed, fb, b1, b2):
    size, width = first.shape
    inner_spec, outer_spec = weight_specs(feed, fb, 0)
    block = pl.BlockSpec((size, width), lambda j: (0, j))
    whole = pl.BlockSpec((size, width), lambda j: (0, 0))
    line = pl.BlockSpec((1, width), lambda j: (0, j))
    const = pl.BlockSpec((1, width), lambda j: (0, 0))
    return pl.pallas_call(
        feed_forward_kernel,
        out_shape=(
            jax.ShapeDtypeStruct((size, fb * width), BF),
            jax.ShapeDtypeStruct((size, fb * width), BF),
            jax.ShapeDtypeStruct((size, width), F32),
        ),
        grid=(fb,),
        in_specs=[whole, inner_spec, outer_spec, line, const],
        out_specs=[block, block, whole],
        compiler_params=pltpu.CompilerParams(vmem_limit_bytes=60 << 20),
        cost_estimate=pl.CostEstimate(flops=20 << 30, bytes_accessed=16 << 20, transcendentals=0),
        name="feed_forward",
    )(first, feed, feed, b1, b2)


def outer_gradient_kernel(act_ref, gs_ref, grad_ref):
    grad = lax.dot_general(act_ref[...], gs_ref[...], TN, preferred_element_type=F32)
    grad_ref[...] = grad.astype(BF).reshape(grad_ref.shape)


def outer_gradient(act, gs, feed, fb):
    size, width = gs.shape
    n, _, r, _ = feed.shape
    if n == 1:
        spec = pl.BlockSpec((1, 1, r, width), lambda j: (0, j, 0, 0))
    else:
        spec = pl.BlockSpec((n // fb, fb, r, width), lambda j: (j, 0, 0, 0))
    return pl.pallas_call(
        outer_gradient_kernel,
        out_shape=jax.ShapeDtypeStruct((n, fb, r, width), BF),
        grid=(fb,),
        in_specs=[
            pl.BlockSpec((size, width), lambda j: (0, j)),
            pl.BlockSpec((size, width), lambda j: (0, 0)),
        ],
        out_specs=spec,
        compiler_params=pltpu.CompilerParams(vmem_limit_bytes=60 << 20),
        cost_estimate=COST,
        name="outer_gradient",
    )(act, gs)


def emit(core, grad, mine_ref, away_ref, at, r):
    for index in range(mine_ref.shape[0]):
        even = grad[2 * index * r : (2 * index + 1) * r, :]
        odd = grad[(2 * index + 1) * r : (2 * index + 2) * r, :]
        mine_ref[index, at, :] = jnp.where(core == 0, even, odd)
        away_ref[index, at, :] = jnp.where(core == 0, odd, even)


def feed_backward_kernel(
    me_ref, gs_ref, first_ref, w1_ref, w2_ref, slope_ref, base_ref, mine_ref, away_ref, gfirst_ref, gbias_ref, turned
):
    j = pl.program_id(0)
    size, width = gs_ref.shape
    w1 = w1_ref[...].reshape(width, width)
    w2 = w2_ref[...].reshape(width, width)

    @pl.when(j == 0)
    def _():
        gfirst_ref[...] = base_ref[...]
        turned[...] = first_ref[...].T

    total = jnp.zeros((1, width), F32)
    pieces = []
    for start in range(0, size, BR):
        at = slice(start, start + BR)
        wide = lax.dot_general(gs_ref[at, :], w2, NT, preferred_element_type=F32) * slope_ref[at, :].astype(F32)
        piece = wide.astype(BF)
        total += jnp.sum(piece.astype(F32), 0, keepdims=True)
        gfirst_ref[at, :] += lax.dot_general(piece, w1, NT, preferred_element_type=F32)
        pieces.append(piece)
    gbias_ref[...] = total
    grad = jnp.dot(turned[...], jnp.concatenate(pieces, 0), preferred_element_type=F32).astype(BF)
    emit(me_ref[0] & 1, grad, mine_ref, away_ref, slice(None), mine_ref.shape[1])


def feed_backward(me, gs, first, feed, fb, slope, base, r):
    size, width = first.shape
    half = width // r // 2
    inner_spec, outer_spec = weight_specs(feed, fb, 0)
    wrap = lambda spec: pl.BlockSpec(spec.block_shape, lambda j, m, f=spec.index_map: f(j))
    block = pl.BlockSpec((size, width), lambda j, m: (0, j))
    whole = pl.BlockSpec((size, width), lambda j, m: (0, 0))
    sides = pl.BlockSpec((half, r, width), lambda j, m: (0, j, 0))
    side = jax.ShapeDtypeStruct((half, fb * r, width), BF)
    return pl.pallas_call(
        feed_backward_kernel,
        out_shape=(
            side,
            side,
            jax.ShapeDtypeStruct((size, width), F32),
            jax.ShapeDtypeStruct((1, fb * width), F32),
        ),
        grid_spec=pltpu.PrefetchScalarGridSpec(
            num_scalar_prefetch=1,
            grid=(fb,),
            in_specs=[whole, whole, wrap(inner_spec), wrap(outer_spec), block, whole],
            out_specs=[sides, sides, whole, pl.BlockSpec((1, width), lambda j, m: (0, j))],
            scratch_shapes=[pltpu.VMEM((width, size), BF)],
        ),
        compiler_params=pltpu.CompilerParams(vmem_limit_bytes=60 << 20),
        cost_estimate=COST,
        name="feed_backward",
    )(me, gs, first, feed, feed, slope, base)


def send(value, bit):
    n = lax.axis_size("dp")
    return lax.ppermute(value, "dp", [(i, i ^ (1 << bit)) for i in range(n)])


def double(value, bit):
    return jnp.concatenate((value, send(value, bit)), 0)


def split_core(blocks):
    pairs = blocks.reshape((blocks.shape[0] // 2, 2) + blocks.shape[1:])
    core = lax.axis_index("dp") & 1
    take = lambda index: lax.dynamic_index_in_dim(pairs, index, 1, keepdims=False)
    return take(core), take(1 - core)


def reduce_steps(mine, away, cut):
    bits = mine.shape[0].bit_length()
    me = lax.axis_index("dp")

    def split(value, left, bit):
        axis = left.index(bit)
        here = (me >> bit) & 1
        other = lax.dynamic_index_in_dim(value, 1 - here, axis, keepdims=False)
        kept = lax.dynamic_index_in_dim(value, here, axis, keepdims=False)
        return kept, other, [b for b in left if b != bit]

    (got,) = yield [send(away, 0)]
    value = (mine.astype(F32) + got.astype(F32)).astype(BF).reshape((2,) * (bits - 1) + mine.shape[1:])
    axis = value.ndim - 2
    pieces = [lax.slice_in_dim(value, low, high, axis=axis) for low, high in ((0, cut), (cut, mine.shape[1]))]
    lefts = [list(range(bits - 1, 0, -1))] * 2
    for turn in ((1, 2), (2, 1)):
        parted = [split(piece, left, bit) for piece, left, bit in zip(pieces, lefts, turn)]
        gots = yield [send(other, bit) for (_, other, _), bit in zip(parted, turn)]
        pieces = [(kept.astype(F32) + got.astype(F32)).astype(BF) for (kept, _, _), got in zip(parted, gots)]
        lefts = [left for _, _, left in parted]
    value, left = jnp.concatenate(pieces, axis - 2), lefts[0]
    for bit in range(3, bits):
        kept, other, left = split(value.astype(BF), left, bit)
        (got,) = yield [send(other, bit)]
        value = kept.astype(F32) + got.astype(F32)
    return value


def finish(steps, received):
    while True:
        try:
            received = steps.send(received)
        except StopIteration as end:
            return end.value


def local(
    hidden,
    cotangent,
    lengths,
    permutation,
    query_weight,
    key_weight,
    value_weight,
    output_weight,
    query_bias,
    value_bias,
    output_bias,
    first_gain,
    first_shift,
    inner_weight,
    inner_bias,
    outer_weight,
    outer_bias,
    second_gain,
    second_shift,
):
    n = lax.axis_size("dp")
    me = lax.axis_index("dp")
    seq_count, part_len, width = hidden.shape
    assert seq_count == n
    length = part_len * n
    r = query_weight.shape[0]
    ff = inner_weight.shape[1]
    fb = ff // width

    def exchange(dealt):
        return lax.all_to_all(dealt, "dp", split_axis=0, concat_axis=0, tiled=True).reshape(length, width)

    dealt_hidden = jnp.take(hidden, permutation, axis=0, mode="clip")
    dealt_cotangent = jnp.take(cotangent, permutation, axis=0, mode="clip")

    def collect(values):
        return lax.all_to_all(values.reshape(n, part_len, width), "dp", split_axis=0, concat_axis=0, tiled=True)

    slabs = r % 32 == 0 and n >= 8
    me_ref = me.astype(jnp.int32).reshape(1)
    tied = lax.optimization_barrier
    small = jnp.concatenate(
        (query_bias, value_bias, output_bias, first_gain, first_shift, outer_bias, second_gain, second_shift, inner_bias)
    )
    feed_pack = jnp.concatenate(
        [inner_weight[:, i * width : (i + 1) * width] for i in range(fb)] + [outer_weight, output_weight], 0
    ).reshape(2 * fb + 1, r, width)
    if slabs:
        top, orders = gather_orders(n)
        line = jnp.pad(small[None], ((0, 15), (0, width - small.shape[0])))
        pack = jnp.concatenate((query_weight, key_weight, value_weight, line), 0)[None]
        pack, dealt_hidden = lax.optimization_barrier((pack, dealt_hidden))
        rows = exchange(dealt_hidden)
        for step, bit in enumerate(top):
            pack = double(pack, bit)
            if step == 0:
                pack, feed_pack = tied((pack, feed_pack))
            else:
                pack, dealt_cotangent = tied((pack, dealt_cotangent))
        cut = 3 * r // 2
        pieces = [pack[:, :cut], pack[:, cut:]]
        for step in (-2, -1):
            pieces = [double(piece, order[step]) for piece, order in zip(pieces, orders)]
        got = [send(piece, 0) for piece in pieces]
        lines = jnp.concatenate((pieces[1][:, cut], got[1][:, cut]), 0)[:, : small.shape[0]]
        apart = me ^ jnp.arange(n, dtype=jnp.int32)
        index = sum(((apart >> bit) & 1) << k for k, bit in enumerate(orders[1])) + (apart & 1) * (n // 2)
        small = jnp.take(lines, index, axis=0, mode="clip")
    else:
        rows = exchange(dealt_hidden)
        small = lax.all_to_all(
            jnp.broadcast_to(small[None], (n, small.shape[0])), "dp", split_axis=0, concat_axis=0, tiled=True
        )
    feed = lax.all_gather(feed_pack, "dp", axis=0, tiled=False)
    full_output = None if slabs else feed[:, 2 * fb].reshape(width, width)
    vectors = [small[:, i * r : (i + 1) * r].reshape(1, width).astype(F32) for i in range(8)]
    full_query_bias, full_value_bias, full_output_bias, full_first_gain, full_first_shift = vectors[:5]
    full_outer_bias, full_second_gain, full_second_shift = vectors[5:]
    full_inner_bias = small[:, 8 * r :].reshape(1, ff).astype(F32)
    bias = jnp.stack((full_query_bias, jnp.zeros_like(full_query_bias), full_value_bias))
    if slabs:
        qkv, weights = project(me_ref, (pieces[0], got[0], pieces[1], got[1]), rows, bias, r)
    else:
        feed = jnp.concatenate(
            (
                jnp.moveaxis(feed[:, :fb], 1, 0).reshape(1, fb, width, width),
                feed[:, fb : 2 * fb].reshape(1, fb, width, width),
            ),
            1,
        )
        gathered = lax.all_gather(jnp.stack((query_weight, key_weight, value_weight)), "dp", axis=0, tiled=False)
        weights = jnp.moveaxis(gathered, 1, 0).reshape(3, width, width)
        qkv = jnp.stack([(matmul(rows, weights[i]) + bias[i]).astype(BF) for i in range(3)])
    dealt_cotangent, qkv = lax.optimization_barrier((dealt_cotangent, qkv))
    arrived_cotangent = exchange(dealt_cotangent)

    my_len = lax.dynamic_slice_in_dim(lengths, me, 1)
    mixed, lse = attention_forward(my_len, qkv)
    wo = (feed, (n, 2 * fb, r)) if slabs else (full_output[None, None], (1, 0, width))
    first, first_norm, first_root, first_sums = norm_call(
        first_norm_kernel,
        "first_norm",
        length,
        width,
        (
            (mixed, "rows"),
            wo,
            (full_output_bias, "line"),
            (rows, "rows"),
            (full_first_gain, "line"),
            (full_first_shift, "line"),
        ),
        (("rows", BF), ("rows", F32), ("root", F32), ("sums", F32)),
        lens=my_len,
    )
    act, slope, second = feed_forward(first, feed, fb, full_inner_bias, full_outer_bias)
    arrived_cotangent, second = tied((arrived_cotangent, second))
    result, grad_res2, grad_second, second_sums = norm_call(
        second_norm_kernel,
        "second_norm",
        length,
        width,
        (
            (second, "rows"),
            (first, "rows"),
            (arrived_cotangent, "rows"),
            (full_second_gain, "line"),
            (full_second_shift, "line"),
        ),
        (("rows", BF), ("rows", F32), ("rows", BF), ("sums", F32)),
        lens=my_len,
    )
    grad_second, second_sums, first_sums, result = tied((grad_second, second_sums, first_sums, result))
    out_back = collect(result)
    outer_blocks = outer_gradient(act, grad_second, feed, fb)
    outer_blocks, grad_second = tied((outer_blocks, grad_second))
    if slabs:
        mine, away, grad_first, inner_bias_grad = feed_backward(
            me_ref, grad_second, first, feed, fb, slope, grad_res2, r
        )
    else:
        even, odd, grad_first, inner_bias_grad = feed_backward(
            jnp.zeros_like(me_ref), grad_second, first, feed, fb, slope, grad_res2, width // 2
        )
        blocks = jnp.stack((even[0], odd[0])).reshape(2, fb, width // 2, width)
        blocks = jnp.moveaxis(blocks, 1, 2).reshape(n, r, fb, width)
        mine, away = split_core(jnp.moveaxis(blocks, 2, 1).reshape(n, fb * r, width))
    inner_steps = reduce_steps(mine, away, fb * r // 2)
    out_back, outer_blocks, grad_first, inner_bias_grad, mine, away = tied(
        (out_back, outer_blocks, grad_first, inner_bias_grad, mine, away)
    )
    second_sums, first_sums, permutation, lengths, grad_first = tied(
        (second_sums, first_sums, permutation, lengths, grad_first)
    )
    outer_owned = lax.psum_scatter(
        outer_blocks.reshape(n, r * fb, width), "dp", scatter_dimension=0, tiled=True
    )
    moving = next(inner_steps)
    inverse = jnp.zeros(seq_count, jnp.int32).at[permutation].set(jnp.arange(seq_count, dtype=jnp.int32))
    layer_out = jnp.take(out_back, inverse, axis=0, mode="clip")

    grad_res1, grad_mixed, output_weight_grad, back_sums = norm_call(
        first_back_kernel,
        "first_back",
        length,
        width,
        (
            (grad_first, "rows"),
            (first_norm, "rows"),
            (first_root, "root"),
            (full_first_gain, "line"),
            (mixed, "rows"),
            wo,
        ),
        (("rows", F32), ("rows", BF), ("whole", BF), ("sums", F32)),
        scratch=(pltpu.VMEM((width, width), F32),),
    )
    sums = (first_sums, second_sums, back_sums, inner_bias_grad)
    moving, grad_mixed, output_weight_grad = tied((moving, grad_mixed, output_weight_grad))
    moving = inner_steps.send(moving)
    grads = attention_backward(my_len, qkv, mixed, grad_mixed, lse)
    moving, grads = tied((moving, grads))
    moving = inner_steps.send(moving)
    if slabs:
        input_grad, mine, away = project_back(me_ref, rows, grads, weights, grad_res1, output_weight_grad, sums, r)
        moving, input_grad, mine, away = tied((moving, input_grad, mine, away))
    else:
        input_grad = grad_res1 + sum(right_product(grads[i], weights[i]) for i in range(3))
        input_grad = input_grad.astype(BF)
        blocks = [left_product(rows, grads[i]).astype(BF) for i in range(3)] + [output_weight_grad]
        lines = [column_sum(grads[i])[None] for i in range(3)] + sum_rows(*sums)
        lines = jnp.concatenate(lines, 0).astype(BF)
        assert lines.shape[0] == SPARE
        blocks = [g.reshape(n, r, width) for g in blocks] + [jnp.broadcast_to(lines[None], (n, SPARE, width))]
        mine, away = split_core(jnp.concatenate(blocks, 1))
    input_back = collect(input_grad)
    ahead = inner_steps.send(moving)
    steps = reduce_steps(mine, away, 2 * r)
    moving = steps.send(next(steps))
    moving, outer_owned, ahead = tied((moving, outer_owned, ahead))
    moving = steps.send(moving)
    try:
        ahead = inner_steps.send(ahead)
        moving, ahead = tied((moving, ahead))
        inner_owned = finish(inner_steps, ahead)
    except StopIteration as end:
        inner_owned = end.value
    outer_owned = outer_owned.astype(F32)[0]
    reduced = finish(steps, moving)
    attention_owned = reduced[: 4 * r]
    owned = reduced[4 * r :]
    vectors = lax.dynamic_slice(owned, (0, me * r), (9, r))
    inner_bias_owned = owned[9 : 9 + fb].reshape(ff)
    inner_bias_owned = lax.dynamic_slice(inner_bias_owned, (me * (ff // n),), (ff // n,))
    sums = jnp.sum(owned[9 + fb : 12 + fb], 1)

    input_gradient = jnp.take(input_back, inverse, axis=0, mode="clip")
    rms = jnp.sqrt(sums / (jnp.sum(lengths).astype(F32) * width))
    return (
        layer_out,
        input_gradient,
        attention_owned[:r],
        attention_owned[r : 2 * r],
        attention_owned[2 * r : 3 * r],
        attention_owned[3 * r :],
        vectors[0],
        vectors[2],
        vectors[3],
        vectors[4],
        vectors[5],
        jnp.moveaxis(inner_owned.reshape(fb, r, width), 0, 1).reshape(r, ff),
        inner_bias_owned,
        outer_owned,
        vectors[6],
        vectors[7],
        vectors[8],
        rms[0],
        rms[1],
        rms[2],
    )


def solution(mesh):
    seq, mat, vec = P(None, "dp", None), P("dp", None), P("dp")
    return jax.shard_map(
        local,
        mesh=mesh,
        in_specs=(seq, seq, P(), P(), mat, mat, mat, mat, vec, vec, vec, vec, vec, mat, vec, mat, vec, vec, vec),
        out_specs=(seq, seq, mat, mat, mat, mat, vec, vec, vec, vec, vec, mat, vec, mat, vec, vec, vec, P(), P(), P()),
        check_vma=False,
    )
```

```python
import functools
import math

import jax
import jax.numpy as jnp
from jax import lax
from jax.experimental import pallas as pl
from jax.experimental.pallas import tpu as pltpu
from jax.sharding import PartitionSpec as P

HEADS = 16
EPS = 1e-05
NEG = -1e30
LOG2E = math.log2(math.e)
BF = jnp.bfloat16
F32 = jnp.float32
BQ = 1024
BR = 256
SPARE = 16
COST = pl.CostEstimate(flops=1 << 20, bytes_accessed=1 << 20, transcendentals=0)
NT = (((1,), (1,)), ((), ()))
TN = (((0,), (0,)), ((), ()))


def matmul(left, right):
    return jnp.dot(left, right, preferred_element_type=F32)


def left_product(left, right):
    return lax.dot_general(left, right, TN, preferred_element_type=F32)


def right_product(left, right):
    return lax.dot_general(left, right, NT, preferred_element_type=F32)


def column_sum(values):
    return jnp.sum(values.astype(F32), 0)


def head_keys(k, lane, half, key_bias):
    own = (lane >= 64 * half) & (lane < 64 * half + 64)
    spare = lane == 64 * (1 - half)
    return jnp.where(own, k, jnp.where(spare, key_bias, jnp.zeros_like(k)))


def head_queries(q, lane, half):
    return jnp.where(lane == 64 * (1 - half), jnp.ones_like(q), q)


def forward_kernel(len_ref, q_ref, k_ref, v_ref, o_ref, lse_ref, kh, vt):
    qi = pl.program_id(1)
    size = k_ref.shape[1]
    length = len_ref[0]

    @pl.when(qi == 0)
    def _():
        lane = lax.broadcasted_iota(jnp.int32, (size, 128), 1)
        row = lax.broadcasted_iota(jnp.int32, (size, 128), 0)
        key_bias = jnp.where(row < length, 0.0, NEG).astype(BF)
        k = k_ref[0]
        for half in (0, 1):
            kh[half] = head_keys(k, lane, half, key_bias)
        vt[...] = v_ref[0].T

    @pl.when(qi * BQ < length)
    def _():
        q = q_ref[0]
        lane = lax.broadcasted_iota(jnp.int32, q.shape, 1)
        scale = 0.125 * LOG2E
        outs = []
        for half in (0, 1):
            st = lax.dot_general(kh[half], head_queries(q, lane, half), NT, preferred_element_type=F32)
            peak = jnp.max(st, 0, keepdims=True) * scale
            pt = jnp.exp2(st * scale - peak)
            total = jnp.sum(pt, 0, keepdims=True)
            ot = jnp.dot(vt[64 * half : 64 * half + 64, :], pt.astype(BF), preferred_element_type=F32)
            outs.append(ot / total)
            lse_ref[0, half : half + 1, :] = peak + jnp.log2(total)
        o_ref[...] = jnp.concatenate(outs, 0).T.astype(BF)

    @pl.when(qi * BQ >= length)
    def _():
        o_ref[...] = jnp.zeros_like(o_ref)
        lse_ref[...] = jnp.zeros_like(lse_ref)


def qkv_specs(size):
    return [
        pl.BlockSpec((1, BQ, 128), lambda h, i, n: (0, i, h)),
        pl.BlockSpec((1, size, 128), lambda h, i, n: (1, 0, h)),
        pl.BlockSpec((1, size, 128), lambda h, i, n: (2, 0, h)),
    ]


def attention_forward(lens, qkv):
    _, size, width = qkv.shape
    pairs = width // 128
    return pl.pallas_call(
        forward_kernel,
        out_shape=(
            jax.ShapeDtypeStruct((size, width), BF),
            jax.ShapeDtypeStruct((pairs, 8, size), F32),
        ),
        grid_spec=pltpu.PrefetchScalarGridSpec(
            num_scalar_prefetch=1,
            grid=(pairs, size // BQ),
            in_specs=qkv_specs(size),
            out_specs=[
                pl.BlockSpec((BQ, 128), lambda h, i, n: (i, h)),
                pl.BlockSpec((1, 8, BQ), lambda h, i, n: (h, 0, i)),
            ],
            scratch_shapes=[pltpu.VMEM((2, size, 128), BF), pltpu.VMEM((128, size), BF)],
        ),
        compiler_params=pltpu.CompilerParams(vmem_limit_bytes=60 << 20),
        cost_estimate=pl.CostEstimate(flops=32 << 30, bytes_accessed=16 << 20, transcendentals=0),
        name="attention_forward",
    )(lens, qkv, qkv, qkv)


def backward_kernel(len_ref, q_ref, k_ref, v_ref, o_ref, g_ref, lse_ref, out_ref, kh, vh, kt, dka, dva):
    qi = pl.program_id(1)
    size = k_ref.shape[1]
    length = len_ref[0]
    here = pl.ds(pl.multiple_of(qi * BQ, BQ), BQ)

    @pl.when(qi == 0)
    def _():
        lane = lax.broadcasted_iota(jnp.int32, (size, 128), 1)
        row = lax.broadcasted_iota(jnp.int32, (size, 128), 0)
        key_bias = jnp.where(row < length, 0.0, NEG).astype(BF)
        k = k_ref[0]
        v = v_ref[0]
        for half in (0, 1):
            kh[half] = head_keys(k, lane, half, key_bias)
            vh[half] = head_keys(v, lane, half, jnp.zeros_like(v))
        kt[...] = k.T
        dka[...] = jnp.zeros_like(dka)
        dva[...] = jnp.zeros_like(dva)

    @pl.when(qi * BQ < length)
    def _():
        q = q_ref[0]
        g = g_ref[...]
        lane = lax.broadcasted_iota(jnp.int32, q.shape, 1)
        scale = 0.125 * LOG2E
        dots = (g.astype(F32) * o_ref[...].astype(F32)).T
        outs = []
        for half in (0, 1):
            qh = head_queries(q, lane, half)
            st = lax.dot_general(kh[half], qh, NT, preferred_element_type=F32)
            pt = jnp.exp2(st * scale - lse_ref[0, half : half + 1, :])
            dpt = lax.dot_general(vh[half], g, NT, preferred_element_type=F32)
            delta = jnp.sum(dots[64 * half : 64 * half + 64, :], 0, keepdims=True)
            dst = (pt * (dpt - delta)).astype(BF)
            dva[half] += jnp.dot(pt.astype(BF), g, preferred_element_type=F32)
            dka[half] += jnp.dot(dst, qh, preferred_element_type=F32)
            outs.append(jnp.dot(kt[64 * half : 64 * half + 64, :], dst, preferred_element_type=F32))
        out_ref[0, here, :] = (jnp.concatenate(outs, 0) * 0.125).T.astype(BF)

    @pl.when(qi * BQ >= length)
    def _():
        out_ref[0, here, :] = jnp.zeros((BQ, 128), BF)

    @pl.when(qi == pl.num_programs(1) - 1)
    def _():
        lane = lax.broadcasted_iota(jnp.int32, (size, 128), 1)
        out_ref[1] = (jnp.where(lane < 64, dka[0], dka[1]) * 0.125).astype(BF)
        out_ref[2] = jnp.where(lane < 64, dva[0], dva[1]).astype(BF)


def attention_backward(lens, qkv, o, g, lse):
    _, size, width = qkv.shape
    pairs = width // 128
    rows = pl.BlockSpec((BQ, 128), lambda h, i, n: (i, h))
    return pl.pallas_call(
        backward_kernel,
        out_shape=jax.ShapeDtypeStruct((3, size, width), BF),
        grid_spec=pltpu.PrefetchScalarGridSpec(
            num_scalar_prefetch=1,
            grid=(pairs, size // BQ),
            in_specs=qkv_specs(size) + [rows, rows, pl.BlockSpec((1, 8, BQ), lambda h, i, n: (h, 0, i))],
            out_specs=pl.BlockSpec((3, size, 128), lambda h, i, n: (0, 0, h)),
            scratch_shapes=[
                pltpu.VMEM((2, size, 128), BF),
                pltpu.VMEM((2, size, 128), BF),
                pltpu.VMEM((128, size), BF),
                pltpu.VMEM((2, size, 128), F32),
                pltpu.VMEM((2, size, 128), F32),
            ],
        ),
        compiler_params=pltpu.CompilerParams(vmem_limit_bytes=60 << 20),
        cost_estimate=COST,
        name="attention_backward",
    )(lens, qkv, qkv, qkv, o, g, lse)


def gather_orders(n):
    top = list(range(n.bit_length() - 2, 2, -1))
    return top, (top + [2, 1], top + [1, 2])


def distance(index, order):
    return sum(((index >> k) & 1) << bit for k, bit in enumerate(order))


def project_kernel(me_ref, a0, a1, b0, b1, x_ref, bias_ref, qkv_ref, w_ref, scratch, *, r, orders):
    j = pl.program_id(0)

    @pl.when(j == 0)
    def _():
        me = me_ref[0]
        half = r // 2
        for core, (a, b) in enumerate(((a0, b0), (a1, b1))):
            for index in range(a.shape[0]):
                off = pl.multiple_of((me ^ (distance(index, orders[0]) | core)) * r, r)
                scratch[0, pl.ds(off, r), :] = a[index, :r, :]
                scratch[1, pl.ds(off, half), :] = a[index, r : r + half, :]
                off = pl.multiple_of((me ^ (distance(index, orders[1]) | core)) * r, r)
                scratch[1, pl.ds(pl.multiple_of(off + half, half), half), :] = b[index, :half, :]
                scratch[2, pl.ds(off, r), :] = b[index, half : half + r, :]

    w = scratch[j]
    w_ref[0] = w
    qkv_ref[0] = (jnp.dot(x_ref[...], w, preferred_element_type=F32) + bias_ref[0]).astype(BF)


def project(me, pieces, x, bias, r):
    size, width = x.shape
    n = width // r
    whole = [pl.BlockSpec(p.shape, lambda j, m: (0, 0, 0)) for p in pieces]
    return pl.pallas_call(
        functools.partial(project_kernel, r=r, orders=gather_orders(n)[1]),
        out_shape=(jax.ShapeDtypeStruct((3, size, width), BF), jax.ShapeDtypeStruct((3, width, width), BF)),
        grid_spec=pltpu.PrefetchScalarGridSpec(
            num_scalar_prefetch=1,
            grid=(3,),
            in_specs=whole
            + [
                pl.BlockSpec((size, width), lambda j, m: (0, 0)),
                pl.BlockSpec((1, 1, width), lambda j, m: (j, 0, 0)),
            ],
            out_specs=[
                pl.BlockSpec((1, size, width), lambda j, m: (j, 0, 0)),
                pl.BlockSpec((1, width, width), lambda j, m: (j, 0, 0)),
            ],
            scratch_shapes=[pltpu.VMEM((3, width, width), BF)],
        ),
        compiler_params=pltpu.CompilerParams(vmem_limit_bytes=60 << 20),
        cost_estimate=pl.CostEstimate(flops=6 << 30, bytes_accessed=16 << 20, transcendentals=0),
        name="project",
    )(me, *pieces, x, bias)


def sum_rows(first_sums, second_sums, back_sums, inner_bias):
    width = first_sums.shape[1]
    rows = [back_sums[k : k + 1, :] for k in (2, 0, 1)] + [second_sums[k : k + 1, :] for k in (2, 0, 1)]
    rows += [inner_bias[0:1, k : k + width] for k in range(0, inner_bias.shape[1], width)]
    return rows + [first_sums[0:1, :], first_sums[1:2, :], second_sums[3:4, :]]


def project_back_kernel(
    me_ref, x_ref, g_ref, w_ref, base_ref, wo_ref, s1_ref, s2_ref, s3_ref, s4_ref, dx_ref, mine_ref, away_ref,
    xt, acc, lines, *, r
):
    j = pl.program_id(0)
    half, _, width = mine_ref.shape

    core = me_ref[0] & 1
    at = pl.ds(pl.multiple_of(j * r, r), r)

    @pl.when(j == 0)
    def _():
        xt[...] = x_ref[...].T
        acc[...] = base_ref[...]
        for k, row in enumerate(sum_rows(s1_ref, s2_ref, s3_ref, s4_ref), 3):
            lines[k : k + 1, :] = row

    @pl.when(j < 3)
    def _():
        g = g_ref[0]
        emit(core, jnp.dot(xt[...], g, preferred_element_type=F32).astype(BF), mine_ref, away_ref, at, r)
        acc[...] += lax.dot_general(g, w_ref[0], NT, preferred_element_type=F32)
        lines[pl.ds(j, 1), :] = jnp.sum(g.astype(F32), 0, keepdims=True)

    @pl.when(j == 3)
    def _():
        emit(core, wo_ref[...], mine_ref, away_ref, at, r)
        block = lines[...].astype(BF)
        for index in range(half):
            mine_ref[index, 4 * r :, :] = block
            away_ref[index, 4 * r :, :] = block
        dx_ref[...] = acc[...].astype(BF)


def project_back(me, x, grads, w, base, output_grad, sums, r):
    size, width = x.shape
    half = width // r // 2
    last = lambda j: jnp.minimum(j, 2)
    whole = pl.BlockSpec((size, width), lambda j, m: (0, 0))
    blocks = pl.BlockSpec((half, 4 * r + SPARE, width), lambda j, m: (0, 0, 0))
    return pl.pallas_call(
        functools.partial(project_back_kernel, r=r),
        out_shape=(
            jax.ShapeDtypeStruct((size, width), BF),
            jax.ShapeDtypeStruct((half, 4 * r + SPARE, width), BF),
            jax.ShapeDtypeStruct((half, 4 * r + SPARE, width), BF),
        ),
        grid_spec=pltpu.PrefetchScalarGridSpec(
            num_scalar_prefetch=1,
            grid=(4,),
            in_specs=[
                whole,
                pl.BlockSpec((1, size, width), lambda j, m: (last(j), 0, 0)),
                pl.BlockSpec((1, width, width), lambda j, m: (last(j), 0, 0)),
                whole,
                pl.BlockSpec((width, width), lambda j, m: (0, 0)),
            ]
            + [pl.BlockSpec(value.shape, lambda j, m: (0, 0)) for value in sums],
            out_specs=[whole, blocks, blocks],
            scratch_shapes=[
                pltpu.VMEM((width, size), BF),
                pltpu.VMEM((size, width), F32),
                pltpu.VMEM((SPARE, width), F32),
            ],
        ),
        compiler_params=pltpu.CompilerParams(vmem_limit_bytes=60 << 20),
        cost_estimate=COST,
        name="project_back",
    )(me, x, grads, w, base, output_grad, *sums)


def norm_rows(resid):
    center = resid - jnp.mean(resid, -1, keepdims=True)
    inverse_root = lax.rsqrt(jnp.mean(center * center, -1, keepdims=True) + EPS)
    return center * inverse_root, inverse_root


def norm_back(grad, norm, inverse_root):
    return (grad - jnp.mean(grad, -1, keepdims=True) - norm * jnp.mean(grad * norm, -1, keepdims=True)) * inverse_root


def valid_rows(len_ref):
    row = pl.program_id(0) * BR + lax.broadcasted_iota(jnp.int32, (BR, 1), 0)
    return (row < len_ref[0]).astype(F32)


def add_rows(sums_ref, values):
    @pl.when(pl.program_id(0) == 0)
    def _():
        sums_ref[...] = jnp.zeros_like(sums_ref)

    for k, value in enumerate(values):
        sums_ref[k : k + 1, :] += jnp.sum(value, 0, keepdims=True)


def first_norm_kernel(
    len_ref, mixed_ref, wo_ref, bias_ref, x_ref, gain_ref, shift_ref, first_ref, norm_ref, root_ref, sums_ref
):
    width = x_ref.shape[1]
    wo = wo_ref[...].reshape(width, width)
    branch = jnp.dot(mixed_ref[...], wo, preferred_element_type=F32) + bias_ref[...]
    x = x_ref[...].astype(F32)
    norm, root = norm_rows(x + branch)
    first_ref[...] = (norm * gain_ref[...] + shift_ref[...]).astype(BF)
    norm_ref[...] = norm
    root_ref[...] = jnp.broadcast_to(root, root_ref.shape)
    valid = valid_rows(len_ref)
    add_rows(sums_ref, (valid * x * x, valid * branch * branch))


def second_norm_kernel(
    len_ref, second_ref, first_ref, cotangent_ref, gain_ref, shift_ref, result_ref, wide_ref, grad_ref, sums_ref
):
    second = second_ref[...]
    norm, root = norm_rows(first_ref[...].astype(F32) + second)
    valid = valid_rows(len_ref)
    gain = gain_ref[...]
    result_ref[...] = ((norm * gain + shift_ref[...]) * valid).astype(BF)
    grad_out = cotangent_ref[...].astype(F32) * valid
    wide = norm_back(grad_out * gain, norm, root)
    grad = wide.astype(BF)
    wide_ref[...] = wide
    grad_ref[...] = grad
    add_rows(sums_ref, (grad_out * norm, grad_out, grad.astype(F32), valid * second * second))


def first_back_kernel(
    grad_ref, norm_ref, root_ref, gain_ref, mixed_ref, wo_ref, wide_ref, gmixed_ref, gweight_ref, sums_ref, total
):
    i = pl.program_id(0)
    width = norm_ref.shape[1]
    wo = wo_ref[...].reshape(width, width)
    grad_first = grad_ref[...]
    norm = norm_ref[...]
    wide = norm_back(grad_first * gain_ref[...], norm, root_ref[:, 0:1])
    grad = wide.astype(BF)
    wide_ref[...] = wide
    gmixed_ref[...] = lax.dot_general(grad, wo, NT, preferred_element_type=F32).astype(BF)
    part = lax.dot_general(mixed_ref[...], grad, TN, preferred_element_type=F32)

    @pl.when(i == 0)
    def _():
        total[...] = part

    @pl.when(i > 0)
    def _():
        total[...] += part

    @pl.when(i == pl.num_programs(0) - 1)
    def _():
        gweight_ref[...] = total[...].astype(BF)

    add_rows(sums_ref, (grad_first * norm, grad_first, grad.astype(F32)))


def norm_call(kernel, name, size, width, inputs, outputs, scratch=(), lens=None):
    prefetch = 0 if lens is None else 1

    def spec(kind):
        if kind == "rows":
            return pl.BlockSpec((BR, width), lambda i, *_: (i, 0))
        if kind == "root":
            return pl.BlockSpec((BR, 128), lambda i, *_: (i, 0))
        if kind == "line":
            return pl.BlockSpec((1, width), lambda i, *_: (0, 0))
        if kind == "sums":
            return pl.BlockSpec((8, width), lambda i, *_: (0, 0))
        if kind == "whole":
            return pl.BlockSpec((width, width), lambda i, *_: (0, 0))
        n, slot, r = kind
        return pl.BlockSpec((n, 1, r, width), lambda i, *_: (0, slot, 0, 0))

    shapes = {"rows": (size, width), "root": (size, 128), "sums": (8, width), "whole": (width, width)}
    call = pl.pallas_call(
        kernel,
        out_shape=tuple(jax.ShapeDtypeStruct(shapes[kind], dtype) for kind, dtype in outputs),
        grid_spec=pltpu.PrefetchScalarGridSpec(
            num_scalar_prefetch=prefetch,
            grid=(size // BR,),
            in_specs=[spec(kind) for _, kind in inputs],
            out_specs=[spec(kind) for kind, _ in outputs],
            scratch_shapes=list(scratch),
        ),
        compiler_params=pltpu.CompilerParams(vmem_limit_bytes=60 << 20),
        cost_estimate=COST,
        name=name,
    )
    arrays = [array for array, _ in inputs]
    return call(*arrays) if lens is None else call(lens, *arrays)


def feed_forward_kernel(first_ref, w1_ref, w2_ref, b1_ref, b2_ref, act_ref, slope_ref, second_ref):
    width = first_ref.shape[1]
    w1 = w1_ref[...].reshape(width, width)
    w2 = w2_ref[...].reshape(width, width)

    @pl.when(pl.program_id(0) == 0)
    def _():
        second_ref[...] = jnp.broadcast_to(b2_ref[...], second_ref.shape)

    for start in range(0, first_ref.shape[0], BR):
        at = slice(start, start + BR)
        inner = jnp.dot(first_ref[at, :], w1, preferred_element_type=F32) + b1_ref[...]
        cdf = 0.5 + 0.5 * lax.erf(inner * (0.5**0.5))
        act = (inner * cdf).astype(BF)
        slope = cdf + inner * (jnp.exp2(inner * inner * (-0.5 * LOG2E)) * ((0.5 / math.pi) ** 0.5))
        act_ref[at, :] = act
        slope_ref[at, :] = slope.astype(BF)
        second_ref[at, :] += jnp.dot(act, w2, preferred_element_type=F32)


def weight_specs(feed, fb, first_slot):
    n, slots, r, width = feed.shape
    if n == 1:
        inner = pl.BlockSpec((1, 1, r, width), lambda j: (0, first_slot + j, 0, 0))
        outer = pl.BlockSpec((1, 1, r, width), lambda j: (0, first_slot + fb + j, 0, 0))
    else:
        inner = pl.BlockSpec((n, 1, r, width), lambda j: (0, first_slot + j, 0, 0))
        outer = pl.BlockSpec((n // fb, fb, r, width), lambda j: (j, first_slot // fb + 1, 0, 0))
    return inner, outer


def feed_forward(first, feed, fb, b1, b2):
    size, width = first.shape
    inner_spec, outer_spec = weight_specs(feed, fb, 0)
    block = pl.BlockSpec((size, width), lambda j: (0, j))
    whole = pl.BlockSpec((size, width), lambda j: (0, 0))
    line = pl.BlockSpec((1, width), lambda j: (0, j))
    const = pl.BlockSpec((1, width), lambda j: (0, 0))
    return pl.pallas_call(
        feed_forward_kernel,
        out_shape=(
            jax.ShapeDtypeStruct((size, fb * width), BF),
            jax.ShapeDtypeStruct((size, fb * width), BF),
            jax.ShapeDtypeStruct((size, width), F32),
        ),
        grid=(fb,),
        in_specs=[whole, inner_spec, outer_spec, line, const],
        out_specs=[block, block, whole],
        compiler_params=pltpu.CompilerParams(vmem_limit_bytes=60 << 20),
        cost_estimate=pl.CostEstimate(flops=20 << 30, bytes_accessed=16 << 20, transcendentals=0),
        name="feed_forward",
    )(first, feed, feed, b1, b2)


def outer_gradient_kernel(act_ref, gs_ref, grad_ref):
    grad = lax.dot_general(act_ref[...], gs_ref[...], TN, preferred_element_type=F32)
    grad_ref[...] = grad.astype(BF).reshape(grad_ref.shape)


def outer_gradient(act, gs, feed, fb):
    size, width = gs.shape
    n, _, r, _ = feed.shape
    if n == 1:
        spec = pl.BlockSpec((1, 1, r, width), lambda j: (0, j, 0, 0))
    else:
        spec = pl.BlockSpec((n // fb, fb, r, width), lambda j: (j, 0, 0, 0))
    return pl.pallas_call(
        outer_gradient_kernel,
        out_shape=jax.ShapeDtypeStruct((n, fb, r, width), BF),
        grid=(fb,),
        in_specs=[
            pl.BlockSpec((size, width), lambda j: (0, j)),
            pl.BlockSpec((size, width), lambda j: (0, 0)),
        ],
        out_specs=spec,
        compiler_params=pltpu.CompilerParams(vmem_limit_bytes=60 << 20),
        cost_estimate=COST,
        name="outer_gradient",
    )(act, gs)


def emit(core, grad, mine_ref, away_ref, at, r):
    for index in range(mine_ref.shape[0]):
        even = grad[2 * index * r : (2 * index + 1) * r, :]
        odd = grad[(2 * index + 1) * r : (2 * index + 2) * r, :]
        mine_ref[index, at, :] = jnp.where(core == 0, even, odd)
        away_ref[index, at, :] = jnp.where(core == 0, odd, even)


def feed_backward_kernel(
    me_ref, gs_ref, first_ref, w1_ref, w2_ref, slope_ref, base_ref, mine_ref, away_ref, gfirst_ref, gbias_ref, turned
):
    j = pl.program_id(0)
    size, width = gs_ref.shape
    w1 = w1_ref[...].reshape(width, width)
    w2 = w2_ref[...].reshape(width, width)

    @pl.when(j == 0)
    def _():
        gfirst_ref[...] = base_ref[...]
        turned[...] = first_ref[...].T

    total = jnp.zeros((1, width), F32)
    pieces = []
    for start in range(0, size, BR):
        at = slice(start, start + BR)
        wide = lax.dot_general(gs_ref[at, :], w2, NT, preferred_element_type=F32) * slope_ref[at, :].astype(F32)
        piece = wide.astype(BF)
        total += jnp.sum(piece.astype(F32), 0, keepdims=True)
        gfirst_ref[at, :] += lax.dot_general(piece, w1, NT, preferred_element_type=F32)
        pieces.append(piece)
    gbias_ref[...] = total
    grad = jnp.dot(turned[...], jnp.concatenate(pieces, 0), preferred_element_type=F32).astype(BF)
    emit(me_ref[0] & 1, grad, mine_ref, away_ref, slice(None), mine_ref.shape[1])


def feed_backward(me, gs, first, feed, fb, slope, base, r):
    size, width = first.shape
    half = width // r // 2
    inner_spec, outer_spec = weight_specs(feed, fb, 0)
    wrap = lambda spec: pl.BlockSpec(spec.block_shape, lambda j, m, f=spec.index_map: f(j))
    block = pl.BlockSpec((size, width), lambda j, m: (0, j))
    whole = pl.BlockSpec((size, width), lambda j, m: (0, 0))
    sides = pl.BlockSpec((half, r, width), lambda j, m: (0, j, 0))
    side = jax.ShapeDtypeStruct((half, fb * r, width), BF)
    return pl.pallas_call(
        feed_backward_kernel,
        out_shape=(
            side,
            side,
            jax.ShapeDtypeStruct((size, width), F32),
            jax.ShapeDtypeStruct((1, fb * width), F32),
        ),
        grid_spec=pltpu.PrefetchScalarGridSpec(
            num_scalar_prefetch=1,
            grid=(fb,),
            in_specs=[whole, whole, wrap(inner_spec), wrap(outer_spec), block, whole],
            out_specs=[sides, sides, whole, pl.BlockSpec((1, width), lambda j, m: (0, j))],
            scratch_shapes=[pltpu.VMEM((width, size), BF)],
        ),
        compiler_params=pltpu.CompilerParams(vmem_limit_bytes=60 << 20),
        cost_estimate=COST,
        name="feed_backward",
    )(me, gs, first, feed, feed, slope, base)


def send(value, bit):
    n = lax.axis_size("dp")
    return lax.ppermute(value, "dp", [(i, i ^ (1 << bit)) for i in range(n)])


def double(value, bit):
    return jnp.concatenate((value, send(value, bit)), 0)


def split_core(blocks):
    pairs = blocks.reshape((blocks.shape[0] // 2, 2) + blocks.shape[1:])
    core = lax.axis_index("dp") & 1
    take = lambda index: lax.dynamic_index_in_dim(pairs, index, 1, keepdims=False)
    return take(core), take(1 - core)


def reduce_steps(mine, away, cut):
    bits = mine.shape[0].bit_length()
    me = lax.axis_index("dp")

    def split(value, left, bit):
        axis = left.index(bit)
        here = (me >> bit) & 1
        other = lax.dynamic_index_in_dim(value, 1 - here, axis, keepdims=False)
        kept = lax.dynamic_index_in_dim(value, here, axis, keepdims=False)
        return kept, other, [b for b in left if b != bit]

    (got,) = yield [send(away, 0)]
    value = (mine.astype(F32) + got.astype(F32)).astype(BF).reshape((2,) * (bits - 1) + mine.shape[1:])
    axis = value.ndim - 2
    pieces = [lax.slice_in_dim(value, low, high, axis=axis) for low, high in ((0, cut), (cut, mine.shape[1]))]
    lefts = [list(range(bits - 1, 0, -1))] * 2
    for turn in ((1, 2), (2, 1)):
        parted = [split(piece, left, bit) for piece, left, bit in zip(pieces, lefts, turn)]
        gots = yield [send(other, bit) for (_, other, _), bit in zip(parted, turn)]
        pieces = [(kept.astype(F32) + got.astype(F32)).astype(BF) for (kept, _, _), got in zip(parted, gots)]
        lefts = [left for _, _, left in parted]
    value, left = jnp.concatenate(pieces, axis - 2), lefts[0]
    for bit in range(3, bits):
        kept, other, left = split(value.astype(BF), left, bit)
        (got,) = yield [send(other, bit)]
        value = kept.astype(F32) + got.astype(F32)
    return value


def finish(steps, received):
    while True:
        try:
            received = steps.send(received)
        except StopIteration as end:
            return end.value


def local(
    hidden,
    cotangent,
    lengths,
    permutation,
    query_weight,
    key_weight,
    value_weight,
    output_weight,
    query_bias,
    value_bias,
    output_bias,
    first_gain,
    first_shift,
    inner_weight,
    inner_bias,
    outer_weight,
    outer_bias,
    second_gain,
    second_shift,
):
    n = lax.axis_size("dp")
    me = lax.axis_index("dp")
    seq_count, part_len, width = hidden.shape
    assert seq_count == n
    length = part_len * n
    r = query_weight.shape[0]
    ff = inner_weight.shape[1]
    fb = ff // width

    def exchange(dealt):
        return lax.all_to_all(dealt, "dp", split_axis=0, concat_axis=0, tiled=True).reshape(length, width)

    dealt_hidden = jnp.take(hidden, permutation, axis=0, mode="clip")
    dealt_cotangent = jnp.take(cotangent, permutation, axis=0, mode="clip")

    def collect(values):
        return lax.all_to_all(values.reshape(n, part_len, width), "dp", split_axis=0, concat_axis=0, tiled=True)

    slabs = r % 32 == 0 and n >= 8
    me_ref = me.astype(jnp.int32).reshape(1)
    tied = lax.optimization_barrier
    small = jnp.concatenate(
        (query_bias, value_bias, output_bias, first_gain, first_shift, outer_bias, second_gain, second_shift, inner_bias)
    )
    feed_pack = jnp.concatenate(
        [inner_weight[:, i * width : (i + 1) * width] for i in range(fb)] + [outer_weight, output_weight], 0
    ).reshape(2 * fb + 1, r, width)
    if slabs:
        top, orders = gather_orders(n)
        line = jnp.pad(small[None], ((0, 15), (0, width - small.shape[0])))
        pack = jnp.concatenate((query_weight, key_weight, value_weight, line), 0)[None]
        pack, dealt_hidden = lax.optimization_barrier((pack, dealt_hidden))
        rows = exchange(dealt_hidden)
        for step, bit in enumerate(top):
            pack = double(pack, bit)
            if step == 0:
                pack, feed_pack = tied((pack, feed_pack))
            else:
                pack, dealt_cotangent = tied((pack, dealt_cotangent))
        cut = 3 * r // 2
        pieces = [pack[:, :cut], pack[:, cut:]]
        for step in (-2, -1):
            pieces = [double(piece, order[step]) for piece, order in zip(pieces, orders)]
        got = [send(piece, 0) for piece in pieces]
        lines = jnp.concatenate((pieces[1][:, cut], got[1][:, cut]), 0)[:, : small.shape[0]]
        apart = me ^ jnp.arange(n, dtype=jnp.int32)
        index = sum(((apart >> bit) & 1) << k for k, bit in enumerate(orders[1])) + (apart & 1) * (n // 2)
        small = jnp.take(lines, index, axis=0, mode="clip")
    else:
        rows = exchange(dealt_hidden)
        small = lax.all_to_all(
            jnp.broadcast_to(small[None], (n, small.shape[0])), "dp", split_axis=0, concat_axis=0, tiled=True
        )
    feed = lax.all_gather(feed_pack, "dp", axis=0, tiled=False)
    full_output = None if slabs else feed[:, 2 * fb].reshape(width, width)
    vectors = [small[:, i * r : (i + 1) * r].reshape(1, width).astype(F32) for i in range(8)]
    full_query_bias, full_value_bias, full_output_bias, full_first_gain, full_first_shift = vectors[:5]
    full_outer_bias, full_second_gain, full_second_shift = vectors[5:]
    full_inner_bias = small[:, 8 * r :].reshape(1, ff).astype(F32)
    bias = jnp.stack((full_query_bias, jnp.zeros_like(full_query_bias), full_value_bias))
    if slabs:
        qkv, weights = project(me_ref, (pieces[0], got[0], pieces[1], got[1]), rows, bias, r)
    else:
        feed = jnp.concatenate(
            (
                jnp.moveaxis(feed[:, :fb], 1, 0).reshape(1, fb, width, width),
                feed[:, fb : 2 * fb].reshape(1, fb, width, width),
            ),
            1,
        )
        gathered = lax.all_gather(jnp.stack((query_weight, key_weight, value_weight)), "dp", axis=0, tiled=False)
        weights = jnp.moveaxis(gathered, 1, 0).reshape(3, width, width)
        qkv = jnp.stack([(matmul(rows, weights[i]) + bias[i]).astype(BF) for i in range(3)])
    dealt_cotangent, qkv = lax.optimization_barrier((dealt_cotangent, qkv))
    arrived_cotangent = exchange(dealt_cotangent)

    my_len = lax.dynamic_slice_in_dim(lengths, me, 1)
    mixed, lse = attention_forward(my_len, qkv)
    wo = (feed, (n, 2 * fb, r)) if slabs else (full_output[None, None], (1, 0, width))
    first, first_norm, first_root, first_sums = norm_call(
        first_norm_kernel,
        "first_norm",
        length,
        width,
        (
            (mixed, "rows"),
            wo,
            (full_output_bias, "line"),
            (rows, "rows"),
            (full_first_gain, "line"),
            (full_first_shift, "line"),
        ),
        (("rows", BF), ("rows", F32), ("root", F32), ("sums", F32)),
        lens=my_len,
    )
    act, slope, second = feed_forward(first, feed, fb, full_inner_bias, full_outer_bias)
    arrived_cotangent, second = tied((arrived_cotangent, second))
    result, grad_res2, grad_second, second_sums = norm_call(
        second_norm_kernel,
        "second_norm",
        length,
        width,
        (
            (second, "rows"),
            (first, "rows"),
            (arrived_cotangent, "rows"),
            (full_second_gain, "line"),
            (full_second_shift, "line"),
        ),
        (("rows", BF), ("rows", F32), ("rows", BF), ("sums", F32)),
        lens=my_len,
    )
    grad_second, second_sums, first_sums, result = tied((grad_second, second_sums, first_sums, result))
    outer_blocks = outer_gradient(act, grad_second, feed, fb)
    outer_blocks, grad_second = tied((outer_blocks, grad_second))
    outer_owned = lax.psum_scatter(
        outer_blocks.reshape(n, r * fb, width), "dp", scatter_dimension=0, tiled=True
    )
    if slabs:
        mine, away, grad_first, inner_bias_grad = feed_backward(
            me_ref, grad_second, first, feed, fb, slope, grad_res2, r
        )
    else:
        even, odd, grad_first, inner_bias_grad = feed_backward(
            jnp.zeros_like(me_ref), grad_second, first, feed, fb, slope, grad_res2, width // 2
        )
        blocks = jnp.stack((even[0], odd[0])).reshape(2, fb, width // 2, width)
        blocks = jnp.moveaxis(blocks, 1, 2).reshape(n, r, fb, width)
        mine, away = split_core(jnp.moveaxis(blocks, 2, 1).reshape(n, fb * r, width))
    inner_steps = reduce_steps(mine, away, fb * r // 2)
    grad_first, inner_bias_grad, mine, away, result = tied((grad_first, inner_bias_grad, mine, away, result))
    out_back = collect(result)
    second_sums, first_sums, permutation, lengths, grad_first = tied(
        (second_sums, first_sums, permutation, lengths, grad_first)
    )
    moving = next(inner_steps)
    inverse = jnp.zeros(seq_count, jnp.int32).at[permutation].set(jnp.arange(seq_count, dtype=jnp.int32))

    grad_res1, grad_mixed, output_weight_grad, back_sums = norm_call(
        first_back_kernel,
        "first_back",
        length,
        width,
        (
            (grad_first, "rows"),
            (first_norm, "rows"),
            (first_root, "root"),
            (full_first_gain, "line"),
            (mixed, "rows"),
            wo,
        ),
        (("rows", F32), ("rows", BF), ("whole", BF), ("sums", F32)),
        scratch=(pltpu.VMEM((width, width), F32),),
    )
    sums = (first_sums, second_sums, back_sums, inner_bias_grad)
    moving, grad_mixed, output_weight_grad = tied((moving, grad_mixed, output_weight_grad))
    moving = inner_steps.send(moving)
    grads = attention_backward(my_len, qkv, mixed, grad_mixed, lse)
    moving, grads, out_back = tied((moving, grads, out_back))
    layer_out = jnp.take(out_back, inverse, axis=0, mode="clip")
    moving = inner_steps.send(moving)
    if slabs:
        input_grad, mine, away = project_back(me_ref, rows, grads, weights, grad_res1, output_weight_grad, sums, r)
        moving, input_grad, mine, away = tied((moving, input_grad, mine, away))
    else:
        input_grad = grad_res1 + sum(right_product(grads[i], weights[i]) for i in range(3))
        input_grad = input_grad.astype(BF)
        blocks = [left_product(rows, grads[i]).astype(BF) for i in range(3)] + [output_weight_grad]
        lines = [column_sum(grads[i])[None] for i in range(3)] + sum_rows(*sums)
        lines = jnp.concatenate(lines, 0).astype(BF)
        assert lines.shape[0] == SPARE
        blocks = [g.reshape(n, r, width) for g in blocks] + [jnp.broadcast_to(lines[None], (n, SPARE, width))]
        mine, away = split_core(jnp.concatenate(blocks, 1))
    input_back = collect(input_grad)
    ahead = inner_steps.send(moving)
    steps = reduce_steps(mine, away, 2 * r)
    moving = steps.send(next(steps))
    moving, outer_owned, ahead = tied((moving, outer_owned, ahead))
    moving = steps.send(moving)
    try:
        ahead = inner_steps.send(ahead)
        moving, ahead = tied((moving, ahead))
        inner_owned = finish(inner_steps, ahead)
    except StopIteration as end:
        inner_owned = end.value
    outer_owned = outer_owned.astype(F32)[0]
    reduced = finish(steps, moving)
    attention_owned = reduced[: 4 * r]
    owned = reduced[4 * r :]
    vectors = lax.dynamic_slice(owned, (0, me * r), (9, r))
    inner_bias_owned = owned[9 : 9 + fb].reshape(ff)
    inner_bias_owned = lax.dynamic_slice(inner_bias_owned, (me * (ff // n),), (ff // n,))
    sums = jnp.sum(owned[9 + fb : 12 + fb], 1)

    input_gradient = jnp.take(input_back, inverse, axis=0, mode="clip")
    rms = jnp.sqrt(sums / (jnp.sum(lengths).astype(F32) * width))
    return (
        layer_out,
        input_gradient,
        attention_owned[:r],
        attention_owned[r : 2 * r],
        attention_owned[2 * r : 3 * r],
        attention_owned[3 * r :],
        vectors[0],
        vectors[2],
        vectors[3],
        vectors[4],
        vectors[5],
        jnp.moveaxis(inner_owned.reshape(fb, r, width), 0, 1).reshape(r, ff),
        inner_bias_owned,
        outer_owned,
        vectors[6],
        vectors[7],
        vectors[8],
        rms[0],
        rms[1],
        rms[2],
    )


def solution(mesh):
    seq, mat, vec = P(None, "dp", None), P("dp", None), P("dp")
    return jax.shard_map(
        local,
        mesh=mesh,
        in_specs=(seq, seq, P(), P(), mat, mat, mat, mat, vec, vec, vec, vec, vec, mat, vec, mat, vec, vec, vec),
        out_specs=(seq, seq, mat, mat, mat, mat, vec, vec, vec, vec, vec, mat, vec, mat, vec, vec, vec, P(), P(), P()),
        check_vma=False,
    )
```

```python
import functools
import math

import jax
import jax.numpy as jnp
from jax import lax
from jax.experimental import pallas as pl
from jax.experimental.pallas import tpu as pltpu
from jax.sharding import PartitionSpec as P

HEADS = 16
EPS = 1e-05
NEG = -1e30
LOG2E = math.log2(math.e)
BF = jnp.bfloat16
F32 = jnp.float32
BQ = 1024
BR = 256
SPARE = 16
COST = pl.CostEstimate(flops=1 << 20, bytes_accessed=1 << 20, transcendentals=0)
NT = (((1,), (1,)), ((), ()))
TN = (((0,), (0,)), ((), ()))


def matmul(left, right):
    return jnp.dot(left, right, preferred_element_type=F32)


def left_product(left, right):
    return lax.dot_general(left, right, TN, preferred_element_type=F32)


def right_product(left, right):
    return lax.dot_general(left, right, NT, preferred_element_type=F32)


def column_sum(values):
    return jnp.sum(values.astype(F32), 0)


def head_keys(k, lane, half, key_bias):
    own = (lane >= 64 * half) & (lane < 64 * half + 64)
    spare = lane == 64 * (1 - half)
    return jnp.where(own, k, jnp.where(spare, key_bias, jnp.zeros_like(k)))


def head_queries(q, lane, half):
    return jnp.where(lane == 64 * (1 - half), jnp.ones_like(q), q)


def forward_kernel(len_ref, q_ref, k_ref, v_ref, o_ref, lse_ref, kh, vt):
    qi = pl.program_id(1)
    size = k_ref.shape[1]
    length = len_ref[0]

    @pl.when(qi == 0)
    def _():
        lane = lax.broadcasted_iota(jnp.int32, (size, 128), 1)
        row = lax.broadcasted_iota(jnp.int32, (size, 128), 0)
        key_bias = jnp.where(row < length, 0.0, NEG).astype(BF)
        k = k_ref[0]
        for half in (0, 1):
            kh[half] = head_keys(k, lane, half, key_bias)
        vt[...] = v_ref[0].T

    @pl.when(qi * BQ < length)
    def _():
        q = q_ref[0]
        lane = lax.broadcasted_iota(jnp.int32, q.shape, 1)
        scale = 0.125 * LOG2E
        outs = []
        for half in (0, 1):
            st = lax.dot_general(kh[half], head_queries(q, lane, half), NT, preferred_element_type=F32)
            peak = jnp.max(st, 0, keepdims=True) * scale
            pt = jnp.exp2(st * scale - peak)
            total = jnp.sum(pt, 0, keepdims=True)
            ot = jnp.dot(vt[64 * half : 64 * half + 64, :], pt.astype(BF), preferred_element_type=F32)
            outs.append(ot / total)
            lse_ref[0, half : half + 1, :] = peak + jnp.log2(total)
        o_ref[...] = jnp.concatenate(outs, 0).T.astype(BF)

    @pl.when(qi * BQ >= length)
    def _():
        o_ref[...] = jnp.zeros_like(o_ref)
        lse_ref[...] = jnp.zeros_like(lse_ref)


def qkv_specs(size):
    return [
        pl.BlockSpec((1, BQ, 128), lambda h, i, n: (0, i, h)),
        pl.BlockSpec((1, size, 128), lambda h, i, n: (1, 0, h)),
        pl.BlockSpec((1, size, 128), lambda h, i, n: (2, 0, h)),
    ]


def attention_forward(lens, qkv):
    _, size, width = qkv.shape
    pairs = width // 128
    return pl.pallas_call(
        forward_kernel,
        out_shape=(
            jax.ShapeDtypeStruct((size, width), BF),
            jax.ShapeDtypeStruct((pairs, 8, size), F32),
        ),
        grid_spec=pltpu.PrefetchScalarGridSpec(
            num_scalar_prefetch=1,
            grid=(pairs, size // BQ),
            in_specs=qkv_specs(size),
            out_specs=[
                pl.BlockSpec((BQ, 128), lambda h, i, n: (i, h)),
                pl.BlockSpec((1, 8, BQ), lambda h, i, n: (h, 0, i)),
            ],
            scratch_shapes=[pltpu.VMEM((2, size, 128), BF), pltpu.VMEM((128, size), BF)],
        ),
        compiler_params=pltpu.CompilerParams(vmem_limit_bytes=60 << 20),
        cost_estimate=pl.CostEstimate(flops=32 << 30, bytes_accessed=16 << 20, transcendentals=0),
        name="attention_forward",
    )(lens, qkv, qkv, qkv)


def backward_kernel(len_ref, q_ref, k_ref, v_ref, o_ref, g_ref, lse_ref, out_ref, kh, vh, kt, dka, dva):
    qi = pl.program_id(1)
    size = k_ref.shape[1]
    length = len_ref[0]
    here = pl.ds(pl.multiple_of(qi * BQ, BQ), BQ)

    @pl.when(qi == 0)
    def _():
        lane = lax.broadcasted_iota(jnp.int32, (size, 128), 1)
        row = lax.broadcasted_iota(jnp.int32, (size, 128), 0)
        key_bias = jnp.where(row < length, 0.0, NEG).astype(BF)
        k = k_ref[0]
        v = v_ref[0]
        for half in (0, 1):
            kh[half] = head_keys(k, lane, half, key_bias)
            vh[half] = head_keys(v, lane, half, jnp.zeros_like(v))
        kt[...] = k.T
        dka[...] = jnp.zeros_like(dka)
        dva[...] = jnp.zeros_like(dva)

    @pl.when(qi * BQ < length)
    def _():
        q = q_ref[0]
        g = g_ref[...]
        lane = lax.broadcasted_iota(jnp.int32, q.shape, 1)
        scale = 0.125 * LOG2E
        dots = (g.astype(F32) * o_ref[...].astype(F32)).T
        outs = []
        for half in (0, 1):
            qh = head_queries(q, lane, half)
            st = lax.dot_general(kh[half], qh, NT, preferred_element_type=F32)
            pt = jnp.exp2(st * scale - lse_ref[0, half : half + 1, :])
            dpt = lax.dot_general(vh[half], g, NT, preferred_element_type=F32)
            delta = jnp.sum(dots[64 * half : 64 * half + 64, :], 0, keepdims=True)
            dst = (pt * (dpt - delta)).astype(BF)
            dva[half] += jnp.dot(pt.astype(BF), g, preferred_element_type=F32)
            dka[half] += jnp.dot(dst, qh, preferred_element_type=F32)
            outs.append(jnp.dot(kt[64 * half : 64 * half + 64, :], dst, preferred_element_type=F32))
        out_ref[0, here, :] = (jnp.concatenate(outs, 0) * 0.125).T.astype(BF)

    @pl.when(qi * BQ >= length)
    def _():
        out_ref[0, here, :] = jnp.zeros((BQ, 128), BF)

    @pl.when(qi == pl.num_programs(1) - 1)
    def _():
        lane = lax.broadcasted_iota(jnp.int32, (size, 128), 1)
        out_ref[1] = (jnp.where(lane < 64, dka[0], dka[1]) * 0.125).astype(BF)
        out_ref[2] = jnp.where(lane < 64, dva[0], dva[1]).astype(BF)


def attention_backward(lens, qkv, o, g, lse):
    _, size, width = qkv.shape
    pairs = width // 128
    rows = pl.BlockSpec((BQ, 128), lambda h, i, n: (i, h))
    return pl.pallas_call(
        backward_kernel,
        out_shape=jax.ShapeDtypeStruct((3, size, width), BF),
        grid_spec=pltpu.PrefetchScalarGridSpec(
            num_scalar_prefetch=1,
            grid=(pairs, size // BQ),
            in_specs=qkv_specs(size) + [rows, rows, pl.BlockSpec((1, 8, BQ), lambda h, i, n: (h, 0, i))],
            out_specs=pl.BlockSpec((3, size, 128), lambda h, i, n: (0, 0, h)),
            scratch_shapes=[
                pltpu.VMEM((2, size, 128), BF),
                pltpu.VMEM((2, size, 128), BF),
                pltpu.VMEM((128, size), BF),
                pltpu.VMEM((2, size, 128), F32),
                pltpu.VMEM((2, size, 128), F32),
            ],
        ),
        compiler_params=pltpu.CompilerParams(vmem_limit_bytes=60 << 20),
        cost_estimate=COST,
        name="attention_backward",
    )(lens, qkv, qkv, qkv, o, g, lse)


def gather_orders(n):
    top = list(range(n.bit_length() - 2, 2, -1))
    return top, (top + [2, 1], top + [1, 2])


def distance(index, order):
    return sum(((index >> k) & 1) << bit for k, bit in enumerate(order))


def project_kernel(me_ref, a0, a1, b0, b1, x_ref, bias_ref, qkv_ref, w_ref, scratch, *, r, orders):
    j = pl.program_id(0)

    @pl.when(j == 0)
    def _():
        me = me_ref[0]
        half = r // 2
        for core, (a, b) in enumerate(((a0, b0), (a1, b1))):
            for index in range(a.shape[0]):
                off = pl.multiple_of((me ^ (distance(index, orders[0]) | core)) * r, r)
                scratch[0, pl.ds(off, r), :] = a[index, :r, :]
                scratch[1, pl.ds(off, half), :] = a[index, r : r + half, :]
                off = pl.multiple_of((me ^ (distance(index, orders[1]) | core)) * r, r)
                scratch[1, pl.ds(pl.multiple_of(off + half, half), half), :] = b[index, :half, :]
                scratch[2, pl.ds(off, r), :] = b[index, half : half + r, :]

    w = scratch[j]
    w_ref[0] = w
    qkv_ref[0] = (jnp.dot(x_ref[...], w, preferred_element_type=F32) + bias_ref[0]).astype(BF)


def project(me, pieces, x, bias, r):
    size, width = x.shape
    n = width // r
    whole = [pl.BlockSpec(p.shape, lambda j, m: (0, 0, 0)) for p in pieces]
    return pl.pallas_call(
        functools.partial(project_kernel, r=r, orders=gather_orders(n)[1]),
        out_shape=(jax.ShapeDtypeStruct((3, size, width), BF), jax.ShapeDtypeStruct((3, width, width), BF)),
        grid_spec=pltpu.PrefetchScalarGridSpec(
            num_scalar_prefetch=1,
            grid=(3,),
            in_specs=whole
            + [
                pl.BlockSpec((size, width), lambda j, m: (0, 0)),
                pl.BlockSpec((1, 1, width), lambda j, m: (j, 0, 0)),
            ],
            out_specs=[
                pl.BlockSpec((1, size, width), lambda j, m: (j, 0, 0)),
                pl.BlockSpec((1, width, width), lambda j, m: (j, 0, 0)),
            ],
            scratch_shapes=[pltpu.VMEM((3, width, width), BF)],
        ),
        compiler_params=pltpu.CompilerParams(vmem_limit_bytes=60 << 20),
        cost_estimate=pl.CostEstimate(flops=6 << 30, bytes_accessed=16 << 20, transcendentals=0),
        name="project",
    )(me, *pieces, x, bias)


def sum_rows(first_sums, second_sums, back_sums, inner_bias):
    width = first_sums.shape[1]
    rows = [back_sums[k : k + 1, :] for k in (2, 0, 1)] + [second_sums[k : k + 1, :] for k in (2, 0, 1)]
    rows += [inner_bias[0:1, k : k + width] for k in range(0, inner_bias.shape[1], width)]
    return rows + [first_sums[0:1, :], first_sums[1:2, :], second_sums[3:4, :]]


def project_back_kernel(
    me_ref, x_ref, g_ref, w_ref, base_ref, wo_ref, s1_ref, s2_ref, s3_ref, s4_ref, dx_ref, mine_ref, away_ref,
    xt, acc, lines, *, r
):
    j = pl.program_id(0)
    half, _, width = mine_ref.shape

    core = me_ref[0] & 1
    at = pl.ds(pl.multiple_of(j * r, r), r)

    @pl.when(j == 0)
    def _():
        xt[...] = x_ref[...].T
        acc[...] = base_ref[...]
        for k, row in enumerate(sum_rows(s1_ref, s2_ref, s3_ref, s4_ref), 3):
            lines[k : k + 1, :] = row

    @pl.when(j < 3)
    def _():
        g = g_ref[0]
        emit(core, jnp.dot(xt[...], g, preferred_element_type=F32).astype(BF), mine_ref, away_ref, at, r)
        acc[...] += lax.dot_general(g, w_ref[0], NT, preferred_element_type=F32)
        lines[pl.ds(j, 1), :] = jnp.sum(g.astype(F32), 0, keepdims=True)

    @pl.when(j == 3)
    def _():
        emit(core, wo_ref[...], mine_ref, away_ref, at, r)
        block = lines[...].astype(BF)
        for index in range(half):
            mine_ref[index, 4 * r :, :] = block
            away_ref[index, 4 * r :, :] = block
        dx_ref[...] = acc[...].astype(BF)


def project_back(me, x, grads, w, base, output_grad, sums, r):
    size, width = x.shape
    half = width // r // 2
    last = lambda j: jnp.minimum(j, 2)
    whole = pl.BlockSpec((size, width), lambda j, m: (0, 0))
    blocks = pl.BlockSpec((half, 4 * r + SPARE, width), lambda j, m: (0, 0, 0))
    return pl.pallas_call(
        functools.partial(project_back_kernel, r=r),
        out_shape=(
            jax.ShapeDtypeStruct((size, width), BF),
            jax.ShapeDtypeStruct((half, 4 * r + SPARE, width), BF),
            jax.ShapeDtypeStruct((half, 4 * r + SPARE, width), BF),
        ),
        grid_spec=pltpu.PrefetchScalarGridSpec(
            num_scalar_prefetch=1,
            grid=(4,),
            in_specs=[
                whole,
                pl.BlockSpec((1, size, width), lambda j, m: (last(j), 0, 0)),
                pl.BlockSpec((1, width, width), lambda j, m: (last(j), 0, 0)),
                whole,
                pl.BlockSpec((width, width), lambda j, m: (0, 0)),
            ]
            + [pl.BlockSpec(value.shape, lambda j, m: (0, 0)) for value in sums],
            out_specs=[whole, blocks, blocks],
            scratch_shapes=[
                pltpu.VMEM((width, size), BF),
                pltpu.VMEM((size, width), F32),
                pltpu.VMEM((SPARE, width), F32),
            ],
        ),
        compiler_params=pltpu.CompilerParams(vmem_limit_bytes=60 << 20),
        cost_estimate=COST,
        name="project_back",
    )(me, x, grads, w, base, output_grad, *sums)


def norm_rows(resid):
    center = resid - jnp.mean(resid, -1, keepdims=True)
    inverse_root = lax.rsqrt(jnp.mean(center * center, -1, keepdims=True) + EPS)
    return center * inverse_root, inverse_root


def norm_back(grad, norm, inverse_root):
    return (grad - jnp.mean(grad, -1, keepdims=True) - norm * jnp.mean(grad * norm, -1, keepdims=True)) * inverse_root


def valid_rows(len_ref):
    row = pl.program_id(0) * BR + lax.broadcasted_iota(jnp.int32, (BR, 1), 0)
    return (row < len_ref[0]).astype(F32)


def add_rows(sums_ref, values):
    @pl.when(pl.program_id(0) == 0)
    def _():
        sums_ref[...] = jnp.zeros_like(sums_ref)

    for k, value in enumerate(values):
        sums_ref[k : k + 1, :] += jnp.sum(value, 0, keepdims=True)


def first_norm_kernel(
    len_ref, mixed_ref, wo_ref, bias_ref, x_ref, gain_ref, shift_ref, first_ref, norm_ref, root_ref, sums_ref
):
    width = x_ref.shape[1]
    wo = wo_ref[...].reshape(width, width)
    branch = jnp.dot(mixed_ref[...], wo, preferred_element_type=F32) + bias_ref[...]
    x = x_ref[...].astype(F32)
    norm, root = norm_rows(x + branch)
    first_ref[...] = (norm * gain_ref[...] + shift_ref[...]).astype(BF)
    norm_ref[...] = norm
    root_ref[...] = jnp.broadcast_to(root, root_ref.shape)
    valid = valid_rows(len_ref)
    add_rows(sums_ref, (valid * x * x, valid * branch * branch))


def second_norm_kernel(
    len_ref, second_ref, first_ref, cotangent_ref, gain_ref, shift_ref, result_ref, wide_ref, grad_ref, sums_ref
):
    second = second_ref[...]
    norm, root = norm_rows(first_ref[...].astype(F32) + second)
    valid = valid_rows(len_ref)
    gain = gain_ref[...]
    result_ref[...] = ((norm * gain + shift_ref[...]) * valid).astype(BF)
    grad_out = cotangent_ref[...].astype(F32) * valid
    wide = norm_back(grad_out * gain, norm, root)
    grad = wide.astype(BF)
    wide_ref[...] = wide
    grad_ref[...] = grad
    add_rows(sums_ref, (grad_out * norm, grad_out, grad.astype(F32), valid * second * second))


def first_back_kernel(
    grad_ref, norm_ref, root_ref, gain_ref, mixed_ref, wo_ref, wide_ref, gmixed_ref, gweight_ref, sums_ref, total
):
    i = pl.program_id(0)
    width = norm_ref.shape[1]
    wo = wo_ref[...].reshape(width, width)
    grad_first = grad_ref[...]
    norm = norm_ref[...]
    wide = norm_back(grad_first * gain_ref[...], norm, root_ref[:, 0:1])
    grad = wide.astype(BF)
    wide_ref[...] = wide
    gmixed_ref[...] = lax.dot_general(grad, wo, NT, preferred_element_type=F32).astype(BF)
    part = lax.dot_general(mixed_ref[...], grad, TN, preferred_element_type=F32)

    @pl.when(i == 0)
    def _():
        total[...] = part

    @pl.when(i > 0)
    def _():
        total[...] += part

    @pl.when(i == pl.num_programs(0) - 1)
    def _():
        gweight_ref[...] = total[...].astype(BF)

    add_rows(sums_ref, (grad_first * norm, grad_first, grad.astype(F32)))


def norm_call(kernel, name, size, width, inputs, outputs, scratch=(), lens=None):
    prefetch = 0 if lens is None else 1

    def spec(kind):
        if kind == "rows":
            return pl.BlockSpec((BR, width), lambda i, *_: (i, 0))
        if kind == "root":
            return pl.BlockSpec((BR, 128), lambda i, *_: (i, 0))
        if kind == "line":
            return pl.BlockSpec((1, width), lambda i, *_: (0, 0))
        if kind == "sums":
            return pl.BlockSpec((8, width), lambda i, *_: (0, 0))
        if kind == "whole":
            return pl.BlockSpec((width, width), lambda i, *_: (0, 0))
        n, slot, r = kind
        return pl.BlockSpec((n, 1, r, width), lambda i, *_: (0, slot, 0, 0))

    shapes = {"rows": (size, width), "root": (size, 128), "sums": (8, width), "whole": (width, width)}
    call = pl.pallas_call(
        kernel,
        out_shape=tuple(jax.ShapeDtypeStruct(shapes[kind], dtype) for kind, dtype in outputs),
        grid_spec=pltpu.PrefetchScalarGridSpec(
            num_scalar_prefetch=prefetch,
            grid=(size // BR,),
            in_specs=[spec(kind) for _, kind in inputs],
            out_specs=[spec(kind) for kind, _ in outputs],
            scratch_shapes=list(scratch),
        ),
        compiler_params=pltpu.CompilerParams(vmem_limit_bytes=60 << 20),
        cost_estimate=COST,
        name=name,
    )
    arrays = [array for array, _ in inputs]
    return call(*arrays) if lens is None else call(lens, *arrays)


def feed_forward_kernel(first_ref, w1_ref, w2_ref, b1_ref, b2_ref, act_ref, slope_ref, second_ref):
    width = first_ref.shape[1]
    w1 = w1_ref[...].reshape(width, width)
    w2 = w2_ref[...].reshape(width, width)

    @pl.when(pl.program_id(0) == 0)
    def _():
        second_ref[...] = jnp.broadcast_to(b2_ref[...], second_ref.shape)

    for start in range(0, first_ref.shape[0], BR):
        at = slice(start, start + BR)
        inner = jnp.dot(first_ref[at, :], w1, preferred_element_type=F32) + b1_ref[...]
        cdf = 0.5 + 0.5 * lax.erf(inner * (0.5**0.5))
        act = (inner * cdf).astype(BF)
        slope = cdf + inner * (jnp.exp2(inner * inner * (-0.5 * LOG2E)) * ((0.5 / math.pi) ** 0.5))
        act_ref[at, :] = act
        slope_ref[at, :] = slope.astype(BF)
        second_ref[at, :] += jnp.dot(act, w2, preferred_element_type=F32)


def weight_specs(feed, fb, first_slot):
    n, slots, r, width = feed.shape
    if n == 1:
        inner = pl.BlockSpec((1, 1, r, width), lambda j: (0, first_slot + j, 0, 0))
        outer = pl.BlockSpec((1, 1, r, width), lambda j: (0, first_slot + fb + j, 0, 0))
    else:
        inner = pl.BlockSpec((n, 1, r, width), lambda j: (0, first_slot + j, 0, 0))
        outer = pl.BlockSpec((n // fb, fb, r, width), lambda j: (j, first_slot // fb + 1, 0, 0))
    return inner, outer


def feed_forward(first, feed, fb, b1, b2):
    size, width = first.shape
    inner_spec, outer_spec = weight_specs(feed, fb, 0)
    block = pl.BlockSpec((size, width), lambda j: (0, j))
    whole = pl.BlockSpec((size, width), lambda j: (0, 0))
    line = pl.BlockSpec((1, width), lambda j: (0, j))
    const = pl.BlockSpec((1, width), lambda j: (0, 0))
    return pl.pallas_call(
        feed_forward_kernel,
        out_shape=(
            jax.ShapeDtypeStruct((size, fb * width), BF),
            jax.ShapeDtypeStruct((size, fb * width), BF),
            jax.ShapeDtypeStruct((size, width), F32),
        ),
        grid=(fb,),
        in_specs=[whole, inner_spec, outer_spec, line, const],
        out_specs=[block, block, whole],
        compiler_params=pltpu.CompilerParams(vmem_limit_bytes=60 << 20),
        cost_estimate=pl.CostEstimate(flops=20 << 30, bytes_accessed=16 << 20, transcendentals=0),
        name="feed_forward",
    )(first, feed, feed, b1, b2)


def outer_gradient_kernel(act_ref, gs_ref, grad_ref):
    grad = lax.dot_general(act_ref[...], gs_ref[...], TN, preferred_element_type=F32)
    grad_ref[...] = grad.astype(BF).reshape(grad_ref.shape)


def outer_gradient(act, gs, feed, fb):
    size, width = gs.shape
    n, _, r, _ = feed.shape
    if n == 1:
        spec = pl.BlockSpec((1, 1, r, width), lambda j: (0, j, 0, 0))
    else:
        spec = pl.BlockSpec((n // fb, fb, r, width), lambda j: (j, 0, 0, 0))
    return pl.pallas_call(
        outer_gradient_kernel,
        out_shape=jax.ShapeDtypeStruct((n, fb, r, width), BF),
        grid=(fb,),
        in_specs=[
            pl.BlockSpec((size, width), lambda j: (0, j)),
            pl.BlockSpec((size, width), lambda j: (0, 0)),
        ],
        out_specs=spec,
        compiler_params=pltpu.CompilerParams(vmem_limit_bytes=60 << 20),
        cost_estimate=COST,
        name="outer_gradient",
    )(act, gs)


def emit(core, grad, mine_ref, away_ref, at, r):
    for index in range(mine_ref.shape[0]):
        even = grad[2 * index * r : (2 * index + 1) * r, :]
        odd = grad[(2 * index + 1) * r : (2 * index + 2) * r, :]
        mine_ref[index, at, :] = jnp.where(core == 0, even, odd)
        away_ref[index, at, :] = jnp.where(core == 0, odd, even)


def feed_backward_kernel(
    me_ref, gs_ref, first_ref, w1_ref, w2_ref, slope_ref, base_ref, mine_ref, away_ref, gfirst_ref, gbias_ref, turned
):
    j = pl.program_id(0)
    size, width = gs_ref.shape
    w1 = w1_ref[...].reshape(width, width)
    w2 = w2_ref[...].reshape(width, width)

    @pl.when(j == 0)
    def _():
        gfirst_ref[...] = base_ref[...]
        turned[...] = first_ref[...].T

    total = jnp.zeros((1, width), F32)
    pieces = []
    for start in range(0, size, BR):
        at = slice(start, start + BR)
        wide = lax.dot_general(gs_ref[at, :], w2, NT, preferred_element_type=F32) * slope_ref[at, :].astype(F32)
        piece = wide.astype(BF)
        total += jnp.sum(piece.astype(F32), 0, keepdims=True)
        gfirst_ref[at, :] += lax.dot_general(piece, w1, NT, preferred_element_type=F32)
        pieces.append(piece)
    gbias_ref[...] = total
    grad = jnp.dot(turned[...], jnp.concatenate(pieces, 0), preferred_element_type=F32).astype(BF)
    emit(me_ref[0] & 1, grad, mine_ref, away_ref, slice(None), mine_ref.shape[1])


def feed_backward(me, gs, first, feed, fb, slope, base, r):
    size, width = first.shape
    half = width // r // 2
    inner_spec, outer_spec = weight_specs(feed, fb, 0)
    wrap = lambda spec: pl.BlockSpec(spec.block_shape, lambda j, m, f=spec.index_map: f(j))
    block = pl.BlockSpec((size, width), lambda j, m: (0, j))
    whole = pl.BlockSpec((size, width), lambda j, m: (0, 0))
    sides = pl.BlockSpec((half, r, width), lambda j, m: (0, j, 0))
    side = jax.ShapeDtypeStruct((half, fb * r, width), BF)
    return pl.pallas_call(
        feed_backward_kernel,
        out_shape=(
            side,
            side,
            jax.ShapeDtypeStruct((size, width), F32),
            jax.ShapeDtypeStruct((1, fb * width), F32),
        ),
        grid_spec=pltpu.PrefetchScalarGridSpec(
            num_scalar_prefetch=1,
            grid=(fb,),
            in_specs=[whole, whole, wrap(inner_spec), wrap(outer_spec), block, whole],
            out_specs=[sides, sides, whole, pl.BlockSpec((1, width), lambda j, m: (0, j))],
            scratch_shapes=[pltpu.VMEM((width, size), BF)],
        ),
        compiler_params=pltpu.CompilerParams(vmem_limit_bytes=60 << 20),
        cost_estimate=COST,
        name="feed_backward",
    )(me, gs, first, feed, feed, slope, base)


def send(value, bit):
    n = lax.axis_size("dp")
    return lax.ppermute(value, "dp", [(i, i ^ (1 << bit)) for i in range(n)])


def double(value, bit):
    return jnp.concatenate((value, send(value, bit)), 0)


def split_core(blocks):
    pairs = blocks.reshape((blocks.shape[0] // 2, 2) + blocks.shape[1:])
    core = lax.axis_index("dp") & 1
    take = lambda index: lax.dynamic_index_in_dim(pairs, index, 1, keepdims=False)
    return take(core), take(1 - core)


def reduce_steps(mine, away, cut):
    bits = mine.shape[0].bit_length()
    me = lax.axis_index("dp")

    def split(value, left, bit):
        axis = left.index(bit)
        here = (me >> bit) & 1
        other = lax.dynamic_index_in_dim(value, 1 - here, axis, keepdims=False)
        kept = lax.dynamic_index_in_dim(value, here, axis, keepdims=False)
        return kept, other, [b for b in left if b != bit]

    (got,) = yield [send(away, 0)]
    value = (mine.astype(F32) + got.astype(F32)).astype(BF).reshape((2,) * (bits - 1) + mine.shape[1:])
    axis = value.ndim - 2
    pieces = [lax.slice_in_dim(value, low, high, axis=axis) for low, high in ((0, cut), (cut, mine.shape[1]))]
    lefts = [list(range(bits - 1, 0, -1))] * 2
    for turn in ((1, 2), (2, 1)):
        parted = [split(piece, left, bit) for piece, left, bit in zip(pieces, lefts, turn)]
        gots = yield [send(other, bit) for (_, other, _), bit in zip(parted, turn)]
        pieces = [(kept.astype(F32) + got.astype(F32)).astype(BF) for (kept, _, _), got in zip(parted, gots)]
        lefts = [left for _, _, left in parted]
    value, left = jnp.concatenate(pieces, axis - 2), lefts[0]
    for bit in range(3, bits):
        kept, other, left = split(value.astype(BF), left, bit)
        (got,) = yield [send(other, bit)]
        value = kept.astype(F32) + got.astype(F32)
    return value


def finish(steps, received):
    while True:
        try:
            received = steps.send(received)
        except StopIteration as end:
            return end.value


def local(
    hidden,
    cotangent,
    lengths,
    permutation,
    query_weight,
    key_weight,
    value_weight,
    output_weight,
    query_bias,
    value_bias,
    output_bias,
    first_gain,
    first_shift,
    inner_weight,
    inner_bias,
    outer_weight,
    outer_bias,
    second_gain,
    second_shift,
):
    n = lax.axis_size("dp")
    me = lax.axis_index("dp")
    seq_count, part_len, width = hidden.shape
    assert seq_count == n
    length = part_len * n
    r = query_weight.shape[0]
    ff = inner_weight.shape[1]
    fb = ff // width

    def exchange(dealt):
        return lax.all_to_all(dealt, "dp", split_axis=0, concat_axis=0, tiled=True).reshape(length, width)

    dealt_hidden = jnp.take(hidden, permutation, axis=0, mode="clip")
    dealt_cotangent = jnp.take(cotangent, permutation, axis=0, mode="clip")

    def collect(values):
        return lax.all_to_all(values.reshape(n, part_len, width), "dp", split_axis=0, concat_axis=0, tiled=True)

    slabs = r % 32 == 0 and n >= 8 and ff // n <= 128
    me_ref = me.astype(jnp.int32).reshape(1)
    tied = lax.optimization_barrier
    small = (query_bias, value_bias, output_bias, first_gain, first_shift, outer_bias, second_gain, second_shift)
    feed_pack = jnp.concatenate(
        [inner_weight[:, i * width : (i + 1) * width] for i in range(fb)] + [outer_weight, output_weight], 0
    ).reshape(2 * fb + 1, r, width)
    if slabs:
        top, orders = gather_orders(n)
        block = jnp.stack(small)
        line = jnp.pad(block, ((0, 8), (0, width - r))) + jnp.pad(inner_bias[None], ((8, 7), (0, width - ff // n)))
        pack = jnp.concatenate((query_weight, key_weight, value_weight, line), 0)[None]
        pack, dealt_hidden = lax.optimization_barrier((pack, dealt_hidden))
        rows = exchange(dealt_hidden)
        for step, bit in enumerate(top):
            pack = double(pack, bit)
            if step == 0:
                pack, feed_pack = tied((pack, feed_pack))
            else:
                pack, dealt_cotangent = tied((pack, dealt_cotangent))
        cut = 3 * r // 2
        pieces = [pack[:, :cut], pack[:, cut:]]
        for step in (-2, -1):
            pieces = [double(piece, order[step]) for piece, order in zip(pieces, orders)]
        got = [send(piece, 0) for piece in pieces]
        lines = jnp.concatenate((pieces[1][:, cut:, :128], got[1][:, cut:, :128]), 0)
        apart = me ^ jnp.arange(n, dtype=jnp.int32)
        index = sum(((apart >> bit) & 1) << k for k, bit in enumerate(orders[1])) + (apart & 1) * (n // 2)
        lines = jnp.take(lines, index, axis=0, mode="clip")
        vectors = [lines[:, i, :r].reshape(1, width).astype(F32) for i in range(8)]
        full_inner_bias = lines[:, 8, : ff // n].reshape(1, ff).astype(F32)
    else:
        rows = exchange(dealt_hidden)
        small = jnp.concatenate(small + (inner_bias,))
        small = lax.all_to_all(
            jnp.broadcast_to(small[None], (n, small.shape[0])), "dp", split_axis=0, concat_axis=0, tiled=True
        )
        vectors = [small[:, i * r : (i + 1) * r].reshape(1, width).astype(F32) for i in range(8)]
        full_inner_bias = small[:, 8 * r :].reshape(1, ff).astype(F32)
    feed = lax.all_gather(feed_pack, "dp", axis=0, tiled=False)
    full_output = None if slabs else feed[:, 2 * fb].reshape(width, width)
    full_query_bias, full_value_bias, full_output_bias, full_first_gain, full_first_shift = vectors[:5]
    full_outer_bias, full_second_gain, full_second_shift = vectors[5:]
    bias = jnp.stack((full_query_bias, jnp.zeros_like(full_query_bias), full_value_bias))
    if slabs:
        qkv, weights = project(me_ref, (pieces[0], got[0], pieces[1], got[1]), rows, bias, r)
    else:
        feed = jnp.concatenate(
            (
                jnp.moveaxis(feed[:, :fb], 1, 0).reshape(1, fb, width, width),
                feed[:, fb : 2 * fb].reshape(1, fb, width, width),
            ),
            1,
        )
        gathered = lax.all_gather(jnp.stack((query_weight, key_weight, value_weight)), "dp", axis=0, tiled=False)
        weights = jnp.moveaxis(gathered, 1, 0).reshape(3, width, width)
        qkv = jnp.stack([(matmul(rows, weights[i]) + bias[i]).astype(BF) for i in range(3)])
    dealt_cotangent, qkv = lax.optimization_barrier((dealt_cotangent, qkv))
    arrived_cotangent = exchange(dealt_cotangent)

    my_len = lax.dynamic_slice_in_dim(lengths, me, 1)
    mixed, lse = attention_forward(my_len, qkv)
    wo = (feed, (n, 2 * fb, r)) if slabs else (full_output[None, None], (1, 0, width))
    first, first_norm, first_root, first_sums = norm_call(
        first_norm_kernel,
        "first_norm",
        length,
        width,
        (
            (mixed, "rows"),
            wo,
            (full_output_bias, "line"),
            (rows, "rows"),
            (full_first_gain, "line"),
            (full_first_shift, "line"),
        ),
        (("rows", BF), ("rows", F32), ("root", F32), ("sums", F32)),
        lens=my_len,
    )
    act, slope, second = feed_forward(first, feed, fb, full_inner_bias, full_outer_bias)
    arrived_cotangent, second = tied((arrived_cotangent, second))
    result, grad_res2, grad_second, second_sums = norm_call(
        second_norm_kernel,
        "second_norm",
        length,
        width,
        (
            (second, "rows"),
            (first, "rows"),
            (arrived_cotangent, "rows"),
            (full_second_gain, "line"),
            (full_second_shift, "line"),
        ),
        (("rows", BF), ("rows", F32), ("rows", BF), ("sums", F32)),
        lens=my_len,
    )
    grad_second, second_sums, first_sums, result = tied((grad_second, second_sums, first_sums, result))
    outer_blocks = outer_gradient(act, grad_second, feed, fb)
    outer_blocks, grad_second = tied((outer_blocks, grad_second))
    outer_owned = lax.psum_scatter(
        outer_blocks.reshape(n, r * fb, width), "dp", scatter_dimension=0, tiled=True
    )
    if slabs:
        mine, away, grad_first, inner_bias_grad = feed_backward(
            me_ref, grad_second, first, feed, fb, slope, grad_res2, r
        )
    else:
        even, odd, grad_first, inner_bias_grad = feed_backward(
            jnp.zeros_like(me_ref), grad_second, first, feed, fb, slope, grad_res2, width // 2
        )
        blocks = jnp.stack((even[0], odd[0])).reshape(2, fb, width // 2, width)
        blocks = jnp.moveaxis(blocks, 1, 2).reshape(n, r, fb, width)
        mine, away = split_core(jnp.moveaxis(blocks, 2, 1).reshape(n, fb * r, width))
    inner_steps = reduce_steps(mine, away, fb * r // 2)
    grad_first, inner_bias_grad, mine, away, result = tied((grad_first, inner_bias_grad, mine, away, result))
    out_back = collect(result)
    second_sums, first_sums, permutation, lengths, grad_first = tied(
        (second_sums, first_sums, permutation, lengths, grad_first)
    )
    moving = next(inner_steps)
    inverse = jnp.zeros(seq_count, jnp.int32).at[permutation].set(jnp.arange(seq_count, dtype=jnp.int32))

    grad_res1, grad_mixed, output_weight_grad, back_sums = norm_call(
        first_back_kernel,
        "first_back",
        length,
        width,
        (
            (grad_first, "rows"),
            (first_norm, "rows"),
            (first_root, "root"),
            (full_first_gain, "line"),
            (mixed, "rows"),
            wo,
        ),
        (("rows", F32), ("rows", BF), ("whole", BF), ("sums", F32)),
        scratch=(pltpu.VMEM((width, width), F32),),
    )
    sums = (first_sums, second_sums, back_sums, inner_bias_grad)
    moving, grad_mixed, output_weight_grad = tied((moving, grad_mixed, output_weight_grad))
    moving = inner_steps.send(moving)
    grads = attention_backward(my_len, qkv, mixed, grad_mixed, lse)
    moving, grads, out_back = tied((moving, grads, out_back))
    layer_out = jnp.take(out_back, inverse, axis=0, mode="clip")
    moving = inner_steps.send(moving)
    if slabs:
        input_grad, mine, away = project_back(me_ref, rows, grads, weights, grad_res1, output_weight_grad, sums, r)
        moving, input_grad, mine, away = tied((moving, input_grad, mine, away))
    else:
        input_grad = grad_res1 + sum(right_product(grads[i], weights[i]) for i in range(3))
        input_grad = input_grad.astype(BF)
        blocks = [left_product(rows, grads[i]).astype(BF) for i in range(3)] + [output_weight_grad]
        lines = [column_sum(grads[i])[None] for i in range(3)] + sum_rows(*sums)
        lines = jnp.concatenate(lines, 0).astype(BF)
        assert lines.shape[0] == SPARE
        blocks = [g.reshape(n, r, width) for g in blocks] + [jnp.broadcast_to(lines[None], (n, SPARE, width))]
        mine, away = split_core(jnp.concatenate(blocks, 1))
    input_back = collect(input_grad)
    ahead = inner_steps.send(moving)
    steps = reduce_steps(mine, away, 2 * r)
    moving = steps.send(next(steps))
    moving, outer_owned, ahead = tied((moving, outer_owned, ahead))
    moving = steps.send(moving)
    try:
        ahead = inner_steps.send(ahead)
        moving, ahead = tied((moving, ahead))
        inner_owned = finish(inner_steps, ahead)
    except StopIteration as end:
        inner_owned = end.value
    outer_owned = outer_owned.astype(F32)[0]
    reduced = finish(steps, moving)
    attention_owned = reduced[: 4 * r]
    owned = reduced[4 * r :]
    vectors = lax.dynamic_slice(owned, (0, me * r), (9, r))
    inner_bias_owned = owned[9 : 9 + fb].reshape(ff)
    inner_bias_owned = lax.dynamic_slice(inner_bias_owned, (me * (ff // n),), (ff // n,))
    sums = jnp.sum(owned[9 + fb : 12 + fb], 1)

    input_gradient = jnp.take(input_back, inverse, axis=0, mode="clip")
    rms = jnp.sqrt(sums / (jnp.sum(lengths).astype(F32) * width))
    return (
        layer_out,
        input_gradient,
        attention_owned[:r],
        attention_owned[r : 2 * r],
        attention_owned[2 * r : 3 * r],
        attention_owned[3 * r :],
        vectors[0],
        vectors[2],
        vectors[3],
        vectors[4],
        vectors[5],
        jnp.moveaxis(inner_owned.reshape(fb, r, width), 0, 1).reshape(r, ff),
        inner_bias_owned,
        outer_owned,
        vectors[6],
        vectors[7],
        vectors[8],
        rms[0],
        rms[1],
        rms[2],
    )


def solution(mesh):
    seq, mat, vec = P(None, "dp", None), P("dp", None), P("dp")
    return jax.shard_map(
        local,
        mesh=mesh,
        in_specs=(seq, seq, P(), P(), mat, mat, mat, mat, vec, vec, vec, vec, vec, mat, vec, mat, vec, vec, vec),
        out_specs=(seq, seq, mat, mat, mat, mat, vec, vec, vec, vec, vec, mat, vec, mat, vec, vec, vec, P(), P(), P()),
        check_vma=False,
    )
```

```python
import functools
import math

import jax
import jax.numpy as jnp
from jax import lax
from jax.experimental import pallas as pl
from jax.experimental.pallas import tpu as pltpu
from jax.sharding import PartitionSpec as P

HEADS = 16
EPS = 1e-05
NEG = -1e30
LOG2E = math.log2(math.e)
BF = jnp.bfloat16
F32 = jnp.float32
BQ = 1024
BR = 256
SPARE = 16
COST = pl.CostEstimate(flops=1 << 20, bytes_accessed=1 << 20, transcendentals=0)
NT = (((1,), (1,)), ((), ()))
TN = (((0,), (0,)), ((), ()))


def matmul(left, right):
    return jnp.dot(left, right, preferred_element_type=F32)


def left_product(left, right):
    return lax.dot_general(left, right, TN, preferred_element_type=F32)


def right_product(left, right):
    return lax.dot_general(left, right, NT, preferred_element_type=F32)


def column_sum(values):
    return jnp.sum(values.astype(F32), 0)


def head_keys(k, lane, half, key_bias):
    own = (lane >= 64 * half) & (lane < 64 * half + 64)
    spare = lane == 64 * (1 - half)
    return jnp.where(own, k, jnp.where(spare, key_bias, jnp.zeros_like(k)))


def head_queries(q, lane, half):
    return jnp.where(lane == 64 * (1 - half), jnp.ones_like(q), q)


def forward_kernel(len_ref, q_ref, k_ref, v_ref, o_ref, lse_ref, kh, vt):
    qi = pl.program_id(1)
    size = k_ref.shape[1]
    length = len_ref[0]

    @pl.when(qi == 0)
    def _():
        lane = lax.broadcasted_iota(jnp.int32, (size, 128), 1)
        row = lax.broadcasted_iota(jnp.int32, (size, 128), 0)
        key_bias = jnp.where(row < length, 0.0, NEG).astype(BF)
        k = k_ref[0]
        for half in (0, 1):
            kh[half] = head_keys(k, lane, half, key_bias)
        vt[...] = v_ref[0].T

    @pl.when(qi * BQ < length)
    def _():
        q = q_ref[0]
        lane = lax.broadcasted_iota(jnp.int32, q.shape, 1)
        scale = 0.125 * LOG2E
        outs = []
        for half in (0, 1):
            st = lax.dot_general(kh[half], head_queries(q, lane, half), NT, preferred_element_type=F32)
            peak = jnp.max(st, 0, keepdims=True) * scale
            pt = jnp.exp2(st * scale - peak)
            total = jnp.sum(pt, 0, keepdims=True)
            ot = jnp.dot(vt[64 * half : 64 * half + 64, :], pt.astype(BF), preferred_element_type=F32)
            outs.append(ot / total)
            lse_ref[0, half : half + 1, :] = peak + jnp.log2(total)
        o_ref[...] = jnp.concatenate(outs, 0).T.astype(BF)

    @pl.when(qi * BQ >= length)
    def _():
        o_ref[...] = jnp.zeros_like(o_ref)
        lse_ref[...] = jnp.zeros_like(lse_ref)


def qkv_specs(size):
    return [
        pl.BlockSpec((1, BQ, 128), lambda h, i, n: (0, i, h)),
        pl.BlockSpec((1, size, 128), lambda h, i, n: (1, 0, h)),
        pl.BlockSpec((1, size, 128), lambda h, i, n: (2, 0, h)),
    ]


def attention_forward(lens, qkv):
    _, size, width = qkv.shape
    pairs = width // 128
    return pl.pallas_call(
        forward_kernel,
        out_shape=(
            jax.ShapeDtypeStruct((size, width), BF),
            jax.ShapeDtypeStruct((pairs, 8, size), F32),
        ),
        grid_spec=pltpu.PrefetchScalarGridSpec(
            num_scalar_prefetch=1,
            grid=(pairs, size // BQ),
            in_specs=qkv_specs(size),
            out_specs=[
                pl.BlockSpec((BQ, 128), lambda h, i, n: (i, h)),
                pl.BlockSpec((1, 8, BQ), lambda h, i, n: (h, 0, i)),
            ],
            scratch_shapes=[pltpu.VMEM((2, size, 128), BF), pltpu.VMEM((128, size), BF)],
        ),
        compiler_params=pltpu.CompilerParams(vmem_limit_bytes=60 << 20),
        cost_estimate=pl.CostEstimate(flops=32 << 30, bytes_accessed=16 << 20, transcendentals=0),
        name="attention_forward",
    )(lens, qkv, qkv, qkv)


def backward_kernel(len_ref, q_ref, k_ref, v_ref, o_ref, g_ref, lse_ref, out_ref, kh, vh, kt, dka, dva):
    qi = pl.program_id(1)
    size = k_ref.shape[1]
    length = len_ref[0]
    here = pl.ds(pl.multiple_of(qi * BQ, BQ), BQ)

    @pl.when(qi == 0)
    def _():
        lane = lax.broadcasted_iota(jnp.int32, (size, 128), 1)
        row = lax.broadcasted_iota(jnp.int32, (size, 128), 0)
        key_bias = jnp.where(row < length, 0.0, NEG).astype(BF)
        k = k_ref[0]
        v = v_ref[0]
        for half in (0, 1):
            kh[half] = head_keys(k, lane, half, key_bias)
            vh[half] = head_keys(v, lane, half, jnp.zeros_like(v))
        kt[...] = k.T
        dka[...] = jnp.zeros_like(dka)
        dva[...] = jnp.zeros_like(dva)

    @pl.when(qi * BQ < length)
    def _():
        q = q_ref[0]
        g = g_ref[...]
        lane = lax.broadcasted_iota(jnp.int32, q.shape, 1)
        scale = 0.125 * LOG2E
        dots = (g.astype(F32) * o_ref[...].astype(F32)).T
        outs = []
        for half in (0, 1):
            qh = head_queries(q, lane, half)
            st = lax.dot_general(kh[half], qh, NT, preferred_element_type=F32)
            pt = jnp.exp2(st * scale - lse_ref[0, half : half + 1, :])
            dpt = lax.dot_general(vh[half], g, NT, preferred_element_type=F32)
            delta = jnp.sum(dots[64 * half : 64 * half + 64, :], 0, keepdims=True)
            dst = (pt * (dpt - delta)).astype(BF)
            dva[half] += jnp.dot(pt.astype(BF), g, preferred_element_type=F32)
            dka[half] += jnp.dot(dst, qh, preferred_element_type=F32)
            outs.append(jnp.dot(kt[64 * half : 64 * half + 64, :], dst, preferred_element_type=F32))
        out_ref[0, here, :] = (jnp.concatenate(outs, 0) * 0.125).T.astype(BF)

    @pl.when(qi * BQ >= length)
    def _():
        out_ref[0, here, :] = jnp.zeros((BQ, 128), BF)

    @pl.when(qi == pl.num_programs(1) - 1)
    def _():
        lane = lax.broadcasted_iota(jnp.int32, (size, 128), 1)
        out_ref[1] = (jnp.where(lane < 64, dka[0], dka[1]) * 0.125).astype(BF)
        out_ref[2] = jnp.where(lane < 64, dva[0], dva[1]).astype(BF)


def attention_backward(lens, qkv, o, g, lse):
    _, size, width = qkv.shape
    pairs = width // 128
    rows = pl.BlockSpec((BQ, 128), lambda h, i, n: (i, h))
    return pl.pallas_call(
        backward_kernel,
        out_shape=jax.ShapeDtypeStruct((3, size, width), BF),
        grid_spec=pltpu.PrefetchScalarGridSpec(
            num_scalar_prefetch=1,
            grid=(pairs, size // BQ),
            in_specs=qkv_specs(size) + [rows, rows, pl.BlockSpec((1, 8, BQ), lambda h, i, n: (h, 0, i))],
            out_specs=pl.BlockSpec((3, size, 128), lambda h, i, n: (0, 0, h)),
            scratch_shapes=[
                pltpu.VMEM((2, size, 128), BF),
                pltpu.VMEM((2, size, 128), BF),
                pltpu.VMEM((128, size), BF),
                pltpu.VMEM((2, size, 128), F32),
                pltpu.VMEM((2, size, 128), F32),
            ],
        ),
        compiler_params=pltpu.CompilerParams(vmem_limit_bytes=60 << 20),
        cost_estimate=COST,
        name="attention_backward",
    )(lens, qkv, qkv, qkv, o, g, lse)


def gather_orders(n):
    top = list(range(n.bit_length() - 2, 2, -1))
    return top, (top + [2, 1], top + [1, 2])


def distance(index, order):
    return sum(((index >> k) & 1) << bit for k, bit in enumerate(order))


def project_kernel(me_ref, a0, a1, b0, b1, x_ref, bias_ref, qkv_ref, w_ref, scratch, *, r, orders):
    j = pl.program_id(0)

    @pl.when(j == 0)
    def _():
        me = me_ref[0]
        half = r // 2
        for core, (a, b) in enumerate(((a0, b0), (a1, b1))):
            for index in range(a.shape[0]):
                off = pl.multiple_of((me ^ (distance(index, orders[0]) | core)) * r, r)
                scratch[0, pl.ds(off, r), :] = a[index, :r, :]
                scratch[1, pl.ds(off, half), :] = a[index, r : r + half, :]
                off = pl.multiple_of((me ^ (distance(index, orders[1]) | core)) * r, r)
                scratch[1, pl.ds(pl.multiple_of(off + half, half), half), :] = b[index, :half, :]
                scratch[2, pl.ds(off, r), :] = b[index, half : half + r, :]

    w = scratch[j]
    w_ref[0] = w
    qkv_ref[0] = (jnp.dot(x_ref[...], w, preferred_element_type=F32) + bias_ref[0]).astype(BF)


def project(me, pieces, x, bias, r):
    size, width = x.shape
    n = width // r
    whole = [pl.BlockSpec(p.shape, lambda j, m: (0, 0, 0)) for p in pieces]
    return pl.pallas_call(
        functools.partial(project_kernel, r=r, orders=gather_orders(n)[1]),
        out_shape=(jax.ShapeDtypeStruct((3, size, width), BF), jax.ShapeDtypeStruct((3, width, width), BF)),
        grid_spec=pltpu.PrefetchScalarGridSpec(
            num_scalar_prefetch=1,
            grid=(3,),
            in_specs=whole
            + [
                pl.BlockSpec((size, width), lambda j, m: (0, 0)),
                pl.BlockSpec((1, 1, width), lambda j, m: (j, 0, 0)),
            ],
            out_specs=[
                pl.BlockSpec((1, size, width), lambda j, m: (j, 0, 0)),
                pl.BlockSpec((1, width, width), lambda j, m: (j, 0, 0)),
            ],
            scratch_shapes=[pltpu.VMEM((3, width, width), BF)],
        ),
        compiler_params=pltpu.CompilerParams(vmem_limit_bytes=60 << 20),
        cost_estimate=pl.CostEstimate(flops=6 << 30, bytes_accessed=16 << 20, transcendentals=0),
        name="project",
    )(me, *pieces, x, bias)


def sum_rows(first_sums, second_sums, back_sums, inner_bias):
    width = first_sums.shape[1]
    rows = [back_sums[k : k + 1, :] for k in (2, 0, 1)] + [second_sums[k : k + 1, :] for k in (2, 0, 1)]
    rows += [inner_bias[0:1, k : k + width] for k in range(0, inner_bias.shape[1], width)]
    return rows + [first_sums[0:1, :], first_sums[1:2, :], second_sums[3:4, :]]


def project_back_kernel(
    me_ref, x_ref, g_ref, w_ref, base_ref, wo_ref, s1_ref, s2_ref, s3_ref, s4_ref, dx_ref, mine_ref, away_ref,
    xt, acc, lines, *, r
):
    j = pl.program_id(0)
    half, _, width = mine_ref.shape

    core = me_ref[0] & 1
    at = pl.ds(pl.multiple_of(j * r, r), r)

    @pl.when(j == 0)
    def _():
        xt[...] = x_ref[...].T
        acc[...] = base_ref[...]
        for k, row in enumerate(sum_rows(s1_ref, s2_ref, s3_ref, s4_ref), 3):
            lines[k : k + 1, :] = row

    @pl.when(j < 3)
    def _():
        g = g_ref[0]
        emit(core, jnp.dot(xt[...], g, preferred_element_type=F32).astype(BF), mine_ref, away_ref, at, r)
        acc[...] += lax.dot_general(g, w_ref[0], NT, preferred_element_type=F32)
        lines[pl.ds(j, 1), :] = jnp.sum(g.astype(F32), 0, keepdims=True)

    @pl.when(j == 3)
    def _():
        emit(core, wo_ref[...], mine_ref, away_ref, at, r)
        block = lines[...].astype(BF)
        for index in range(half):
            mine_ref[index, 4 * r :, :] = block
            away_ref[index, 4 * r :, :] = block
        dx_ref[...] = acc[...].astype(BF)


def project_back(me, x, grads, w, base, output_grad, sums, r):
    size, width = x.shape
    half = width // r // 2
    last = lambda j: jnp.minimum(j, 2)
    whole = pl.BlockSpec((size, width), lambda j, m: (0, 0))
    blocks = pl.BlockSpec((half, 4 * r + SPARE, width), lambda j, m: (0, 0, 0))
    return pl.pallas_call(
        functools.partial(project_back_kernel, r=r),
        out_shape=(
            jax.ShapeDtypeStruct((size, width), BF),
            jax.ShapeDtypeStruct((half, 4 * r + SPARE, width), BF),
            jax.ShapeDtypeStruct((half, 4 * r + SPARE, width), BF),
        ),
        grid_spec=pltpu.PrefetchScalarGridSpec(
            num_scalar_prefetch=1,
            grid=(4,),
            in_specs=[
                whole,
                pl.BlockSpec((1, size, width), lambda j, m: (last(j), 0, 0)),
                pl.BlockSpec((1, width, width), lambda j, m: (last(j), 0, 0)),
                whole,
                pl.BlockSpec((width, width), lambda j, m: (0, 0)),
            ]
            + [pl.BlockSpec(value.shape, lambda j, m: (0, 0)) for value in sums],
            out_specs=[whole, blocks, blocks],
            scratch_shapes=[
                pltpu.VMEM((width, size), BF),
                pltpu.VMEM((size, width), F32),
                pltpu.VMEM((SPARE, width), F32),
            ],
        ),
        compiler_params=pltpu.CompilerParams(vmem_limit_bytes=60 << 20),
        cost_estimate=COST,
        name="project_back",
    )(me, x, grads, w, base, output_grad, *sums)


def norm_rows(resid):
    center = resid - jnp.mean(resid, -1, keepdims=True)
    inverse_root = lax.rsqrt(jnp.mean(center * center, -1, keepdims=True) + EPS)
    return center * inverse_root, inverse_root


def norm_back(grad, norm, inverse_root):
    return (grad - jnp.mean(grad, -1, keepdims=True) - norm * jnp.mean(grad * norm, -1, keepdims=True)) * inverse_root


def valid_rows(len_ref):
    row = pl.program_id(0) * BR + lax.broadcasted_iota(jnp.int32, (BR, 1), 0)
    return (row < len_ref[0]).astype(F32)


def add_rows(sums_ref, values):
    @pl.when(pl.program_id(0) == 0)
    def _():
        sums_ref[...] = jnp.zeros_like(sums_ref)

    for k, value in enumerate(values):
        sums_ref[k : k + 1, :] += jnp.sum(value, 0, keepdims=True)


def first_norm_kernel(
    len_ref, mixed_ref, wo_ref, bias_ref, x_ref, gain_ref, shift_ref, first_ref, norm_ref, root_ref, sums_ref
):
    width = x_ref.shape[1]
    wo = wo_ref[...].reshape(width, width)
    branch = jnp.dot(mixed_ref[...], wo, preferred_element_type=F32) + bias_ref[...]
    x = x_ref[...].astype(F32)
    norm, root = norm_rows(x + branch)
    first_ref[...] = (norm * gain_ref[...] + shift_ref[...]).astype(BF)
    norm_ref[...] = norm
    root_ref[...] = jnp.broadcast_to(root, root_ref.shape)
    valid = valid_rows(len_ref)
    add_rows(sums_ref, (valid * x * x, valid * branch * branch))


def second_norm_kernel(
    len_ref, second_ref, first_ref, cotangent_ref, gain_ref, shift_ref, result_ref, wide_ref, grad_ref, sums_ref
):
    second = second_ref[...]
    norm, root = norm_rows(first_ref[...].astype(F32) + second)
    valid = valid_rows(len_ref)
    gain = gain_ref[...]
    result_ref[...] = ((norm * gain + shift_ref[...]) * valid).astype(BF)
    grad_out = cotangent_ref[...].astype(F32) * valid
    wide = norm_back(grad_out * gain, norm, root)
    grad = wide.astype(BF)
    wide_ref[...] = wide
    grad_ref[...] = grad
    add_rows(sums_ref, (grad_out * norm, grad_out, grad.astype(F32), valid * second * second))


def first_back_kernel(
    grad_ref, norm_ref, root_ref, gain_ref, mixed_ref, wo_ref, wide_ref, gmixed_ref, gweight_ref, sums_ref, total
):
    i = pl.program_id(0)
    width = norm_ref.shape[1]
    wo = wo_ref[...].reshape(width, width)
    grad_first = grad_ref[...]
    norm = norm_ref[...]
    wide = norm_back(grad_first * gain_ref[...], norm, root_ref[:, 0:1])
    grad = wide.astype(BF)
    wide_ref[...] = wide
    gmixed_ref[...] = lax.dot_general(grad, wo, NT, preferred_element_type=F32).astype(BF)
    part = lax.dot_general(mixed_ref[...], grad, TN, preferred_element_type=F32)

    @pl.when(i == 0)
    def _():
        total[...] = part

    @pl.when(i > 0)
    def _():
        total[...] += part

    @pl.when(i == pl.num_programs(0) - 1)
    def _():
        gweight_ref[...] = total[...].astype(BF)

    add_rows(sums_ref, (grad_first * norm, grad_first, grad.astype(F32)))


def norm_call(kernel, name, size, width, inputs, outputs, scratch=(), lens=None):
    prefetch = 0 if lens is None else 1

    def spec(kind):
        if kind == "rows":
            return pl.BlockSpec((BR, width), lambda i, *_: (i, 0))
        if kind == "root":
            return pl.BlockSpec((BR, 128), lambda i, *_: (i, 0))
        if kind == "line":
            return pl.BlockSpec((1, width), lambda i, *_: (0, 0))
        if kind == "sums":
            return pl.BlockSpec((8, width), lambda i, *_: (0, 0))
        if kind == "whole":
            return pl.BlockSpec((width, width), lambda i, *_: (0, 0))
        n, slot, r = kind
        return pl.BlockSpec((n, 1, r, width), lambda i, *_: (0, slot, 0, 0))

    shapes = {"rows": (size, width), "root": (size, 128), "sums": (8, width), "whole": (width, width)}
    call = pl.pallas_call(
        kernel,
        out_shape=tuple(jax.ShapeDtypeStruct(shapes[kind], dtype) for kind, dtype in outputs),
        grid_spec=pltpu.PrefetchScalarGridSpec(
            num_scalar_prefetch=prefetch,
            grid=(size // BR,),
            in_specs=[spec(kind) for _, kind in inputs],
            out_specs=[spec(kind) for kind, _ in outputs],
            scratch_shapes=list(scratch),
        ),
        compiler_params=pltpu.CompilerParams(vmem_limit_bytes=60 << 20),
        cost_estimate=COST,
        name=name,
    )
    arrays = [array for array, _ in inputs]
    return call(*arrays) if lens is None else call(lens, *arrays)


def feed_forward_kernel(first_ref, w1_ref, w2_ref, b1_ref, b2_ref, act_ref, slope_ref, second_ref):
    width = first_ref.shape[1]
    w1 = w1_ref[...].reshape(width, width)
    w2 = w2_ref[...].reshape(width, width)

    @pl.when(pl.program_id(0) == 0)
    def _():
        second_ref[...] = jnp.broadcast_to(b2_ref[...], second_ref.shape)

    for start in range(0, first_ref.shape[0], BR):
        at = slice(start, start + BR)
        inner = jnp.dot(first_ref[at, :], w1, preferred_element_type=F32) + b1_ref[...]
        cdf = 0.5 + 0.5 * lax.erf(inner * (0.5**0.5))
        act = (inner * cdf).astype(BF)
        slope = cdf + inner * (jnp.exp2(inner * inner * (-0.5 * LOG2E)) * ((0.5 / math.pi) ** 0.5))
        act_ref[at, :] = act
        slope_ref[at, :] = slope.astype(BF)
        second_ref[at, :] += jnp.dot(act, w2, preferred_element_type=F32)


def weight_specs(feed, fb, first_slot):
    n, slots, r, width = feed.shape
    if n == 1:
        inner = pl.BlockSpec((1, 1, r, width), lambda j: (0, first_slot + j, 0, 0))
        outer = pl.BlockSpec((1, 1, r, width), lambda j: (0, first_slot + fb + j, 0, 0))
    else:
        inner = pl.BlockSpec((n, 1, r, width), lambda j: (0, first_slot + j, 0, 0))
        outer = pl.BlockSpec((n // fb, fb, r, width), lambda j: (j, first_slot // fb + 1, 0, 0))
    return inner, outer


def feed_forward(first, feed, fb, b1, b2):
    size, width = first.shape
    inner_spec, outer_spec = weight_specs(feed, fb, 0)
    block = pl.BlockSpec((size, width), lambda j: (0, j))
    whole = pl.BlockSpec((size, width), lambda j: (0, 0))
    line = pl.BlockSpec((1, width), lambda j: (0, j))
    const = pl.BlockSpec((1, width), lambda j: (0, 0))
    return pl.pallas_call(
        feed_forward_kernel,
        out_shape=(
            jax.ShapeDtypeStruct((size, fb * width), BF),
            jax.ShapeDtypeStruct((size, fb * width), BF),
            jax.ShapeDtypeStruct((size, width), F32),
        ),
        grid=(fb,),
        in_specs=[whole, inner_spec, outer_spec, line, const],
        out_specs=[block, block, whole],
        compiler_params=pltpu.CompilerParams(vmem_limit_bytes=60 << 20),
        cost_estimate=pl.CostEstimate(flops=20 << 30, bytes_accessed=16 << 20, transcendentals=0),
        name="feed_forward",
    )(first, feed, feed, b1, b2)


def outer_gradient_kernel(act_ref, gs_ref, grad_ref):
    grad = lax.dot_general(act_ref[...], gs_ref[...], TN, preferred_element_type=F32)
    grad_ref[...] = grad.astype(BF).reshape(grad_ref.shape)


def outer_gradient(act, gs, feed, fb):
    size, width = gs.shape
    n, _, r, _ = feed.shape
    if n == 1:
        spec = pl.BlockSpec((1, 1, r, width), lambda j: (0, j, 0, 0))
    else:
        spec = pl.BlockSpec((n // fb, fb, r, width), lambda j: (j, 0, 0, 0))
    return pl.pallas_call(
        outer_gradient_kernel,
        out_shape=jax.ShapeDtypeStruct((n, fb, r, width), BF),
        grid=(fb,),
        in_specs=[
            pl.BlockSpec((size, width), lambda j: (0, j)),
            pl.BlockSpec((size, width), lambda j: (0, 0)),
        ],
        out_specs=spec,
        compiler_params=pltpu.CompilerParams(vmem_limit_bytes=60 << 20),
        cost_estimate=COST,
        name="outer_gradient",
    )(act, gs)


def emit(core, grad, mine_ref, away_ref, at, r):
    for index in range(mine_ref.shape[0]):
        even = grad[2 * index * r : (2 * index + 1) * r, :]
        odd = grad[(2 * index + 1) * r : (2 * index + 2) * r, :]
        mine_ref[index, at, :] = jnp.where(core == 0, even, odd)
        away_ref[index, at, :] = jnp.where(core == 0, odd, even)


def feed_backward_kernel(
    me_ref, gs_ref, first_ref, w1_ref, w2_ref, slope_ref, base_ref, mine_ref, away_ref, gfirst_ref, gbias_ref, turned
):
    j = pl.program_id(0)
    size, width = gs_ref.shape
    w1 = w1_ref[...].reshape(width, width)
    w2 = w2_ref[...].reshape(width, width)

    @pl.when(j == 0)
    def _():
        gfirst_ref[...] = base_ref[...]
        turned[...] = first_ref[...].T

    total = jnp.zeros((1, width), F32)
    pieces = []
    for start in range(0, size, BR):
        at = slice(start, start + BR)
        wide = lax.dot_general(gs_ref[at, :], w2, NT, preferred_element_type=F32) * slope_ref[at, :].astype(F32)
        piece = wide.astype(BF)
        total += jnp.sum(piece.astype(F32), 0, keepdims=True)
        gfirst_ref[at, :] += lax.dot_general(piece, w1, NT, preferred_element_type=F32)
        pieces.append(piece)
    gbias_ref[...] = total
    grad = jnp.dot(turned[...], jnp.concatenate(pieces, 0), preferred_element_type=F32).astype(BF)
    emit(me_ref[0] & 1, grad, mine_ref, away_ref, slice(None), mine_ref.shape[1])


def feed_backward(me, gs, first, feed, fb, slope, base, r):
    size, width = first.shape
    half = width // r // 2
    inner_spec, outer_spec = weight_specs(feed, fb, 0)
    wrap = lambda spec: pl.BlockSpec(spec.block_shape, lambda j, m, f=spec.index_map: f(j))
    block = pl.BlockSpec((size, width), lambda j, m: (0, j))
    whole = pl.BlockSpec((size, width), lambda j, m: (0, 0))
    sides = pl.BlockSpec((half, r, width), lambda j, m: (0, j, 0))
    side = jax.ShapeDtypeStruct((half, fb * r, width), BF)
    return pl.pallas_call(
        feed_backward_kernel,
        out_shape=(
            side,
            side,
            jax.ShapeDtypeStruct((size, width), F32),
            jax.ShapeDtypeStruct((1, fb * width), F32),
        ),
        grid_spec=pltpu.PrefetchScalarGridSpec(
            num_scalar_prefetch=1,
            grid=(fb,),
            in_specs=[whole, whole, wrap(inner_spec), wrap(outer_spec), block, whole],
            out_specs=[sides, sides, whole, pl.BlockSpec((1, width), lambda j, m: (0, j))],
            scratch_shapes=[pltpu.VMEM((width, size), BF)],
        ),
        compiler_params=pltpu.CompilerParams(vmem_limit_bytes=60 << 20),
        cost_estimate=COST,
        name="feed_backward",
    )(me, gs, first, feed, feed, slope, base)


def send(value, bit):
    n = lax.axis_size("dp")
    return lax.ppermute(value, "dp", [(i, i ^ (1 << bit)) for i in range(n)])


def double(value, bit):
    return jnp.concatenate((value, send(value, bit)), 0)


def split_core(blocks):
    pairs = blocks.reshape((blocks.shape[0] // 2, 2) + blocks.shape[1:])
    core = lax.axis_index("dp") & 1
    take = lambda index: lax.dynamic_index_in_dim(pairs, index, 1, keepdims=False)
    return take(core), take(1 - core)


def reduce_steps(mine, away, cut):
    bits = mine.shape[0].bit_length()
    me = lax.axis_index("dp")

    def split(value, left, bit):
        axis = left.index(bit)
        here = (me >> bit) & 1
        other = lax.dynamic_index_in_dim(value, 1 - here, axis, keepdims=False)
        kept = lax.dynamic_index_in_dim(value, here, axis, keepdims=False)
        return kept, other, [b for b in left if b != bit]

    (got,) = yield [send(away, 0)]
    value = (mine.astype(F32) + got.astype(F32)).astype(BF).reshape((2,) * (bits - 1) + mine.shape[1:])
    axis = value.ndim - 2
    pieces = [lax.slice_in_dim(value, low, high, axis=axis) for low, high in ((0, cut), (cut, mine.shape[1]))]
    lefts = [list(range(bits - 1, 0, -1))] * 2
    for turn in ((1, 2), (2, 1)):
        parted = [split(piece, left, bit) for piece, left, bit in zip(pieces, lefts, turn)]
        gots = yield [send(other, bit) for (_, other, _), bit in zip(parted, turn)]
        pieces = [(kept.astype(F32) + got.astype(F32)).astype(BF) for (kept, _, _), got in zip(parted, gots)]
        lefts = [left for _, _, left in parted]
    value, left = jnp.concatenate(pieces, axis - 2), lefts[0]
    for bit in range(3, bits):
        kept, other, left = split(value.astype(BF), left, bit)
        (got,) = yield [send(other, bit)]
        value = kept.astype(F32) + got.astype(F32)
    return value


def finish(steps, received):
    while True:
        try:
            received = steps.send(received)
        except StopIteration as end:
            return end.value


def local(
    hidden,
    cotangent,
    lengths,
    permutation,
    query_weight,
    key_weight,
    value_weight,
    output_weight,
    query_bias,
    value_bias,
    output_bias,
    first_gain,
    first_shift,
    inner_weight,
    inner_bias,
    outer_weight,
    outer_bias,
    second_gain,
    second_shift,
):
    n = lax.axis_size("dp")
    me = lax.axis_index("dp")
    seq_count, part_len, width = hidden.shape
    assert seq_count == n
    length = part_len * n
    r = query_weight.shape[0]
    ff = inner_weight.shape[1]
    fb = ff // width

    def exchange(dealt):
        return lax.all_to_all(dealt, "dp", split_axis=0, concat_axis=0, tiled=True).reshape(length, width)

    dealt_hidden = jnp.take(hidden, permutation, axis=0, mode="clip")
    dealt_cotangent = jnp.take(cotangent, permutation, axis=0, mode="clip")

    def collect(values):
        return lax.all_to_all(values.reshape(n, part_len, width), "dp", split_axis=0, concat_axis=0, tiled=True)

    slabs = r % 32 == 0 and n >= 8 and ff // n <= 128
    me_ref = me.astype(jnp.int32).reshape(1)
    tied = lax.optimization_barrier
    small = (query_bias, value_bias, output_bias, first_gain, first_shift, outer_bias, second_gain, second_shift)
    feed_pack = jnp.concatenate(
        [inner_weight[:, i * width : (i + 1) * width] for i in range(fb)] + [outer_weight, output_weight], 0
    ).reshape(2 * fb + 1, r, width)
    if slabs:
        top, orders = gather_orders(n)
        block = jnp.stack(small)
        line = jnp.pad(block, ((0, 8), (0, width - r))) + jnp.pad(inner_bias[None], ((8, 7), (0, width - ff // n)))
        pack = jnp.concatenate((query_weight, key_weight, value_weight, line), 0)[None]
        pack, dealt_hidden = lax.optimization_barrier((pack, dealt_hidden))
        rows = exchange(dealt_hidden)
        for step, bit in enumerate(top):
            pack = double(pack, bit)
            if step == 0:
                pack, feed_pack = tied((pack, feed_pack))
            else:
                pack, dealt_cotangent = tied((pack, dealt_cotangent))
        cut = 3 * r // 2
        pieces = [pack[:, :cut], pack[:, cut:]]
        for step in (-2, -1):
            pieces = [double(piece, order[step]) for piece, order in zip(pieces, orders)]
        got = [send(piece, 0) for piece in pieces]
        lines = jnp.concatenate((pieces[1][:, cut:, :128], got[1][:, cut:, :128]), 0)
        apart = me ^ jnp.arange(n, dtype=jnp.int32)
        index = sum(((apart >> bit) & 1) << k for k, bit in enumerate(orders[1])) + (apart & 1) * (n // 2)
        lines = jnp.take(lines, index, axis=0, mode="clip")
        vectors = [lines[:, i, :r].reshape(1, width).astype(F32) for i in range(8)]
        full_inner_bias = lines[:, 8, : ff // n].reshape(1, ff).astype(F32)
    else:
        rows = exchange(dealt_hidden)
        small = jnp.concatenate(small + (inner_bias,))
        small = lax.all_to_all(
            jnp.broadcast_to(small[None], (n, small.shape[0])), "dp", split_axis=0, concat_axis=0, tiled=True
        )
        vectors = [small[:, i * r : (i + 1) * r].reshape(1, width).astype(F32) for i in range(8)]
        full_inner_bias = small[:, 8 * r :].reshape(1, ff).astype(F32)
    feed = lax.all_gather(feed_pack, "dp", axis=0, tiled=False)
    full_output = None if slabs else feed[:, 2 * fb].reshape(width, width)
    full_query_bias, full_value_bias, full_output_bias, full_first_gain, full_first_shift = vectors[:5]
    full_outer_bias, full_second_gain, full_second_shift = vectors[5:]
    bias = jnp.stack((full_query_bias, jnp.zeros_like(full_query_bias), full_value_bias))
    if slabs:
        qkv, weights = project(me_ref, (pieces[0], got[0], pieces[1], got[1]), rows, bias, r)
    else:
        feed = jnp.concatenate(
            (
                jnp.moveaxis(feed[:, :fb], 1, 0).reshape(1, fb, width, width),
                feed[:, fb : 2 * fb].reshape(1, fb, width, width),
            ),
            1,
        )
        gathered = lax.all_gather(jnp.stack((query_weight, key_weight, value_weight)), "dp", axis=0, tiled=False)
        weights = jnp.moveaxis(gathered, 1, 0).reshape(3, width, width)
        qkv = jnp.stack([(matmul(rows, weights[i]) + bias[i]).astype(BF) for i in range(3)])
    dealt_cotangent, qkv = lax.optimization_barrier((dealt_cotangent, qkv))
    arrived_cotangent = exchange(dealt_cotangent)

    my_len = lax.dynamic_slice_in_dim(lengths, me, 1)
    mixed, lse = attention_forward(my_len, qkv)
    wo = (feed, (n, 2 * fb, r)) if slabs else (full_output[None, None], (1, 0, width))
    first, first_norm, first_root, first_sums = norm_call(
        first_norm_kernel,
        "first_norm",
        length,
        width,
        (
            (mixed, "rows"),
            wo,
            (full_output_bias, "line"),
            (rows, "rows"),
            (full_first_gain, "line"),
            (full_first_shift, "line"),
        ),
        (("rows", BF), ("rows", F32), ("root", F32), ("sums", F32)),
        lens=my_len,
    )
    act, slope, second = feed_forward(first, feed, fb, full_inner_bias, full_outer_bias)
    arrived_cotangent, second = tied((arrived_cotangent, second))
    result, grad_res2, grad_second, second_sums = norm_call(
        second_norm_kernel,
        "second_norm",
        length,
        width,
        (
            (second, "rows"),
            (first, "rows"),
            (arrived_cotangent, "rows"),
            (full_second_gain, "line"),
            (full_second_shift, "line"),
        ),
        (("rows", BF), ("rows", F32), ("rows", BF), ("sums", F32)),
        lens=my_len,
    )
    grad_second, second_sums, first_sums, result = tied((grad_second, second_sums, first_sums, result))
    outer_blocks = outer_gradient(act, grad_second, feed, fb)
    outer_blocks, grad_second = tied((outer_blocks, grad_second))
    outer_owned = lax.psum_scatter(
        outer_blocks.reshape(n, r * fb, width), "dp", scatter_dimension=0, tiled=True
    )
    if slabs:
        mine, away, grad_first, inner_bias_grad = feed_backward(
            me_ref, grad_second, first, feed, fb, slope, grad_res2, r
        )
    else:
        even, odd, grad_first, inner_bias_grad = feed_backward(
            jnp.zeros_like(me_ref), grad_second, first, feed, fb, slope, grad_res2, width // 2
        )
        blocks = jnp.stack((even[0], odd[0])).reshape(2, fb, width // 2, width)
        blocks = jnp.moveaxis(blocks, 1, 2).reshape(n, r, fb, width)
        mine, away = split_core(jnp.moveaxis(blocks, 2, 1).reshape(n, fb * r, width))
    inner_steps = reduce_steps(mine, away, fb * r // 2)
    grad_first, inner_bias_grad, mine, away, result = tied((grad_first, inner_bias_grad, mine, away, result))
    out_back = collect(result)
    second_sums, first_sums, permutation, lengths, grad_first = tied(
        (second_sums, first_sums, permutation, lengths, grad_first)
    )
    moving = next(inner_steps)
    inverse = jnp.zeros(seq_count, jnp.int32).at[permutation].set(jnp.arange(seq_count, dtype=jnp.int32))

    grad_res1, grad_mixed, output_weight_grad, back_sums = norm_call(
        first_back_kernel,
        "first_back",
        length,
        width,
        (
            (grad_first, "rows"),
            (first_norm, "rows"),
            (first_root, "root"),
            (full_first_gain, "line"),
            (mixed, "rows"),
            wo,
        ),
        (("rows", F32), ("rows", BF), ("whole", BF), ("sums", F32)),
        scratch=(pltpu.VMEM((width, width), F32),),
    )
    sums = (first_sums, second_sums, back_sums, inner_bias_grad)
    moving, grad_mixed, output_weight_grad = tied((moving, grad_mixed, output_weight_grad))
    moving = inner_steps.send(moving)
    grads = attention_backward(my_len, qkv, mixed, grad_mixed, lse)
    moving, grads, out_back = tied((moving, grads, out_back))
    layer_out = jnp.take(out_back, inverse, axis=0, mode="clip")
    moving = inner_steps.send(moving)
    if slabs:
        input_grad, mine, away = project_back(me_ref, rows, grads, weights, grad_res1, output_weight_grad, sums, r)
        moving, input_grad, mine, away = tied((moving, input_grad, mine, away))
    else:
        input_grad = grad_res1 + sum(right_product(grads[i], weights[i]) for i in range(3))
        input_grad = input_grad.astype(BF)
        blocks = [left_product(rows, grads[i]).astype(BF) for i in range(3)] + [output_weight_grad]
        lines = [column_sum(grads[i])[None] for i in range(3)] + sum_rows(*sums)
        lines = jnp.concatenate(lines, 0).astype(BF)
        assert lines.shape[0] == SPARE
        blocks = [g.reshape(n, r, width) for g in blocks] + [jnp.broadcast_to(lines[None], (n, SPARE, width))]
        mine, away = split_core(jnp.concatenate(blocks, 1))
    input_back = collect(input_grad)
    ahead = inner_steps.send(moving)
    steps = reduce_steps(mine, away, mine.shape[1] // 2)
    moving = steps.send(next(steps))
    moving, outer_owned, ahead = tied((moving, outer_owned, ahead))
    moving = steps.send(moving)
    try:
        ahead = inner_steps.send(ahead)
        moving, ahead = tied((moving, ahead))
        inner_owned = finish(inner_steps, ahead)
    except StopIteration as end:
        inner_owned = end.value
    outer_owned = outer_owned.astype(F32)[0]
    reduced = finish(steps, moving)
    attention_owned = reduced[: 4 * r]
    owned = reduced[4 * r :]
    vectors = lax.dynamic_slice(owned, (0, me * r), (9, r))
    inner_bias_owned = owned[9 : 9 + fb].reshape(ff)
    inner_bias_owned = lax.dynamic_slice(inner_bias_owned, (me * (ff // n),), (ff // n,))
    sums = jnp.sum(owned[9 + fb : 12 + fb], 1)

    input_gradient = jnp.take(input_back, inverse, axis=0, mode="clip")
    rms = jnp.sqrt(sums / (jnp.sum(lengths).astype(F32) * width))
    return (
        layer_out,
        input_gradient,
        attention_owned[:r],
        attention_owned[r : 2 * r],
        attention_owned[2 * r : 3 * r],
        attention_owned[3 * r :],
        vectors[0],
        vectors[2],
        vectors[3],
        vectors[4],
        vectors[5],
        jnp.moveaxis(inner_owned.reshape(fb, r, width), 0, 1).reshape(r, ff),
        inner_bias_owned,
        outer_owned,
        vectors[6],
        vectors[7],
        vectors[8],
        rms[0],
        rms[1],
        rms[2],
    )


def solution(mesh):
    seq, mat, vec = P(None, "dp", None), P("dp", None), P("dp")
    return jax.shard_map(
        local,
        mesh=mesh,
        in_specs=(seq, seq, P(), P(), mat, mat, mat, mat, vec, vec, vec, vec, vec, mat, vec, mat, vec, vec, vec),
        out_specs=(seq, seq, mat, mat, mat, mat, vec, vec, vec, vec, vec, mat, vec, mat, vec, vec, vec, P(), P(), P()),
        check_vma=False,
    )
```
